256 devices in a mesh: ka: 32 (over y_hi, z, core), band: 8 (over y_lo, x).
Axes of the slice: x: 4, y: 4 (y_hi: 2, y_lo: 2; y = y_hi * 2 + y_lo), z: 8, core: 2. Of those that a mesh axis runs over, the one named last changes fastest.
Arguments:
- coefficients: bfloat16 [32, 2, 160, 2400], P('ka'), may hold values from -6 to 6
- class_weight: float32 [32], replicated, may hold values from 0.5 to 5
- diff_class: int32 [32, 32], replicated, may hold values from 0 to 31
- frag_cells: int32 [2], replicated, may hold values from 0 to 31
- block_pattern: int32 [2, 30], replicated, may hold values 0 or 1
Outputs:
- cluster: float32 [2, 2, 160, 2400], P(None, None, 'band', 'ka')
The draws below stay inside these ranges and needn't reach their ends.
All inputs are finite; a program needn't handle non-finite values.
Results may differ from the reference program's by a relative error of at most 0.0017.
Values may be sent and summed in bfloat16 or wider, within the bound.
No kernel may reach another device: no remote copies, remote signals or barrier semaphores. Data moves between devices by JAX's collectives and lax.ppermute only.
A program may use at most 64 MiB of HBM per device.

```python
import math
import jax
import jax.numpy as jnp
from jax import lax

NAO = 2400
NBLK = 30
NFRAG = 2
NK = 32
NOCC = 160
BLK = 80


def set_ends(drawn, own_key, least, largest):
    shape = drawn.shape
    spot = [jax.random.randint(jax.random.fold_in(own_key, axis), (), 0, shape[axis]) for axis in range(len(shape))]
    drawn = drawn.at[tuple(spot)].set(least)
    longest = shape.index(max(shape))
    spot[longest] = (spot[longest] + 1) % shape[longest]
    return drawn.at[tuple(spot)].set(largest)


def levels(own_key, dims, split, low, top_value):
    loudness, own = 1.0, jax.random.fold_in(own_key, 6)
    for dim, parts in split:
        draws = jnp.exp(jax.random.uniform(jax.random.fold_in(own, dim), (parts,), jnp.float32, low / len(split), top_value / len(split)))
        loudness = loudness * jnp.repeat(draws, dims[dim] // parts).reshape([-1 if axis == dim else 1 for axis in range(len(dims))])
    return loudness


def normal_values(own_key, shape, scale, reach, split=(), held_as=jnp.bfloat16):
    array = jax.random.normal(own_key, shape, jnp.float32) * scale
    if len(split) > 0:
        array = levels(own_key, shape, split, -0.22, 0.18) * array
    return jnp.clip(array, min=-reach, max=reach).astype(held_as)


def setup_inputs(seed: int = 0) -> dict:
    arg_keys = jax.random.split(jax.random.key(seed), 6)
    return {
        "coefficients": normal_values(arg_keys[0], (NK, 2, NOCC, NAO), 1.0, 6.0, ((0, 32),)),
        "class_weight": jnp.clip(jnp.exp(jax.random.uniform(arg_keys[1], (NK,), jnp.float32, math.log(0.5), math.log(5.0))), 0.5, 5.0),
        "diff_class": set_ends(jax.random.randint(arg_keys[2], (NK, NK), 0, NK), jax.random.fold_in(arg_keys[2], 1), 0, NK - 1).astype(jnp.int32),
        "frag_cells": jax.random.randint(arg_keys[3], (NFRAG,), 0, NK).astype(jnp.int32),
        "block_pattern": set_ends((jax.random.randint(arg_keys[4], (NFRAG, NBLK), 0, 2) < 1).astype(jnp.int32), jax.random.fold_in(arg_keys[4], 1), 0, 1),
    }


def reference(coefficients, class_weight, diff_class, frag_cells, block_pattern):
    flat_coeff = coefficients.astype(jnp.float32).reshape(NK, 2 * NOCC, NAO)
    pair_weight = class_weight[diff_class]

    def step(running, kpoint):
        coeff_q = lax.dynamic_index_in_dim(flat_coeff, kpoint, 0, keepdims=False)
        intersection = jnp.einsum("ia,kja->kij", coeff_q, flat_coeff)
        m_real = intersection[:, :NOCC, :NOCC] + intersection[:, NOCC:, NOCC:]
        m_imag = intersection[:, :NOCC, NOCC:] - intersection[:, NOCC:, :NOCC]
        scaling = (lax.dynamic_index_in_dim(pair_weight, kpoint, 1, keepdims=False) / NAO)[:, None, None]
        m_real = lax.optimization_barrier((scaling * m_real).astype(jnp.bfloat16)).astype(jnp.float32)
        m_imag = lax.optimization_barrier((scaling * m_imag).astype(jnp.bfloat16)).astype(jnp.float32)
        m_block = jnp.concatenate([jnp.concatenate([m_real, m_imag], 2), jnp.concatenate([-m_imag, m_real], 2)], 1)
        return running + jnp.einsum("kio,ia->koa", m_block, coeff_q), None

    start_value = jnp.zeros((NK, 2 * NOCC, NAO), jnp.float32)
    exchange, _ = lax.scan(step, start_value, jnp.arange(NK, dtype=jnp.int32))
    w_real = exchange[:, :NOCC]
    w_imag = exchange[:, NOCC:]
    kpoints = jnp.arange(NK, dtype=jnp.int32)
    phase_index = (kpoints[None, :] * frag_cells[:, None]) % NK
    angles = 2.0 * jnp.pi * phase_index.astype(jnp.float32) / NK
    cosines = jnp.cos(angles) / NK
    sines = jnp.sin(angles) / NK
    high = lax.Precision.HIGHEST
    x_real = jnp.einsum("fk,kja->fja", cosines, w_real, precision=high) - jnp.einsum("fk,kja->fja", sines, w_imag, precision=high)
    x_imag = jnp.einsum("fk,kja->fja", sines, w_real, precision=high) + jnp.einsum("fk,kja->fja", cosines, w_imag, precision=high)
    block_ids = jnp.arange(NAO, dtype=jnp.int32) // BLK
    block_mask = block_pattern[:, block_ids].astype(jnp.float32)
    return jnp.stack([x_real, x_imag], 1) * block_mask[:, None, None, :]
```

```python
import jax
import jax.numpy as jnp
import numpy as np
from jax import lax
from jax.experimental import pallas as pl
from jax.experimental.pallas import tpu as pltpu
from jax.sharding import Mesh
from jax.sharding import PartitionSpec as P

AXES = ("yh", "z", "core", "yl", "x")
KA = ("yh", "z", "core")
BAND = ("yl", "x")
PARTS = (2, 8, 2, 2, 4)
F32 = jnp.float32
BF16 = jnp.bfloat16


def phase_signs(width, blocks):
    rows = np.arange(8 * width)
    cols = np.arange(2 * blocks * width)
    partner, part = (rows // (4 * width))[:, None], (rows // width % 2)[:, None]
    part_m = (cols // width % 2)[None, :]
    same = (rows % width)[:, None] == (cols % width)[None, :]
    real = np.where(partner == 0, part == 0, part == 1)
    sign = np.where((partner == 1) & (part == 0), -1, 1)
    cos_sign = same * sign * np.where(real, part_m == 0, part_m == 1)
    sin_sign = same * sign * np.where(real, -1 * (part_m == 1), part_m == 0)
    return cos_sign.astype(np.float32), sin_sign.astype(np.float32)


def turned(width):
    turn = np.zeros((2 * width, 2 * width), np.float32)
    turn[:width, width:] = np.eye(width)
    turn[width:, :width] = -np.eye(width)
    return turn


def cluster_kernel(core_ref, own, near, far_r, far_i, diag_r, diag_i, *refs):
    blocks, (weights, g_high, g_low, turn, mine, other, b_ref, bt_ref, u_ref) = refs[:8], refs[8:]
    rows = blocks[0].shape[0]
    for step, block in enumerate(blocks):
        value = block[...]
        b_ref[pl.ds(step * rows, rows), :] = value
        swapped = jnp.dot(turn[...], value, preferred_element_type=F32)
        bt_ref[pl.ds(step * rows, rows), :] = swapped.astype(BF16)
    outs = g_high.shape[0] // 2
    contract = (((1,), (1,)), ((), ()))
    for q in range(4):
        real, imag = (
            (own[0], own[1]),
            (near[0], near[1]),
            (far_r[...], far_i[...]),
            (diag_r[...], diag_i[...]),
        )[q]
        m = lax.dot_general(b_ref[...], real, contract, preferred_element_type=F32)
        m = m + lax.dot_general(bt_ref[...], imag, contract, preferred_element_type=F32)
        m = (weights[q] * m).astype(BF16)
        t = jnp.dot(g_high[...], m, preferred_element_type=F32)
        t = t + jnp.dot(g_low[...], m, preferred_element_type=F32)
        t_high = t.astype(BF16)
        t_low = (t - t_high.astype(F32)).astype(BF16)
        u = jnp.dot(t_high[:outs], real, preferred_element_type=F32)
        u = u + jnp.dot(t_high[outs:], imag, preferred_element_type=F32)
        u = u + jnp.dot(t_low[:outs], real, preferred_element_type=F32)
        u = u + jnp.dot(t_low[outs:], imag, preferred_element_type=F32)
        u_ref[...] = u if q == 0 else u_ref[...] + u
    chips, _, columns = mine.shape
    for core in range(2):

        @pl.when(core_ref[0] == core)
        def _():
            for chip in range(chips):
                at = (2 * chip + core) * columns
                mine[chip] = u_ref[:, at : at + columns]
                at = (2 * chip + 1 - core) * columns
                other[chip] = u_ref[:, at : at + columns]


def shards(coefficients, class_weight, diff_class, frag_cells, block_pattern):
    own = coefficients[0]
    _, occupied, functions = own.shape
    yh, z, core = (lax.axis_index(name) for name in KA)
    band = lax.axis_index("yl") * PARTS[4] + lax.axis_index("x")
    width = occupied // (PARTS[3] * PARTS[4])
    kpoint_count = PARTS[0] * PARTS[1] * PARTS[2]
    up = [(i, (i + 1) % PARTS[1]) for i in range(PARTS[1])]
    down = [(j, i) for i, j in up]
    swap = [(0, 1), (1, 0)]

    block = lax.dynamic_slice_in_dim(own, band * width, width, 1).reshape(2 * width, functions)
    near = lax.ppermute(own, "core", swap)
    far_r = lax.ppermute(own[0], "yh", swap)
    far_i = lax.ppermute(own[1], "yh", swap)
    diag_r = lax.ppermute(far_r, "core", swap)
    diag_i = lax.ppermute(far_i, "core", swap)
    blocks, offsets = [block], [0]
    from_below = from_above = block
    for step in range(1, PARTS[1] // 2 + 1):
        from_below = lax.ppermute(from_below, "z", up)
        blocks.append(from_below)
        offsets.append(-step)
        if step < PARTS[1] // 2:
            from_above = lax.ppermute(from_above, "z", down)
            blocks.append(from_above)
            offsets.append(step)

    kpoints = (yh * PARTS[1] + (z + jnp.array(offsets, jnp.int32)) % PARTS[1]) * 2 + core
    q_yh = jnp.stack([yh, yh, 1 - yh, 1 - yh])
    q_core = jnp.stack([core, 1 - core, core, 1 - core])
    q_points = (q_yh * PARTS[1] + z) * 2 + q_core
    picked = jnp.take(jnp.take(diff_class, kpoints, axis=0), q_points, axis=1)
    weights = jnp.take(class_weight, picked.T) / functions
    weights = jnp.repeat(weights, 2 * width, axis=1)[:, :, None]

    phase_index = frag_cells[:, None] * kpoints[None, :] % kpoint_count
    angles = 2.0 * jnp.pi * phase_index.astype(F32) / kpoint_count
    cells = frag_cells.shape[0]
    spread = (1, cells, 2 * width, 2 * width * len(blocks))
    full = (2,) + spread[1:]
    cosines = jnp.repeat(jnp.cos(angles) / kpoint_count, 2 * width, axis=1)[None, :, None, :]
    sines = jnp.repeat(jnp.sin(angles) / kpoint_count, 2 * width, axis=1)[None, :, None, :]
    cos_sign, sin_sign = (jnp.asarray(a.reshape(full)) for a in phase_signs(width, len(blocks)))
    g = (cos_sign * cosines + sin_sign * sines).reshape(8 * width, -1)
    g_high = g.astype(BF16)
    g_low = (g - g_high.astype(F32)).astype(BF16)

    chips = PARTS[0] * PARTS[1]
    columns = functions // kpoint_count
    piece = jax.ShapeDtypeStruct((chips, 4 * width, columns), F32)
    mine, other = pl.pallas_call(
        cluster_kernel,
        out_shape=(piece, piece),
        in_specs=[pl.BlockSpec(memory_space=pltpu.SMEM)] + [pl.BlockSpec(memory_space=pltpu.VMEM)] * 18,
        out_specs=(pl.BlockSpec(memory_space=pltpu.VMEM),) * 2,
        scratch_shapes=[
            pltpu.VMEM((2 * width * len(blocks), functions), BF16),
            pltpu.VMEM((2 * width * len(blocks), functions), BF16),
            pltpu.VMEM((4 * width, functions), F32),
        ],
        compiler_params=pltpu.CompilerParams(vmem_limit_bytes=48 * 2**20),
        cost_estimate=pl.CostEstimate(flops=3 * 10**9, bytes_accessed=10**7, transcendentals=0),
        name="cluster_terms",
    )(core[None], own, near, far_r, far_i, diag_r, diag_i, *blocks, weights, g_high, g_low, jnp.asarray(turned(width), BF16))

    sums = (mine + lax.ppermute(other, "core", swap)).astype(BF16)
    arrived = lax.all_to_all(sums, ("yh", "z"), 0, 0, tiled=True)
    cluster = jnp.sum(arrived.astype(F32), axis=0).reshape(cells, 2, width, columns)
    index = (yh * PARTS[1] + z) * 2 + core
    block_size = functions // block_pattern.shape[1]
    local_ids = (index * columns + jnp.arange(columns, dtype=jnp.int32)) // block_size
    block_ids = jnp.arange(block_pattern.shape[1], dtype=jnp.int32)
    onehot = (block_ids[:, None] == local_ids[None, :]).astype(F32)
    mask = jnp.dot(block_pattern.astype(F32), onehot, precision=lax.Precision.HIGHEST)
    return cluster * mask[:, None, None, :]


def solution(mesh):
    placed = (P(KA, None, None, None), P(), P(), P(), P())
    return jax.shard_map(
        shards,
        mesh=Mesh(mesh.devices.reshape(PARTS), AXES),
        in_specs=placed,
        out_specs=P(None, None, BAND, KA),
        check_vma=False,
    )
```

```python
import jax
import jax.numpy as jnp
import numpy as np
from jax import lax
from jax.experimental import pallas as pl
from jax.experimental.pallas import tpu as pltpu
from jax.sharding import Mesh
from jax.sharding import PartitionSpec as P

AXES = ("yh", "z", "core", "yl", "x")
KA = ("yh", "z", "core")
BAND = ("yl", "x")
PARTS = (2, 8, 2, 2, 4)
F32 = jnp.float32
BF16 = jnp.bfloat16


def phase_signs(width, blocks):
    rows = np.arange(8 * width)
    cols = np.arange(2 * blocks * width)
    partner, part = (rows // (4 * width))[:, None], (rows // width % 2)[:, None]
    part_m = (cols // width % 2)[None, :]
    same = (rows % width)[:, None] == (cols % width)[None, :]
    real = np.where(partner == 0, part == 0, part == 1)
    sign = np.where((partner == 1) & (part == 0), -1, 1)
    cos_sign = same * sign * np.where(real, part_m == 0, part_m == 1)
    sin_sign = same * sign * np.where(real, -1 * (part_m == 1), part_m == 0)
    return cos_sign.astype(np.float32), sin_sign.astype(np.float32)


def cluster_kernel(core_ref, own, far, b0, b1, b2, b3, w_own, w_far, g, mine, other, b_ref, u_ref):
    at = 0
    for part in (b0, b1, b2, b3):
        b_ref[pl.ds(at, part.shape[0]), :] = part[...]
        at += part.shape[0]
    k_rows = b_ref.shape[0]
    width = u_ref.shape[0] // 4
    outs = 8 * width
    occupied = own.shape[1]
    contract = (((1,), (1,)), ((), ()))
    is_real = lax.broadcasted_iota(jnp.int32, (k_rows, occupied), 0) % (2 * width) < width
    ms = []
    for q_ref, w in ((own, w_own), (far, w_far)):
        m = lax.dot_general(b_ref[...], q_ref[0], contract, preferred_element_type=F32)
        turn = lax.dot_general(b_ref[...], q_ref[1], contract, preferred_element_type=F32)
        turn = jnp.where(is_real, pltpu.roll(turn, k_rows - width, 0), -pltpu.roll(turn, width, 0))
        ms.append((w[...] * (m + turn)).astype(BF16))
    us = []
    for q_ref, m in zip((own, far), ms):
        t = jnp.dot(g[...], m, preferred_element_type=F32)
        t = t[:outs] + t[outs:]
        t_high = t.astype(BF16)
        t_low = (t - t_high.astype(F32)).astype(BF16)
        half = outs // 2
        for part in range(2):
            rows = slice(part * half, (part + 1) * half)
            pair = jnp.concatenate([t_high[rows], t_low[rows]], 0)
            us.append(jnp.dot(pair, q_ref[part], preferred_element_type=F32))
    u = (us[0] + us[1]) + (us[2] + us[3])
    u_ref[...] = u[: outs // 2] + u[outs // 2 :]
    chips, _, columns = mine.shape
    for core in range(2):

        @pl.when(core_ref[0] == core)
        def _():
            for chip in range(chips):
                at = (2 * chip + core) * columns
                mine[chip] = u_ref[:, at : at + columns]
                at = (2 * chip + 1 - core) * columns
                other[chip] = u_ref[:, at : at + columns]


def shards(coefficients, class_weight, diff_class, frag_cells, block_pattern):
    own = coefficients[0]
    _, occupied, functions = own.shape
    yh, z, core = (lax.axis_index(name) for name in KA)
    band = lax.axis_index("yl") * PARTS[4] + lax.axis_index("x")
    width = occupied // (PARTS[3] * PARTS[4])
    kpoint_count = PARTS[0] * PARTS[1] * PARTS[2]
    up = [(i, (i + 1) % PARTS[1]) for i in range(PARTS[1])]
    down = [(j, i) for i, j in up]
    swap = [(0, 1), (1, 0)]

    block = lax.dynamic_slice_in_dim(own, band * width, width, 1).reshape(2 * width, functions)
    far = lax.ppermute(own, "yh", swap)
    blocks = [block]
    offsets = [0, -1, 1, -2, 2, -3, 3, -4]
    from_below = from_above = block
    for step in range(1, PARTS[1] // 2 + 1):
        from_below = lax.ppermute(from_below, "z", up)
        blocks.append(from_below)
        if step < PARTS[1] // 2:
            from_above = lax.ppermute(from_above, "z", down)
            blocks.append(from_above)
    split = 5
    first = jnp.concatenate(blocks[:split], 0)
    first_near = lax.ppermute(first, "core", swap)
    last = jnp.concatenate(blocks[split:], 0)
    last_near = lax.ppermute(last, "core", swap)

    order = offsets[:split] * 2 + offsets[split:] * 2
    cores = [0] * split + [1] * split + [0] * (len(offsets) - split) + [1] * (len(offsets) - split)
    cores = jnp.bitwise_xor(jnp.array(cores, jnp.int32), core)
    kpoints = (yh * PARTS[1] + jnp.bitwise_and(z + jnp.array(order, jnp.int32), PARTS[1] - 1)) * 2 + cores
    all_points = jnp.arange(kpoint_count, dtype=jnp.int32)
    high = lax.Precision.HIGHEST
    classes = (diff_class[:, :, None] == all_points).astype(F32)
    pair_weight = jnp.sum(classes * class_weight, axis=2)
    k_onehot = (kpoints[:, None] == all_points).astype(F32)
    q_points = (jnp.stack([yh, 1 - yh]) * PARTS[1] + z) * 2 + core
    q_onehot = (q_points[:, None] == all_points).astype(F32)
    weights = jnp.einsum("ka,ab,qb->qk", k_onehot, pair_weight, q_onehot, precision=high) / functions
    weights = jnp.repeat(weights, 2 * width, axis=1)[:, :, None]

    phase_index = frag_cells[:, None] * kpoints[None, :] % kpoint_count
    angles = 2.0 * jnp.pi * phase_index.astype(F32) / kpoint_count
    cells = frag_cells.shape[0]
    full = (2, cells, 2 * width, 2 * width * kpoints.shape[0])
    cosines = jnp.repeat(jnp.cos(angles) / kpoint_count, 2 * width, axis=1)[None, :, None, :]
    sines = jnp.repeat(jnp.sin(angles) / kpoint_count, 2 * width, axis=1)[None, :, None, :]
    cos_sign, sin_sign = (jnp.asarray(a.reshape(full)) for a in phase_signs(width, kpoints.shape[0]))
    g = (cos_sign * cosines + sin_sign * sines).reshape(8 * width, -1)
    g_high = g.astype(BF16)
    g_low = (g - g_high.astype(F32)).astype(BF16)
    g = jnp.concatenate([g_high, g_low], 0)

    chips = PARTS[0] * PARTS[1]
    columns = functions // kpoint_count
    piece = jax.ShapeDtypeStruct((chips, 4 * width, columns), F32)
    mine, other = pl.pallas_call(
        cluster_kernel,
        out_shape=(piece, piece),
        in_specs=[pl.BlockSpec(memory_space=pltpu.SMEM)] + [pl.BlockSpec(memory_space=pltpu.VMEM)] * 9,
        out_specs=(pl.BlockSpec(memory_space=pltpu.VMEM),) * 2,
        scratch_shapes=[
            pltpu.VMEM((2 * width * kpoints.shape[0], functions), BF16),
            pltpu.VMEM((4 * width, functions), F32),
        ],
        compiler_params=pltpu.CompilerParams(vmem_limit_bytes=32 * 2**20),
        cost_estimate=pl.CostEstimate(flops=3 * 10**9, bytes_accessed=10**7, transcendentals=0),
        name="cluster_terms",
    )(core[None], own, far, first, first_near, last, last_near, weights[0], weights[1], g)

    sums = mine + lax.ppermute(other, "core", swap)
    arrived = lax.all_to_all(sums, ("yh", "z"), 0, 0, tiled=True)
    cluster = jnp.sum(arrived, axis=0).reshape(cells, 2, width, columns)
    index = (yh * PARTS[1] + z) * 2 + core
    block_size = functions // block_pattern.shape[1]
    local_ids = (index * columns + jnp.arange(columns, dtype=jnp.int32)) // block_size
    block_ids = jnp.arange(block_pattern.shape[1], dtype=jnp.int32)
    onehot = (block_ids[:, None] == local_ids[None, :]).astype(F32)
    mask = jnp.dot(block_pattern.astype(F32), onehot, precision=high)
    return cluster * mask[:, None, None, :]


def solution(mesh):
    placed = (P(KA, None, None, None), P(), P(), P(), P())
    return jax.shard_map(
        shards,
        mesh=Mesh(mesh.devices.reshape(PARTS), AXES),
        in_specs=placed,
        out_specs=P(None, None, BAND, KA),
        check_vma=False,
    )
```

```python
import functools

import jax
import jax.numpy as jnp
import numpy as np
from jax import lax
from jax.experimental import pallas as pl
from jax.experimental.pallas import tpu as pltpu
from jax.sharding import Mesh
from jax.sharding import PartitionSpec as P

AXES = ("yh", "z", "core", "yl", "x")
KA = ("yh", "z", "core")
BAND = ("yl", "x")
PARTS = (2, 8, 2, 2, 4)
F32 = jnp.float32
BF16 = jnp.bfloat16


def phase_signs(width, blocks):
    rows = np.arange(8 * width)
    cols = np.arange(2 * blocks * width)
    partner, part = (rows // (4 * width))[:, None], (rows // width % 2)[:, None]
    part_m = (cols // width % 2)[None, :]
    same = (rows % width)[:, None] == (cols % width)[None, :]
    real = np.where(partner == 0, part == 0, part == 1)
    sign = np.where((partner == 1) & (part == 0), -1, 1)
    cos_sign = same * sign * np.where(real, part_m == 0, part_m == 1)
    sin_sign = same * sign * np.where(real, -1 * (part_m == 1), part_m == 0)
    return cos_sign.astype(np.float32), sin_sign.astype(np.float32)


def scaled_m(b, q_ref, w_ref, q, k_start, width):
    contract = (((1,), (1,)), ((), ()))
    m = lax.dot_general(b, q_ref[0], contract, preferred_element_type=F32)
    turn = lax.dot_general(b, q_ref[1], contract, preferred_element_type=F32)
    rows = m.shape[0]
    is_real = lax.broadcasted_iota(jnp.int32, m.shape, 0) % (2 * width) < width
    turn = jnp.where(is_real, pltpu.roll(turn, rows - width, 0), -pltpu.roll(turn, width, 0))
    m = m + turn
    blocks = range(rows // (2 * width))
    scaled = [m[k * 2 * width : (k + 1) * 2 * width] * w_ref[q, k_start + k] for k in blocks]
    return jnp.concatenate(scaled, 0).astype(BF16)


def phased(g_ref, m):
    t = jnp.dot(g_ref[...], m, preferred_element_type=F32)
    half = t.shape[0] // 2
    return t[:half] + t[half:]


def early_kernel(width, w, own, b0, b1, g, t_ref, b_ref):
    half = b0.shape[0]
    b_ref[:half, :] = b0[...]
    b_ref[half:, :] = b1[...]
    t_ref[...] = phased(g, scaled_m(b_ref[...], own, w, 0, 0, width))


def packed(u, at, columns):
    third = columns // 3
    tall = jnp.concatenate([u[:, at + p * third : at + (p + 1) * third] for p in range(3)], 0)
    rows = tall.shape[0] // 5
    return jnp.concatenate([tall[g * rows : (g + 1) * rows] for g in range(5)], 1)


def unpacked(value, columns):
    third = columns // 3
    tall = jnp.concatenate([value[:, g * third : (g + 1) * third] for g in range(5)], 0)
    rows = tall.shape[0] // 3
    return jnp.concatenate([tall[p * rows : (p + 1) * rows] for p in range(3)], 1)


def cluster_kernel(columns, core_ref, w, own, far, b0, b1, b2, b3, g0, g1, t_early, mine, other, b_ref, u_ref):
    at = 0
    for part in (b0, b1, b2, b3):
        b_ref[pl.ds(at, part.shape[0]), :] = part[...]
        at += part.shape[0]
    early = b0.shape[0] + b1.shape[0]
    width = u_ref.shape[0] // 4
    half = 4 * width
    m_far = scaled_m(b_ref[...], far, w, 1, 0, width)
    m_own = scaled_m(b_ref[early:, :], own, w, 0, early // (2 * width), width)
    t_far = phased(g0, m_far[:early]) + phased(g1, m_far[early:])
    t_own = t_early[...] + phased(g1, m_own)
    us = []
    for q_ref, t in ((own, t_own), (far, t_far)):
        t_high = t.astype(BF16)
        t_low = (t - t_high.astype(F32)).astype(BF16)
        for part in range(2):
            rows = slice(part * half, (part + 1) * half)
            pair = jnp.concatenate([t_high[rows], t_low[rows]], 0)
            us.append(jnp.dot(pair, q_ref[part], preferred_element_type=F32))
    u = (us[0] + us[1]) + (us[2] + us[3])
    u_ref[...] = u[:half] + u[half:]
    chips, _, lanes = mine.shape
    for core in range(2):

        @pl.when(core_ref[0] == core)
        def _():
            for chip in range(chips):
                for out, parity in ((mine, core), (other, 1 - core)):
                    piece = packed(u_ref[...], (2 * chip + parity) * columns, columns)
                    spare = jnp.zeros((piece.shape[0], lanes - piece.shape[1]), F32)
                    out[chip] = jnp.concatenate([piece, spare], 1)


def final_kernel(arrived, mask, out):
    total = arrived[0]
    for chip in range(1, arrived.shape[0]):
        total = total + arrived[chip]
    cells, width, parts, columns = out.shape
    value = unpacked(total, columns)
    for f in range(cells):
        for part in range(parts):
            for j in range(width):
                row = (f * parts + part) * width + j
                out[f, j, pl.ds(part, 1), :] = value[row : row + 1] * mask[pl.ds(f, 1), :]


def shards(coefficients, class_weight, diff_class, frag_cells, block_pattern):
    own = coefficients[0]
    _, occupied, functions = own.shape
    yh, z, core = (lax.axis_index(name) for name in KA)
    band = lax.axis_index("yl") * PARTS[4] + lax.axis_index("x")
    width = occupied // (PARTS[3] * PARTS[4])
    kpoint_count = PARTS[0] * PARTS[1] * PARTS[2]
    up = [(i, (i + 1) % PARTS[1]) for i in range(PARTS[1])]
    down = [(j, i) for i, j in up]
    swap = [(0, 1), (1, 0)]

    block = lax.dynamic_slice_in_dim(own, band * width, width, 1).reshape(2 * width, functions)
    far = lax.ppermute(own, "yh", swap)
    blocks = [block]
    offsets = [0, -1, 1, -2, 2, -3, 3, -4]
    from_below = from_above = block
    for step in range(1, PARTS[1] // 2):
        from_below = lax.ppermute(from_below, "z", up)
        from_above = lax.ppermute(from_above, "z", down)
        blocks += [from_below, from_above]
    cut = 24
    blocks.append(lax.ppermute(from_below[:cut], "z", up))
    blocks.append(lax.ppermute(from_above[cut:], "z", down))
    split = 5
    first = jnp.concatenate(blocks[:split], 0)
    first_near = lax.ppermute(first, "core", swap)
    last = jnp.concatenate(blocks[split:], 0)
    last_near = lax.ppermute(last, "core", swap)

    order = offsets[:split] * 2 + offsets[split:] * 2
    cores = [0] * split + [1] * split + [0] * (len(offsets) - split) + [1] * (len(offsets) - split)
    cores = jnp.bitwise_xor(jnp.array(cores, jnp.int32), core)
    kpoints = (yh * PARTS[1] + jnp.bitwise_and(z + jnp.array(order, jnp.int32), PARTS[1] - 1)) * 2 + cores
    all_points = jnp.arange(kpoint_count, dtype=jnp.int32)
    high = lax.Precision.HIGHEST
    classes = (diff_class[:, :, None] == all_points).astype(F32)
    pair_weight = jnp.sum(classes * class_weight, axis=2)
    k_onehot = (kpoints[:, None] == all_points).astype(F32)
    q_points = (jnp.stack([yh, 1 - yh]) * PARTS[1] + z) * 2 + core
    q_onehot = (q_points[:, None] == all_points).astype(F32)
    weights = jnp.einsum("ka,ab,qb->qk", k_onehot, pair_weight, q_onehot, precision=high) / functions

    phase_index = frag_cells[:, None] * kpoints[None, :] % kpoint_count
    angles = 2.0 * jnp.pi * phase_index.astype(F32) / kpoint_count
    cells = frag_cells.shape[0]
    full = (2, cells, 2 * width, 2 * width * kpoints.shape[0])
    cosines = jnp.repeat(jnp.cos(angles) / kpoint_count, 2 * width, axis=1)[None, :, None, :]
    sines = jnp.repeat(jnp.sin(angles) / kpoint_count, 2 * width, axis=1)[None, :, None, :]
    cos_sign, sin_sign = (jnp.asarray(a.reshape(full)) for a in phase_signs(width, kpoints.shape[0]))
    g = (cos_sign * cosines + sin_sign * sines).reshape(8 * width, -1)
    g_high = lax.reduce_precision(g, 8, 7)
    g = jnp.concatenate([g_high, g - g_high], 0).astype(BF16)
    early = 2 * split * 2 * width
    g0, g1 = g[:, :early], g[:, early:]

    vmem, smem = (pl.BlockSpec(memory_space=space) for space in (pltpu.VMEM, pltpu.SMEM))
    t_early = pl.pallas_call(
        functools.partial(early_kernel, width),
        out_shape=jax.ShapeDtypeStruct((8 * width, occupied), F32),
        in_specs=[smem] + [vmem] * 4,
        out_specs=vmem,
        scratch_shapes=[pltpu.VMEM((early, functions), BF16)],
        compiler_params=pltpu.CompilerParams(vmem_limit_bytes=16 * 2**20),
        cost_estimate=pl.CostEstimate(flops=10**9, bytes_accessed=4 * 10**6, transcendentals=0),
        name="early_terms",
    )(weights, own, first, first_near, g0)

    chips = PARTS[0] * PARTS[1]
    columns = functions // kpoint_count
    piece = jax.ShapeDtypeStruct((chips, 4 * width * 3 // 5, 128), F32)
    mine, other = pl.pallas_call(
        functools.partial(cluster_kernel, columns),
        out_shape=(piece, piece),
        in_specs=[smem] * 2 + [vmem] * 9,
        out_specs=(vmem, vmem),
        scratch_shapes=[
            pltpu.VMEM((2 * width * kpoints.shape[0], functions), BF16),
            pltpu.VMEM((4 * width, functions), F32),
        ],
        compiler_params=pltpu.CompilerParams(vmem_limit_bytes=24 * 2**20),
        cost_estimate=pl.CostEstimate(flops=3 * 10**9, bytes_accessed=10**7, transcendentals=0),
        name="cluster_terms",
    )(core[None], weights, own, far, first, first_near, last, last_near, g0, g1, t_early)

    sums = mine + lax.ppermute(other, "core", swap)
    arrived = lax.all_to_all(sums, ("yh", "z"), 0, 0, tiled=True)
    index = (yh * PARTS[1] + z) * 2 + core
    block_size = functions // block_pattern.shape[1]
    local_ids = (index * columns + jnp.arange(columns, dtype=jnp.int32)) // block_size
    block_ids = jnp.arange(block_pattern.shape[1], dtype=jnp.int32)
    onehot = (block_ids[:, None] == local_ids[None, :]).astype(F32)
    mask = jnp.dot(block_pattern.astype(F32), onehot, precision=high)
    cluster = pl.pallas_call(
        final_kernel,
        out_shape=jax.ShapeDtypeStruct((cells, width, 2, columns), F32),
        in_specs=[vmem] * 2,
        out_specs=vmem,
        compiler_params=pltpu.CompilerParams(vmem_limit_bytes=4 * 2**20),
        name="sum_and_mask",
    )(arrived, mask)
    return jnp.transpose(cluster, (0, 2, 1, 3))


def solution(mesh):
    placed = (P(KA, None, None, None), P(), P(), P(), P())
    return jax.shard_map(
        shards,
        mesh=Mesh(mesh.devices.reshape(PARTS), AXES),
        in_specs=placed,
        out_specs=P(None, None, BAND, KA),
        check_vma=False,
    )
```

```python
import functools

import jax
import jax.numpy as jnp
import numpy as np
from jax import lax
from jax.experimental import pallas as pl
from jax.experimental.pallas import tpu as pltpu
from jax.sharding import Mesh
from jax.sharding import PartitionSpec as P

AXES = ("yh", "z", "core", "yl", "x")
KA = ("yh", "z", "core")
BAND = ("yl", "x")
PARTS = (2, 8, 2, 2, 4)
F32 = jnp.float32
BF16 = jnp.bfloat16


def prep_kernel(width, functions, k_points, ids, cells, diff_class, class_weight, cos_table, sin_table, w_ref, g0, g1):
    yh, z, core = ids[0], ids[1], ids[2]
    group = 2 * width
    count = len(k_points)
    rows, lanes = 4 * width, group * count
    points = []
    for offset, flip in k_points:
        points.append((yh * PARTS[1] + lax.rem(z + offset + PARTS[1], PARTS[1])) * 2 + (1 - core if flip else core))
    for q, row in enumerate((yh, 1 - yh)):
        q_point = (row * PARTS[1] + z) * 2 + core
        for at, point in enumerate(points):
            weight = jnp.full((group, 1), class_weight[diff_class[point, q_point]], F32)
            w_ref[q, pl.ds(at * group, group), :] = weight / functions
    lane = lax.broadcasted_iota(jnp.int32, (1, lanes), 1)
    tables = []
    for f in range(2):
        cosines = jnp.zeros((1, lanes), F32)
        sines = jnp.zeros((1, lanes), F32)
        for at, point in enumerate(points):
            here = (lane >= at * group) & (lane < (at + 1) * group)
            index = lax.rem(point * cells[f], cos_table.shape[0])
            cosines = jnp.where(here, cos_table[index], cosines)
            sines = jnp.where(here, sin_table[index], sines)
        tables.append((cosines, sines))
    row = lax.broadcasted_iota(jnp.int32, (rows, lanes), 0)
    col = lax.broadcasted_iota(jnp.int32, (rows, lanes), 1)
    first = row < group
    cosines = jnp.where(first, tables[0][0], tables[1][0])
    sines = jnp.where(first, tables[0][1], tables[1][1])
    real, real_m = row % group < width, col % group < width
    value = jnp.where(real == real_m, cosines, jnp.where(real, -sines, sines))
    value = jnp.where(row % width == col % width, value, 0.0)
    high = value.astype(BF16)
    low = (value - high.astype(F32)).astype(BF16)
    both = jnp.concatenate([high, low], 0)
    g0[...] = both[:, : g0.shape[1]]
    g1[...] = both[:, g0.shape[1] :]


def turned(value, width, sign):
    rows = value.shape[0]
    real = lax.broadcasted_iota(jnp.int32, value.shape, 0) % (2 * width) < width
    up, down = pltpu.roll(value, rows - width, 0), pltpu.roll(value, width, 0)
    return jnp.where(real, up, -down) if sign > 0 else jnp.where(real, -up, down)


def part_of_t(b, q_ref, w, g, width):
    contract = (((1,), (1,)), ((), ()))
    m = lax.dot_general(b, q_ref[0], contract, preferred_element_type=F32)
    m = m + turned(lax.dot_general(b, q_ref[1], contract, preferred_element_type=F32), width, 1)
    t = jnp.dot(g, (w * m).astype(BF16), preferred_element_type=F32)
    half = t.shape[0] // 2
    return t[:half] + t[half:]


def first_kernel(width, q, q_ref, b0, b1, w, g, t_ref, b_ref):
    half = b0.shape[0]
    b_ref[:half, :] = b0[...]
    b_ref[half:, :] = b1[...]
    t_ref[...] = part_of_t(b_ref[...], q_ref, w[q, : 2 * half, :], g[...], width)


def last_kernel(width, own, far, b0, b1, w, g, t_own, t_far, t_ref, b_ref):
    half = b0.shape[0]
    b_ref[:half, :] = b0[...]
    b_ref[half:, :] = b1[...]
    start = w.shape[1] - 2 * half
    for q, (q_ref, t) in enumerate(((own, t_own), (far, t_far))):
        t_ref[q] = t[...] + part_of_t(b_ref[...], q_ref, w[q, start:, :], g[...], width)


def packed(u, at, columns):
    third = columns // 3
    tall = jnp.concatenate([u[:, at + p * third : at + (p + 1) * third] for p in range(3)], 0)
    rows = tall.shape[0] // 5
    return jnp.concatenate([tall[g * rows : (g + 1) * rows] for g in range(5)], 1)


def unpacked(value, columns):
    third = columns // 3
    tall = jnp.concatenate([value[:, g * third : (g + 1) * third] for g in range(5)], 0)
    rows = tall.shape[0] // 3
    return jnp.concatenate([tall[p * rows : (p + 1) * rows] for p in range(3)], 1)


def cluster_kernel(width, columns, ids, own, far, near, diag, t, t_yh, t_core, t_diag, out, u_ref):
    yh, core = ids[0], ids[2]
    chips, _, lanes = out.shape
    span = 2 * chips * columns
    shift = span % 128
    window = pl.ds(pl.multiple_of(yh * (span - shift), 128), span + shift)
    half = 4 * width
    total = None
    sums = (
        (own, t[0] + t_yh[1]),
        (far, t[1] + t_yh[0]),
        (near, t_core[0] + t_diag[1]),
        (diag, t_core[1] + t_diag[0]),
    )
    for q_ref, value in sums:
        for part in range(2):
            piece = value if part == 0 else turned(value, width, -1)
            high = piece.astype(BF16)
            low = (piece - high.astype(F32)).astype(BF16)
            u = jnp.dot(jnp.concatenate([high, low], 0), q_ref[part, :, window], preferred_element_type=F32)
            total = u if total is None else total + u
    u_ref[...] = total[:half] + total[half:]
    for row in range(2):
        for parity in range(2):

            @pl.when((yh == row) & (core == parity))
            def _():
                for chip in range(chips):
                    piece = packed(u_ref[...], (2 * chip + parity) * columns + row * shift, columns)
                    spare = jnp.zeros((piece.shape[0], lanes - piece.shape[1]), F32)
                    out[chip] = jnp.concatenate([piece, spare], 1)


def final_kernel(arrived, mask, out):
    total = arrived[0]
    for chip in range(1, arrived.shape[0]):
        total = total + arrived[chip]
    cells, width, parts, columns = out.shape
    value = unpacked(total, columns)
    for f in range(cells):
        for part in range(parts):
            for j in range(width):
                row = (f * parts + part) * width + j
                out[f, j, pl.ds(part, 1), :] = value[row : row + 1] * mask[pl.ds(f, 1), :]


def call(kernel, name, shapes, specs, scratch=(), mib=16, flops=0):
    return pl.pallas_call(
        kernel,
        out_shape=shapes,
        in_specs=[pl.BlockSpec(memory_space=space) for space in specs],
        out_specs=jax.tree.map(lambda _: pl.BlockSpec(memory_space=pltpu.VMEM), shapes),
        scratch_shapes=scratch,
        compiler_params=pltpu.CompilerParams(vmem_limit_bytes=mib * 2**20),
        cost_estimate=pl.CostEstimate(flops=flops, bytes_accessed=2**20, transcendentals=0),
        name=name,
    )


def shards(coefficients, class_weight, diff_class, frag_cells, block_pattern):
    own = coefficients[0]
    _, occupied, functions = own.shape
    yh, z, core = (lax.axis_index(name) for name in KA)
    band = lax.axis_index("yl") * PARTS[4] + lax.axis_index("x")
    width = occupied // (PARTS[3] * PARTS[4])
    group = 2 * width
    kpoint_count = PARTS[0] * PARTS[1] * PARTS[2]
    cells = frag_cells.shape[0]
    up = [(i, (i + 1) % PARTS[1]) for i in range(PARTS[1])]
    down = [(j, i) for i, j in up]
    swap = [(0, 1), (1, 0)]
    cross = [(0, 3), (1, 2), (2, 1), (3, 0)]
    vmem, smem = pltpu.VMEM, pltpu.SMEM

    far = lax.ppermute(own, "yh", swap)
    near = lax.ppermute(own, "core", swap)
    diag = lax.ppermute(far, "core", swap)
    block = lax.dynamic_slice_in_dim(own, band * width, width, 1).reshape(group, functions)
    blocks = [block]
    offsets = [0, -1, 1, -2, 2, -3, 3, -4]
    from_below = from_above = block
    for step in range(1, PARTS[1] // 2):
        from_below = lax.ppermute(from_below, "z", up)
        from_above = lax.ppermute(from_above, "z", down)
        blocks += [from_below, from_above]
    cut = 24
    blocks.append(lax.ppermute(from_below[:cut], "z", up))
    blocks.append(lax.ppermute(from_above[cut:], "z", down))
    split = 5
    first = jnp.concatenate(blocks[:split], 0)
    first_near = lax.ppermute(first, "core", swap)
    last = jnp.concatenate(blocks[split:], 0)
    last_near = lax.ppermute(last, "core", swap)

    k_points = []
    for these in (offsets[:split], offsets[split:]):
        k_points += [(offset, False) for offset in these] + [(offset, True) for offset in these]
    early, late = 2 * split * group, 2 * (len(offsets) - split) * group
    angles = 2.0 * np.pi * np.arange(kpoint_count) / kpoint_count
    tables = [jnp.asarray((f(angles) / kpoint_count).astype(np.float32)) for f in (np.cos, np.sin)]
    ids = jnp.stack([yh, z, core]).astype(jnp.int32)
    weights, g_first, g_last = call(
        functools.partial(prep_kernel, width, functions, k_points),
        "phases",
        (
            jax.ShapeDtypeStruct((2, early + late, 1), F32),
            jax.ShapeDtypeStruct((8 * width, early), BF16),
            jax.ShapeDtypeStruct((8 * width, late), BF16),
        ),
        [smem] * 6,
    )(ids, frag_cells, diff_class, class_weight, *tables)

    one = jax.ShapeDtypeStruct((4 * width, occupied), F32)
    t_first = []
    for q, (name, q_block) in enumerate((("own_first", own), ("far_first", far))):
        t_first.append(
            call(
                functools.partial(first_kernel, width, q),
                name,
                one,
                [vmem] * 5,
                [pltpu.VMEM((early, functions), BF16)],
                flops=(1 + 20 * q) * 10**9,
            )(q_block, first, first_near, weights, g_first)
        )
    t = call(
        functools.partial(last_kernel, width),
        "last_terms",
        jax.ShapeDtypeStruct((2,) + one.shape, F32),
        [vmem] * 8,
        [pltpu.VMEM((late, functions), BF16)],
        flops=10**9,
    )(own, far, last, last_near, weights, g_last, *t_first)

    t_core = lax.ppermute(t, "core", swap)
    t_yh = lax.ppermute(t, "yh", swap)
    t_diag = lax.ppermute(t, ("yh", "core"), cross)
    chips = PARTS[1]
    columns = functions // kpoint_count
    span = 2 * chips * columns
    pieces = call(
        functools.partial(cluster_kernel, width, columns),
        "cluster_terms",
        jax.ShapeDtypeStruct((chips, 4 * width * 3 // 5, 128), F32),
        [smem] + [vmem] * 8,
        [pltpu.VMEM((4 * width, span + span % 128), F32)],
        flops=10**9,
    )(ids, own, far, near, diag, t, t_yh, t_core, t_diag)

    arrived = lax.all_to_all(pieces, "z", 0, 0, tiled=True)
    index = (yh * PARTS[1] + z) * 2 + core
    block_size = functions // block_pattern.shape[1]
    local_ids = (index * columns + jnp.arange(columns, dtype=jnp.int32)) // block_size
    block_ids = jnp.arange(block_pattern.shape[1], dtype=jnp.int32)
    onehot = (block_ids[:, None] == local_ids[None, :]).astype(F32)
    mask = jnp.dot(block_pattern.astype(F32), onehot, precision=lax.Precision.HIGHEST)
    cluster = call(
        final_kernel,
        "sum_and_mask",
        jax.ShapeDtypeStruct((cells, width, 2, columns), F32),
        [vmem] * 2,
        mib=4,
    )(arrived, mask)
    return jnp.transpose(cluster, (0, 2, 1, 3))


def solution(mesh):
    placed = (P(KA, None, None, None), P(), P(), P(), P())
    return jax.shard_map(
        shards,
        mesh=Mesh(mesh.devices.reshape(PARTS), AXES),
        in_specs=placed,
        out_specs=P(None, None, BAND, KA),
        check_vma=False,
    )
```

```python
import functools

import jax
import jax.numpy as jnp
import numpy as np
from jax import lax
from jax.experimental import pallas as pl
from jax.experimental.pallas import tpu as pltpu
from jax.sharding import Mesh
from jax.sharding import PartitionSpec as P

AXES = ("yh", "z", "core", "yl", "x")
KA = ("yh", "z", "core")
BAND = ("yl", "x")
PARTS = (2, 8, 2, 2, 4)
F32 = jnp.float32
BF16 = jnp.bfloat16


def prep_kernel(width, functions, k_points, ids, cells, diff_class, class_weight, cos_table, sin_table, w_ref, g0, g1):
    yh, z, core = ids[0], ids[1], ids[2]
    group = 2 * width
    count = len(k_points)
    rows, lanes = 4 * width, group * count
    points = []
    for offset, flip in k_points:
        points.append((yh * PARTS[1] + lax.rem(z + offset + PARTS[1], PARTS[1])) * 2 + (1 - core if flip else core))
    for q, row in enumerate((yh, 1 - yh)):
        q_point = (row * PARTS[1] + z) * 2 + core
        for at, point in enumerate(points):
            weight = jnp.full((group, 1), class_weight[diff_class[point, q_point]], F32)
            w_ref[q, pl.ds(at * group, group), :] = weight / functions
    lane = lax.broadcasted_iota(jnp.int32, (1, lanes), 1)
    tables = []
    for f in range(2):
        cosines = jnp.zeros((1, lanes), F32)
        sines = jnp.zeros((1, lanes), F32)
        for at, point in enumerate(points):
            here = (lane >= at * group) & (lane < (at + 1) * group)
            index = lax.rem(point * cells[f], cos_table.shape[0])
            cosines = jnp.where(here, cos_table[index], cosines)
            sines = jnp.where(here, sin_table[index], sines)
        tables.append((cosines, sines))
    row = lax.broadcasted_iota(jnp.int32, (rows, lanes), 0)
    col = lax.broadcasted_iota(jnp.int32, (rows, lanes), 1)
    first = row < group
    cosines = jnp.where(first, tables[0][0], tables[1][0])
    sines = jnp.where(first, tables[0][1], tables[1][1])
    real, real_m = row % group < width, col % group < width
    value = jnp.where(real == real_m, cosines, jnp.where(real, -sines, sines))
    value = jnp.where(row % width == col % width, value, 0.0)
    high = value.astype(BF16)
    low = (value - high.astype(F32)).astype(BF16)
    both = jnp.concatenate([high, low], 0)
    g0[...] = both[:, : g0.shape[1]]
    g1[...] = both[:, g0.shape[1] :]


def turned(value, width, sign):
    rows = value.shape[0]
    real = lax.broadcasted_iota(jnp.int32, value.shape, 0) % (2 * width) < width
    up, down = pltpu.roll(value, rows - width, 0), pltpu.roll(value, width, 0)
    return jnp.where(real, up, -down) if sign > 0 else jnp.where(real, -up, down)


def part_of_t(b, q_ref, w, g, width):
    contract = (((1,), (1,)), ((), ()))
    m = lax.dot_general(b, q_ref[0], contract, preferred_element_type=F32)
    m = m + turned(lax.dot_general(b, q_ref[1], contract, preferred_element_type=F32), width, 1)
    t = jnp.dot(g, (w * m).astype(BF16), preferred_element_type=F32)
    half = t.shape[0] // 2
    return t[:half] + t[half:]


def first_kernel(width, q, q_ref, b0, b1, w, g, t_ref, b_ref):
    half = b0.shape[0]
    b_ref[:half, :] = b0[...]
    b_ref[half:, :] = b1[...]
    t_ref[...] = part_of_t(b_ref[...], q_ref, w[q, : 2 * half, :], g[...], width)


def last_kernel(width, own, far, b0, b1, w, g, t_own, t_far, t_ref, b_ref):
    half = b0.shape[0]
    b_ref[:half, :] = b0[...]
    b_ref[half:, :] = b1[...]
    start = w.shape[1] - 2 * half
    for q, (q_ref, t) in enumerate(((own, t_own), (far, t_far))):
        t_ref[q] = t[...] + part_of_t(b_ref[...], q_ref, w[q, start:, :], g[...], width)


def packed(u, at, columns):
    third = columns // 3
    tall = jnp.concatenate([u[:, at + p * third : at + (p + 1) * third] for p in range(3)], 0)
    rows = tall.shape[0] // 5
    return jnp.concatenate([tall[g * rows : (g + 1) * rows] for g in range(5)], 1)


def unpacked(value, columns):
    third = columns // 3
    tall = jnp.concatenate([value[:, g * third : (g + 1) * third] for g in range(5)], 0)
    rows = tall.shape[0] // 3
    return jnp.concatenate([tall[p * rows : (p + 1) * rows] for p in range(3)], 1)


def cluster_kernel(width, columns, ids, own, far, near, diag, t, t_yh, t_core, t_diag, out, u_ref):
    yh, core = ids[0], ids[2]
    chips, _, lanes = out.shape
    span = 2 * chips * columns
    shift = span % 128
    window = pl.ds(pl.multiple_of(yh * (span - shift), 128), span + shift)
    half = 4 * width
    total = None
    sums = (
        (own, t[0] + t_yh[1]),
        (far, t[1] + t_yh[0]),
        (near, t_core[0] + t_diag[1]),
        (diag, t_core[1] + t_diag[0]),
    )
    for q_ref, value in sums:
        for part in range(2):
            piece = value if part == 0 else turned(value, width, -1)
            high = piece.astype(BF16)
            low = (piece - high.astype(F32)).astype(BF16)
            u = jnp.dot(jnp.concatenate([high, low], 0), q_ref[part, :, window], preferred_element_type=F32)
            total = u if total is None else total + u
    u_ref[...] = total[:half] + total[half:]
    for row in range(2):
        for parity in range(2):

            @pl.when((yh == row) & (core == parity))
            def _():
                for chip in range(chips):
                    piece = packed(u_ref[...], (2 * chip + parity) * columns + row * shift, columns)
                    spare = jnp.zeros((piece.shape[0], lanes - piece.shape[1]), F32)
                    out[chip] = jnp.concatenate([piece, spare], 1)


def final_kernel(arrived, mask, out):
    total = arrived[0]
    for chip in range(1, arrived.shape[0]):
        total = total + arrived[chip]
    cells, width, parts, columns = out.shape
    value = unpacked(total, columns)
    for f in range(cells):
        for part in range(parts):
            for j in range(width):
                row = (f * parts + part) * width + j
                out[f, j, pl.ds(part, 1), :] = value[row : row + 1] * mask[pl.ds(f, 1), :]


def call(kernel, name, shapes, specs, scratch=(), mib=16, flops=0):
    return pl.pallas_call(
        kernel,
        out_shape=shapes,
        in_specs=[pl.BlockSpec(memory_space=space) for space in specs],
        out_specs=jax.tree.map(lambda _: pl.BlockSpec(memory_space=pltpu.VMEM), shapes),
        scratch_shapes=scratch,
        compiler_params=pltpu.CompilerParams(vmem_limit_bytes=mib * 2**20),
        cost_estimate=pl.CostEstimate(flops=flops, bytes_accessed=2**20, transcendentals=0),
        name=name,
    )


def shards(coefficients, class_weight, diff_class, frag_cells, block_pattern):
    own = coefficients[0]
    _, occupied, functions = own.shape
    yh, z, core = (lax.axis_index(name) for name in KA)
    band = lax.axis_index("yl") * PARTS[4] + lax.axis_index("x")
    width = occupied // (PARTS[3] * PARTS[4])
    group = 2 * width
    kpoint_count = PARTS[0] * PARTS[1] * PARTS[2]
    cells = frag_cells.shape[0]
    up = [(i, (i + 1) % PARTS[1]) for i in range(PARTS[1])]
    down = [(j, i) for i, j in up]
    swap = [(0, 1), (1, 0)]
    right = [(i, (i + 1) % PARTS[4]) for i in range(PARTS[4])]
    left = [(j, i) for i, j in right]
    vmem, smem = pltpu.VMEM, pltpu.SMEM

    x = lax.axis_index("x")
    quarters = own.reshape(PARTS[4], -1, functions)
    quarter = lax.ppermute(lax.dynamic_index_in_dim(quarters, x, 0, keepdims=False), "yh", swap)
    near = lax.ppermute(own, "core", swap)
    block = lax.dynamic_slice_in_dim(own, band * width, width, 1).reshape(group, functions)
    blocks = [block]
    offsets = [0, -1, 1, -2, 2, -3, 3, -4]
    from_below = from_above = block
    for step in range(1, PARTS[1] // 2):
        from_below = lax.ppermute(from_below, "z", up)
        from_above = lax.ppermute(from_above, "z", down)
        blocks += [from_below, from_above]
        if step == 2:
            held = (from_below, from_above, quarter, near)
            from_below, from_above, quarter, near = lax.optimization_barrier(held)
            from_left = lax.ppermute(quarter, "x", right)
            from_right = lax.ppermute(quarter, "x", left)
    held = (from_below, from_above, from_left, from_right)
    from_below, from_above, from_left, from_right = lax.optimization_barrier(held)
    mid = quarter.shape[0] // 2
    from_left_2 = lax.ppermute(from_left[:mid], "x", right)
    from_right_2 = lax.ppermute(from_right[mid:], "x", left)
    far = jnp.zeros(quarters.shape, BF16)
    for value, distance, row in (
        (quarter, 0, 0),
        (from_left, 3, 0),
        (from_right, 1, 0),
        (from_left_2, 2, 0),
        (from_right_2, 2, mid),
    ):
        slot = jnp.bitwise_and(x + distance, PARTS[4] - 1)
        far = lax.dynamic_update_slice(far, value[None], (slot, row, 0))
    far = far.reshape(own.shape)
    diag = lax.ppermute(far, "core", swap)
    cut = 24
    blocks.append(lax.ppermute(from_below[:cut], "z", up))
    blocks.append(lax.ppermute(from_above[cut:], "z", down))
    split = 5
    first = jnp.concatenate(blocks[:split], 0)
    first_near = lax.ppermute(first, "core", swap)
    last = jnp.concatenate(blocks[split:], 0)
    last_near = lax.ppermute(last, "core", swap)

    k_points = []
    for these in (offsets[:split], offsets[split:]):
        k_points += [(offset, False) for offset in these] + [(offset, True) for offset in these]
    early, late = 2 * split * group, 2 * (len(offsets) - split) * group
    angles = 2.0 * np.pi * np.arange(kpoint_count) / kpoint_count
    tables = [jnp.asarray((f(angles) / kpoint_count).astype(np.float32)) for f in (np.cos, np.sin)]
    ids = jnp.stack([yh, z, core]).astype(jnp.int32)
    later_ids, _ = lax.optimization_barrier((ids, last))
    weights, g_first, g_last = call(
        functools.partial(prep_kernel, width, functions, k_points),
        "phases",
        (
            jax.ShapeDtypeStruct((2, early + late, 1), F32),
            jax.ShapeDtypeStruct((8 * width, early), BF16),
            jax.ShapeDtypeStruct((8 * width, late), BF16),
        ),
        [smem] * 6,
    )(later_ids, frag_cells, diff_class, class_weight, *tables)

    one = jax.ShapeDtypeStruct((4 * width, occupied), F32)
    t_first = []
    for q, (name, q_block) in enumerate((("own_first", own), ("far_first", far))):
        t_first.append(
            call(
                functools.partial(first_kernel, width, q),
                name,
                one,
                [vmem] * 5,
                [pltpu.VMEM((early, functions), BF16)],
                flops=(1 + 20 * q) * 10**9,
            )(q_block, first, first_near, weights, g_first)
        )
    t = call(
        functools.partial(last_kernel, width),
        "last_terms",
        jax.ShapeDtypeStruct((2,) + one.shape, F32),
        [vmem] * 8,
        [pltpu.VMEM((late, functions), BF16)],
        flops=10**9,
    )(own, far, last, last_near, weights, g_last, *t_first)

    t_core = lax.ppermute(t, "core", swap)
    t_yh = lax.ppermute(t, "yh", swap)
    t_diag = lax.ppermute(t_yh, "core", swap)
    chips = PARTS[1]
    columns = functions // kpoint_count
    span = 2 * chips * columns
    pieces = call(
        functools.partial(cluster_kernel, width, columns),
        "cluster_terms",
        jax.ShapeDtypeStruct((chips, 4 * width * 3 // 5, 128), F32),
        [smem] + [vmem] * 8,
        [pltpu.VMEM((4 * width, span + span % 128), F32)],
        flops=10**9,
    )(ids, own, far, near, diag, t, t_yh, t_core, t_diag)

    arrived = lax.all_to_all(pieces, "z", 0, 0, tiled=True)
    index = (yh * PARTS[1] + z) * 2 + core
    block_size = functions // block_pattern.shape[1]
    local_ids = (index * columns + jnp.arange(columns, dtype=jnp.int32)) // block_size
    block_ids = jnp.arange(block_pattern.shape[1], dtype=jnp.int32)
    onehot = (block_ids[:, None] == local_ids[None, :]).astype(F32)
    mask = jnp.dot(block_pattern.astype(F32), onehot, precision=lax.Precision.HIGHEST)
    cluster = call(
        final_kernel,
        "sum_and_mask",
        jax.ShapeDtypeStruct((cells, width, 2, columns), F32),
        [vmem] * 2,
        mib=4,
    )(arrived, mask)
    return jnp.transpose(cluster, (0, 2, 1, 3))


def solution(mesh):
    placed = (P(KA, None, None, None), P(), P(), P(), P())
    return jax.shard_map(
        shards,
        mesh=Mesh(mesh.devices.reshape(PARTS), AXES),
        in_specs=placed,
        out_specs=P(None, None, BAND, KA),
        check_vma=False,
    )
```

```python
import functools

import jax
import jax.numpy as jnp
import numpy as np
from jax import lax
from jax.experimental import pallas as pl
from jax.experimental.pallas import tpu as pltpu
from jax.sharding import Mesh
from jax.sharding import PartitionSpec as P

AXES = ("yh", "z", "core", "yl", "x")
KA = ("yh", "z", "core")
BAND = ("yl", "x")
PARTS = (2, 8, 2, 2, 4)
F32 = jnp.float32
BF16 = jnp.bfloat16


def prep_kernel(width, functions, k_points, ids, cells, diff_class, class_weight, cos_table, sin_table, w_ref, g0, g1):
    yh, z, core = ids[0], ids[1], ids[2]
    group = 2 * width
    count = len(k_points)
    rows, lanes = 4 * width, group * count
    points = []
    for offset, flip in k_points:
        points.append((yh * PARTS[1] + lax.rem(z + offset + PARTS[1], PARTS[1])) * 2 + (1 - core if flip else core))
    for q, row in enumerate((yh, 1 - yh)):
        q_point = (row * PARTS[1] + z) * 2 + core
        for at, point in enumerate(points):
            weight = jnp.full((group, 1), class_weight[diff_class[point, q_point]], F32)
            w_ref[q, pl.ds(at * group, group), :] = weight / functions
    lane = lax.broadcasted_iota(jnp.int32, (1, lanes), 1)
    tables = []
    for f in range(2):
        cosines = jnp.zeros((1, lanes), F32)
        sines = jnp.zeros((1, lanes), F32)
        for at, point in enumerate(points):
            here = (lane >= at * group) & (lane < (at + 1) * group)
            index = lax.rem(point * cells[f], cos_table.shape[0])
            cosines = jnp.where(here, cos_table[index], cosines)
            sines = jnp.where(here, sin_table[index], sines)
        tables.append((cosines, sines))
    row = lax.broadcasted_iota(jnp.int32, (rows, lanes), 0)
    col = lax.broadcasted_iota(jnp.int32, (rows, lanes), 1)
    first = row < group
    cosines = jnp.where(first, tables[0][0], tables[1][0])
    sines = jnp.where(first, tables[0][1], tables[1][1])
    real, real_m = row % group < width, col % group < width
    value = jnp.where(real == real_m, cosines, jnp.where(real, -sines, sines))
    value = jnp.where(row % width == col % width, value, 0.0)
    high = value.astype(BF16)
    low = (value - high.astype(F32)).astype(BF16)
    both = jnp.concatenate([high, low], 0)
    g0[...] = both[:, : g0.shape[1]]
    g1[...] = both[:, g0.shape[1] :]


def turned(value, width, sign):
    rows = value.shape[0]
    real = lax.broadcasted_iota(jnp.int32, value.shape, 0) % (2 * width) < width
    up, down = pltpu.roll(value, rows - width, 0), pltpu.roll(value, width, 0)
    return jnp.where(real, up, -down) if sign > 0 else jnp.where(real, -up, down)


def part_of_t(b, parts, swapped, w, g, width):
    contract = (((1,), (1,)), ((), ()))
    real, imag = (lax.dot_general(b, part, contract, preferred_element_type=F32) for part in parts)
    if swapped is not None:
        swap = jnp.full(real.shape, swapped) > 0
        real, imag = jnp.where(swap, imag, real), jnp.where(swap, real, imag)
    m = real + turned(imag, width, 1)
    t = jnp.dot(g, (w * m).astype(BF16), preferred_element_type=F32)
    half = t.shape[0] // 2
    return t[:half] + t[half:]


def own_kernel(width, own, b0, b1, w, g, t_ref, b_ref):
    half = b0.shape[0]
    b_ref[:half, :] = b0[...]
    b_ref[half:, :] = b1[...]
    t_ref[...] = part_of_t(b_ref[...], (own[0], own[1]), None, w[0, : 2 * half, :], g[...], width)


def far_kernel(width, ids, far_a, far_b, b0, b1, w, g, t_ref, b_ref):
    half = b0.shape[0]
    b_ref[:half, :] = b0[...]
    b_ref[half:, :] = b1[...]
    t_ref[...] = part_of_t(b_ref[...], (far_a[...], far_b[...]), ids[3], w[1, : 2 * half, :], g[...], width)


def last_kernel(width, ids, own, far_a, far_b, b0, b1, w, g, t_own, t_far, t_ref, b_ref):
    half = b0.shape[0]
    b_ref[:half, :] = b0[...]
    b_ref[half:, :] = b1[...]
    b = b_ref[...]
    start = w.shape[1] - 2 * half
    t_ref[0] = t_own[...] + part_of_t(b, (own[0], own[1]), None, w[0, start:, :], g[...], width)
    t_ref[1] = t_far[...] + part_of_t(b, (far_a[...], far_b[...]), ids[3], w[1, start:, :], g[...], width)


def packed(u, at, columns):
    third = columns // 3
    tall = jnp.concatenate([u[:, at + p * third : at + (p + 1) * third] for p in range(3)], 0)
    rows = tall.shape[0] // 5
    return jnp.concatenate([tall[g * rows : (g + 1) * rows] for g in range(5)], 1)


def unpacked(value, columns):
    third = columns // 3
    tall = jnp.concatenate([value[:, g * third : (g + 1) * third] for g in range(5)], 0)
    rows = tall.shape[0] // 3
    return jnp.concatenate([tall[p * rows : (p + 1) * rows] for p in range(3)], 1)


def cluster_kernel(width, columns, ids, own, far_a, far_b, t, t_yh, mine, other, u_ref):
    yh, core, swapped = ids[0], ids[2], ids[3]
    chips, _, lanes = mine.shape
    span = 2 * chips * columns
    shift = span % 128
    window = pl.ds(pl.multiple_of(yh * (span - shift), 128), span + shift)
    half = 4 * width
    t_own, t_far = t[0] + t_yh[1], t[1] + t_yh[0]
    own_2, far_2 = turned(t_own, width, -1), turned(t_far, width, -1)
    swap = jnp.full(t_far.shape, swapped) > 0
    total = None
    for value, data in (
        (t_own, own[0, :, window]),
        (own_2, own[1, :, window]),
        (jnp.where(swap, far_2, t_far), far_a[:, window]),
        (jnp.where(swap, t_far, far_2), far_b[:, window]),
    ):
        high = value.astype(BF16)
        low = (value - high.astype(F32)).astype(BF16)
        u = jnp.dot(jnp.concatenate([high, low], 0), data, preferred_element_type=F32)
        total = u if total is None else total + u
    u_ref[...] = total[:half] + total[half:]
    for row in range(2):
        for parity in range(2):

            @pl.when((yh == row) & (core == parity))
            def _():
                for chip in range(chips):
                    for out, odd in ((mine, parity), (other, 1 - parity)):
                        piece = packed(u_ref[...], (2 * chip + odd) * columns + row * shift, columns)
                        spare = jnp.zeros((piece.shape[0], lanes - piece.shape[1]), F32)
                        out[chip] = jnp.concatenate([piece, spare], 1)


def final_kernel(arrived, mask, out):
    total = arrived[0]
    for chip in range(1, arrived.shape[0]):
        total = total + arrived[chip]
    cells, width, parts, columns = out.shape
    value = unpacked(total, columns)
    for f in range(cells):
        for part in range(parts):
            for j in range(width):
                row = (f * parts + part) * width + j
                out[f, j, pl.ds(part, 1), :] = value[row : row + 1] * mask[pl.ds(f, 1), :]


def call(kernel, name, shapes, specs, scratch=(), mib=16, flops=0):
    return pl.pallas_call(
        kernel,
        out_shape=shapes,
        in_specs=[pl.BlockSpec(memory_space=space) for space in specs],
        out_specs=jax.tree.map(lambda _: pl.BlockSpec(memory_space=pltpu.VMEM), shapes),
        scratch_shapes=scratch,
        compiler_params=pltpu.CompilerParams(vmem_limit_bytes=mib * 2**20),
        cost_estimate=pl.CostEstimate(flops=flops, bytes_accessed=2**20, transcendentals=0),
        name=name,
    )


def shards(coefficients, class_weight, diff_class, frag_cells, block_pattern):
    own = coefficients[0]
    _, occupied, functions = own.shape
    yh, z, core = (lax.axis_index(name) for name in KA)
    band = lax.axis_index("yl") * PARTS[4] + lax.axis_index("x")
    width = occupied // (PARTS[3] * PARTS[4])
    group = 2 * width
    kpoint_count = PARTS[0] * PARTS[1] * PARTS[2]
    cells = frag_cells.shape[0]
    up = [(i, (i + 1) % PARTS[1]) for i in range(PARTS[1])]
    down = [(j, i) for i, j in up]
    swap = [(0, 1), (1, 0)]
    right = [(i, (i + 1) % PARTS[4]) for i in range(PARTS[4])]
    left = [(j, i) for i, j in right]
    vmem, smem = pltpu.VMEM, pltpu.SMEM

    odd = jnp.bitwise_and(lax.axis_index("x"), 1)
    far_a = lax.ppermute(lax.dynamic_index_in_dim(own, odd, 0, keepdims=False), "yh", swap)
    block = lax.dynamic_slice_in_dim(own, band * width, width, 1).reshape(group, functions)
    blocks = [block]
    offsets = [0, -1, 1, -2, 2, -3, 3, -4]
    from_below = from_above = block
    for step in range(1, PARTS[1] // 2):
        from_below = lax.ppermute(from_below, "z", up)
        from_above = lax.ppermute(from_above, "z", down)
        blocks += [from_below, from_above]
        if step == 3:
            held = (from_below, from_above, far_a)
            from_below, from_above, far_a = lax.optimization_barrier(held)
    mid = occupied // 2
    from_left = lax.ppermute(far_a[:mid], "x", right)
    from_right = lax.ppermute(far_a[mid:], "x", left)
    far_b = jnp.concatenate([from_left, from_right], 0)
    cut = 24
    blocks.append(lax.ppermute(from_below[:cut], "z", up))
    blocks.append(lax.ppermute(from_above[cut:], "z", down))
    split = 5
    first = jnp.concatenate(blocks[:split], 0)
    first_near = lax.ppermute(first, "core", swap)
    last = jnp.concatenate(blocks[split:], 0)
    last_near = lax.ppermute(last, "core", swap)

    k_points = []
    for these in (offsets[:split], offsets[split:]):
        k_points += [(offset, False) for offset in these] + [(offset, True) for offset in these]
    early, late = 2 * split * group, 2 * (len(offsets) - split) * group
    angles = 2.0 * np.pi * np.arange(kpoint_count) / kpoint_count
    tables = [jnp.asarray((f(angles) / kpoint_count).astype(np.float32)) for f in (np.cos, np.sin)]
    ids = jnp.stack([yh, z, core, odd]).astype(jnp.int32)
    later_ids, _ = lax.optimization_barrier((ids, last))
    weights, g_first, g_last = call(
        functools.partial(prep_kernel, width, functions, k_points),
        "phases",
        (
            jax.ShapeDtypeStruct((2, early + late, 1), F32),
            jax.ShapeDtypeStruct((8 * width, early), BF16),
            jax.ShapeDtypeStruct((8 * width, late), BF16),
        ),
        [smem] * 6,
    )(later_ids, frag_cells, diff_class, class_weight, *tables)

    one = jax.ShapeDtypeStruct((4 * width, occupied), F32)
    scratch = [pltpu.VMEM((early, functions), BF16)]
    b_first = (first, first_near, weights, g_first)
    kernel = functools.partial(own_kernel, width)
    t_own = call(kernel, "own_first", one, [vmem] * 5, scratch, flops=10**9)(own, *b_first)
    kernel = functools.partial(far_kernel, width)
    t_far = call(kernel, "far_first", one, [smem] + [vmem] * 6, scratch, flops=10**9)(ids, far_a, far_b, *b_first)
    t = call(
        functools.partial(last_kernel, width),
        "last_terms",
        jax.ShapeDtypeStruct((2,) + one.shape, F32),
        [smem] + [vmem] * 9,
        [pltpu.VMEM((late, functions), BF16)],
        flops=10**9,
    )(ids, own, far_a, far_b, last, last_near, weights, g_last, t_own, t_far)

    t_yh = lax.ppermute(t, "yh", swap)
    chips = PARTS[1]
    columns = functions // kpoint_count
    span = 2 * chips * columns
    piece = jax.ShapeDtypeStruct((chips, 4 * width * 3 // 5, 128), F32)
    mine, other = call(
        functools.partial(cluster_kernel, width, columns),
        "cluster_terms",
        (piece, piece),
        [smem] + [vmem] * 5,
        [pltpu.VMEM((4 * width, span + span % 128), F32)],
        flops=10**9,
    )(ids, own, far_a, far_b, t, t_yh)
    pieces = mine + lax.ppermute(other, "core", swap)

    arrived = lax.all_to_all(pieces, "z", 0, 0, tiled=True)
    index = (yh * PARTS[1] + z) * 2 + core
    block_size = functions // block_pattern.shape[1]
    local_ids = (index * columns + jnp.arange(columns, dtype=jnp.int32)) // block_size
    block_ids = jnp.arange(block_pattern.shape[1], dtype=jnp.int32)
    onehot = (block_ids[:, None] == local_ids[None, :]).astype(F32)
    mask = jnp.dot(block_pattern.astype(F32), onehot, precision=lax.Precision.HIGHEST)
    cluster = call(
        final_kernel,
        "sum_and_mask",
        jax.ShapeDtypeStruct((cells, width, 2, columns), F32),
        [vmem] * 2,
        mib=4,
    )(arrived, mask)
    return jnp.transpose(cluster, (0, 2, 1, 3))


def solution(mesh):
    placed = (P(KA, None, None, None), P(), P(), P(), P())
    return jax.shard_map(
        shards,
        mesh=Mesh(mesh.devices.reshape(PARTS), AXES),
        in_specs=placed,
        out_specs=P(None, None, BAND, KA),
        check_vma=False,
    )
```

```python
import functools

import jax
import jax.numpy as jnp
import numpy as np
from jax import lax
from jax.experimental import pallas as pl
from jax.experimental.pallas import tpu as pltpu
from jax.sharding import Mesh
from jax.sharding import PartitionSpec as P

AXES = ("yh", "z", "core", "yl", "x")
KA = ("yh", "z", "core")
BAND = ("yl", "x")
PARTS = (2, 8, 2, 2, 4)
F32 = jnp.float32
BF16 = jnp.bfloat16


def prep_kernel(width, functions, k_points, ids, cells, diff_class, class_weight, cos_table, sin_table, w_ref, g0, g1):
    yh, z, core = ids[0], ids[1], ids[2]
    group = 2 * width
    count = len(k_points)
    rows, lanes = 4 * width, group * count
    points = []
    for offset, flip in k_points:
        points.append((yh * PARTS[1] + lax.rem(z + offset + PARTS[1], PARTS[1])) * 2 + (1 - core if flip else core))
    for q, row in enumerate((yh, 1 - yh)):
        q_point = (row * PARTS[1] + z) * 2 + core
        for at, point in enumerate(points):
            weight = jnp.full((group, 1), class_weight[diff_class[point, q_point]], F32)
            w_ref[q, pl.ds(at * group, group), :] = weight / functions
    lane = lax.broadcasted_iota(jnp.int32, (1, lanes), 1)
    tables = []
    for f in range(2):
        cosines = jnp.zeros((1, lanes), F32)
        sines = jnp.zeros((1, lanes), F32)
        for at, point in enumerate(points):
            here = (lane >= at * group) & (lane < (at + 1) * group)
            index = lax.rem(point * cells[f], cos_table.shape[0])
            cosines = jnp.where(here, cos_table[index], cosines)
            sines = jnp.where(here, sin_table[index], sines)
        tables.append((cosines, sines))
    row = lax.broadcasted_iota(jnp.int32, (rows, lanes), 0)
    col = lax.broadcasted_iota(jnp.int32, (rows, lanes), 1)
    first = row < group
    cosines = jnp.where(first, tables[0][0], tables[1][0])
    sines = jnp.where(first, tables[0][1], tables[1][1])
    real, real_m = row % group < width, col % group < width
    value = jnp.where(real == real_m, cosines, jnp.where(real, -sines, sines))
    value = jnp.where(row % width == col % width, value, 0.0)
    high = value.astype(BF16)
    low = (value - high.astype(F32)).astype(BF16)
    both = jnp.concatenate([high, low], 0)
    g0[...] = both[:, : g0.shape[1]]
    g1[...] = both[:, g0.shape[1] :]


def turned(value, width, sign):
    rows = value.shape[0]
    real = lax.broadcasted_iota(jnp.int32, value.shape, 0) % (2 * width) < width
    up, down = pltpu.roll(value, rows - width, 0), pltpu.roll(value, width, 0)
    return jnp.where(real, up, -down) if sign > 0 else jnp.where(real, -up, down)


def part_of_t(b, real, imag, w, g, width):
    contract = (((1,), (1,)), ((), ()))
    m = lax.dot_general(b, real[...], contract, preferred_element_type=F32)
    m = m + turned(lax.dot_general(b, imag[...], contract, preferred_element_type=F32), width, 1)
    t = jnp.dot(g, (w * m).astype(BF16), preferred_element_type=F32)
    half = t.shape[0] // 2
    return t[:half] + t[half:]


def either_way(odd, far_a, far_b, run):
    @pl.when(odd == 0)
    def _():
        run(far_a, far_b)

    @pl.when(odd != 0)
    def _():
        run(far_b, far_a)


def gathered(b_ref, b0, b1):
    half = b0.shape[0]
    b_ref[:half, :] = b0[...]
    b_ref[half:, :] = b1[...]
    return b_ref[...]


def own_kernel(width, own, b0, b1, w, g, t_ref, b_ref):
    b = gathered(b_ref, b0, b1)
    t_ref[...] = part_of_t(b, own.at[0], own.at[1], w[0, : b.shape[0], :], g[...], width)


def far_kernel(width, ids, far_a, far_b, b0, b1, w, g, t_ref, b_ref):
    b = gathered(b_ref, b0, b1)

    def run(real, imag):
        t_ref[...] = part_of_t(b, real, imag, w[1, : b.shape[0], :], g[...], width)

    either_way(ids[3], far_a, far_b, run)


def last_kernel(width, ids, own, far_a, far_b, b0, b1, w, g, t_own, t_far, t_ref, b_ref):
    b = gathered(b_ref, b0, b1)
    start = w.shape[1] - b.shape[0]

    def run(real, imag):
        t_ref[0] = t_own[...] + part_of_t(b, own.at[0], own.at[1], w[0, start:, :], g[...], width)
        t_ref[1] = t_far[...] + part_of_t(b, real, imag, w[1, start:, :], g[...], width)

    either_way(ids[3], far_a, far_b, run)


def packed(u, at, columns):
    third = columns // 3
    tall = jnp.concatenate([u[:, at + p * third : at + (p + 1) * third] for p in range(3)], 0)
    rows = tall.shape[0] // 5
    return jnp.concatenate([tall[g * rows : (g + 1) * rows] for g in range(5)], 1)


def unpacked(value, columns):
    third = columns // 3
    tall = jnp.concatenate([value[:, g * third : (g + 1) * third] for g in range(5)], 0)
    rows = tall.shape[0] // 3
    return jnp.concatenate([tall[p * rows : (p + 1) * rows] for p in range(3)], 1)


def cluster_kernel(
    width, columns, ids, own, near, far_a, far_b, diag_a, diag_b, t, t_yh, t_core, t_diag, out, u_ref
):
    yh, core, odd = ids[0], ids[2], ids[3]
    chips, _, lanes = out.shape
    span = 2 * chips * columns
    shift = span % 128
    window = pl.ds(pl.multiple_of(yh * (span - shift), 128), span + shift)
    half = 4 * width
    swap = jnp.full(t.shape[1:], odd) > 0
    total = None
    for value, first, second, swapped in (
        (t[0] + t_yh[1], own.at[0], own.at[1], False),
        (t_core[0] + t_diag[1], near.at[0], near.at[1], False),
        (t[1] + t_yh[0], far_a, far_b, True),
        (t_core[1] + t_diag[0], diag_a, diag_b, True),
    ):
        partner = turned(value, width, -1)
        if swapped:
            value, partner = jnp.where(swap, partner, value), jnp.where(swap, value, partner)
        for factor, data in ((value, first), (partner, second)):
            high = factor.astype(BF16)
            low = (factor - high.astype(F32)).astype(BF16)
            u = jnp.dot(jnp.concatenate([high, low], 0), data[:, window], preferred_element_type=F32)
            total = u if total is None else total + u
    u_ref[...] = total[:half] + total[half:]
    for row in range(2):
        for parity in range(2):

            @pl.when((yh == row) & (core == parity))
            def _():
                for chip in range(chips):
                    piece = packed(u_ref[...], (2 * chip + parity) * columns + row * shift, columns)
                    spare = jnp.zeros((piece.shape[0], lanes - piece.shape[1]), F32)
                    out[chip] = jnp.concatenate([piece, spare], 1)


def final_kernel(arrived, mask, out):
    total = arrived[0]
    for chip in range(1, arrived.shape[0]):
        total = total + arrived[chip]
    cells, width, parts, columns = out.shape
    value = unpacked(total, columns)
    for f in range(cells):
        for part in range(parts):
            for j in range(width):
                row = (f * parts + part) * width + j
                out[f, j, pl.ds(part, 1), :] = value[row : row + 1] * mask[pl.ds(f, 1), :]


def call(kernel, name, shapes, specs, scratch=(), mib=16, flops=0):
    return pl.pallas_call(
        kernel,
        out_shape=shapes,
        in_specs=[pl.BlockSpec(memory_space=space) for space in specs],
        out_specs=jax.tree.map(lambda _: pl.BlockSpec(memory_space=pltpu.VMEM), shapes),
        scratch_shapes=scratch,
        compiler_params=pltpu.CompilerParams(vmem_limit_bytes=mib * 2**20),
        cost_estimate=pl.CostEstimate(flops=flops, bytes_accessed=2**20, transcendentals=0),
        name=name,
    )


def shards(coefficients, class_weight, diff_class, frag_cells, block_pattern):
    own = coefficients[0]
    _, occupied, functions = own.shape
    yh, z, core = (lax.axis_index(name) for name in KA)
    band = lax.axis_index("yl") * PARTS[4] + lax.axis_index("x")
    width = occupied // (PARTS[3] * PARTS[4])
    group = 2 * width
    kpoint_count = PARTS[0] * PARTS[1] * PARTS[2]
    cells = frag_cells.shape[0]
    up = [(i, (i + 1) % PARTS[1]) for i in range(PARTS[1])]
    down = [(j, i) for i, j in up]
    swap = [(0, 1), (1, 0)]
    right = [(i, (i + 1) % PARTS[4]) for i in range(PARTS[4])]
    left = [(j, i) for i, j in right]
    vmem, smem = pltpu.VMEM, pltpu.SMEM

    odd = jnp.bitwise_and(lax.axis_index("x"), 1)
    far_a = lax.ppermute(lax.dynamic_index_in_dim(own, odd, 0, keepdims=False), "yh", swap)
    near = lax.ppermute(own, "core", swap)
    block = lax.dynamic_slice_in_dim(own, band * width, width, 1).reshape(group, functions)
    blocks = [block]
    offsets = [0, -1, 1, -2, 2, -3, 3, -4]
    from_below = from_above = block
    for step in range(1, PARTS[1] // 2):
        from_below = lax.ppermute(from_below, "z", up)
        from_above = lax.ppermute(from_above, "z", down)
        if step == 2:
            from_below, from_above, near = lax.optimization_barrier((from_below, from_above, near))
        if step == 3:
            from_below, from_above, far_a = lax.optimization_barrier((from_below, from_above, far_a))
        blocks += [from_below, from_above]
    mid = occupied // 2
    from_left = lax.ppermute(far_a[:mid], "x", right)
    from_right = lax.ppermute(far_a[mid:], "x", left)
    split = 5
    first = jnp.concatenate(blocks[:split], 0)
    first_near = lax.ppermute(first, "core", swap)

    k_points = []
    for these in (offsets[:split], offsets[split:]):
        k_points += [(offset, False) for offset in these] + [(offset, True) for offset in these]
    early, late = 2 * split * group, 2 * (len(offsets) - split) * group
    angles = 2.0 * np.pi * np.arange(kpoint_count) / kpoint_count
    tables = [jnp.asarray((f(angles) / kpoint_count).astype(np.float32)) for f in (np.cos, np.sin)]
    ids = jnp.stack([yh, z, core, odd]).astype(jnp.int32)
    later_ids, _ = lax.optimization_barrier((ids, first))
    weights, g_first, g_last = call(
        functools.partial(prep_kernel, width, functions, k_points),
        "phases",
        (
            jax.ShapeDtypeStruct((2, early + late, 1), F32),
            jax.ShapeDtypeStruct((8 * width, early), BF16),
            jax.ShapeDtypeStruct((8 * width, late), BF16),
        ),
        [smem] * 6,
    )(later_ids, frag_cells, diff_class, class_weight, *tables)

    one = jax.ShapeDtypeStruct((4 * width, occupied), F32)
    scratch = [pltpu.VMEM((early, functions), BF16)]
    b_first = (first, first_near, weights, g_first)
    kernel = functools.partial(own_kernel, width)
    t_own = call(kernel, "own_first", one, [vmem] * 5, scratch, flops=10**9)(own, *b_first)
    from_below, from_above, t_own = lax.optimization_barrier((from_below, from_above, t_own))
    cut = 24
    blocks.append(lax.ppermute(from_below[:cut], "z", up))
    blocks.append(lax.ppermute(from_above[cut:], "z", down))
    last = jnp.concatenate(blocks[split:], 0)
    last_near = lax.ppermute(last, "core", swap)
    from_left, from_right, _ = lax.optimization_barrier((from_left, from_right, last))
    far_b = jnp.concatenate([from_left, from_right], 0)
    later_a, _ = lax.optimization_barrier((far_a, far_b))
    diag_a, diag_b = (lax.ppermute(half, "core", swap) for half in (later_a, far_b))
    kernel = functools.partial(far_kernel, width)
    t_far = call(kernel, "far_first", one, [smem] + [vmem] * 6, scratch, flops=10**9)(ids, far_a, far_b, *b_first)
    t = call(
        functools.partial(last_kernel, width),
        "last_terms",
        jax.ShapeDtypeStruct((2,) + one.shape, F32),
        [smem] + [vmem] * 9,
        [pltpu.VMEM((late, functions), BF16)],
        flops=10**9,
    )(ids, own, far_a, far_b, last, last_near, weights, g_last, t_own, t_far)

    t_yh = lax.ppermute(t, "yh", swap)
    t_core = lax.ppermute(t, "core", swap)
    t_diag = lax.ppermute(t_yh, "core", swap)
    chips = PARTS[1]
    columns = functions // kpoint_count
    span = 2 * chips * columns
    pieces = call(
        functools.partial(cluster_kernel, width, columns),
        "cluster_terms",
        jax.ShapeDtypeStruct((chips, 4 * width * 3 // 5, 128), F32),
        [smem] + [vmem] * 10,
        [pltpu.VMEM((4 * width, span + span % 128), F32)],
        flops=10**9,
    )(ids, own, near, far_a, far_b, diag_a, diag_b, t, t_yh, t_core, t_diag)

    arrived = lax.all_to_all(pieces, "z", 0, 0, tiled=True)
    index = (yh * PARTS[1] + z) * 2 + core
    block_size = functions // block_pattern.shape[1]
    local_ids = (index * columns + jnp.arange(columns, dtype=jnp.int32)) // block_size
    block_ids = jnp.arange(block_pattern.shape[1], dtype=jnp.int32)
    onehot = (block_ids[:, None] == local_ids[None, :]).astype(F32)
    mask = jnp.dot(block_pattern.astype(F32), onehot, precision=lax.Precision.HIGHEST)
    cluster = call(
        final_kernel,
        "sum_and_mask",
        jax.ShapeDtypeStruct((cells, width, 2, columns), F32),
        [vmem] * 2,
        mib=4,
    )(arrived, mask)
    return jnp.transpose(cluster, (0, 2, 1, 3))


def solution(mesh):
    placed = (P(KA, None, None, None), P(), P(), P(), P())
    return jax.shard_map(
        shards,
        mesh=Mesh(mesh.devices.reshape(PARTS), AXES),
        in_specs=placed,
        out_specs=P(None, None, BAND, KA),
        check_vma=False,
    )
```

```python
import functools

import jax
import jax.numpy as jnp
import numpy as np
from jax import lax
from jax.experimental import pallas as pl
from jax.experimental.pallas import tpu as pltpu
from jax.sharding import Mesh
from jax.sharding import PartitionSpec as P

AXES = ("yh", "z", "core", "yl", "x")
KA = ("yh", "z", "core")
BAND = ("yl", "x")
PARTS = (2, 8, 2, 2, 4)
F32 = jnp.float32
BF16 = jnp.bfloat16


def prep_kernel(width, functions, k_points, cells, diff_class, class_weight, cos_table, sin_table, w_ref, g0, g1):
    yh, z, core = (lax.axis_index(name) for name in KA)
    group = 2 * width
    count = len(k_points)
    rows, lanes = 4 * width, group * count
    points = []
    for offset, flip in k_points:
        points.append((yh * PARTS[1] + lax.rem(z + offset + PARTS[1], PARTS[1])) * 2 + (1 - core if flip else core))
    for q, row in enumerate((yh, 1 - yh)):
        q_point = (row * PARTS[1] + z) * 2 + core
        for at, point in enumerate(points):
            weight = jnp.full((group, 1), class_weight[diff_class[point, q_point]], F32)
            w_ref[q, pl.ds(at * group, group), :] = weight / functions
    lane = lax.broadcasted_iota(jnp.int32, (1, lanes), 1)
    tables = []
    for f in range(2):
        cosines = jnp.zeros((1, lanes), F32)
        sines = jnp.zeros((1, lanes), F32)
        for at, point in enumerate(points):
            here = (lane >= at * group) & (lane < (at + 1) * group)
            index = lax.rem(point * cells[f], cos_table.shape[0])
            cosines = jnp.where(here, cos_table[index], cosines)
            sines = jnp.where(here, sin_table[index], sines)
        tables.append((cosines, sines))
    row = lax.broadcasted_iota(jnp.int32, (rows, lanes), 0)
    col = lax.broadcasted_iota(jnp.int32, (rows, lanes), 1)
    first = row < group
    cosines = jnp.where(first, tables[0][0], tables[1][0])
    sines = jnp.where(first, tables[0][1], tables[1][1])
    real, real_m = row % group < width, col % group < width
    value = jnp.where(real == real_m, cosines, jnp.where(real, -sines, sines))
    value = jnp.where(row % width == col % width, value, 0.0)
    high = value.astype(BF16)
    low = (value - high.astype(F32)).astype(BF16)
    both = jnp.concatenate([high, low], 0)
    g0[...] = both[:, : g0.shape[1]]
    g1[...] = both[:, g0.shape[1] :]


def turned(value, width, sign):
    rows = value.shape[0]
    real = lax.broadcasted_iota(jnp.int32, value.shape, 0) % (2 * width) < width
    up, down = pltpu.roll(value, rows - width, 0), pltpu.roll(value, width, 0)
    return jnp.where(real, up, -down) if sign > 0 else jnp.where(real, -up, down)


def part_of_t(b, real, imag, w, g, width):
    contract = (((1,), (1,)), ((), ()))
    m = lax.dot_general(b, real[...], contract, preferred_element_type=F32)
    m = m + turned(lax.dot_general(b, imag[...], contract, preferred_element_type=F32), width, 1)
    t = jnp.dot(g, (w * m).astype(BF16), preferred_element_type=F32)
    half = t.shape[0] // 2
    return t[:half] + t[half:]


def odd_x():
    return jnp.bitwise_and(lax.axis_index("x"), 1)


def either_way(far_a, far_b, run):
    odd = odd_x()

    @pl.when(odd == 0)
    def _():
        run(far_a, far_b)

    @pl.when(odd != 0)
    def _():
        run(far_b, far_a)


def gathered(b_ref, b0, b1):
    half = b0.shape[0]
    b_ref[:half, :] = b0[...]
    b_ref[half:, :] = b1[...]
    return b_ref[...]


def own_kernel(width, own, b0, b1, w, g, t_ref, b_ref):
    b = gathered(b_ref, b0, b1)
    t_ref[...] = part_of_t(b, own.at[0], own.at[1], w[0, : b.shape[0], :], g[...], width)


def far_kernel(width, far_a, far_b, b0, b1, w, g, t_ref, b_ref):
    b = gathered(b_ref, b0, b1)

    def run(real, imag):
        t_ref[...] = part_of_t(b, real, imag, w[1, : b.shape[0], :], g[...], width)

    either_way(far_a, far_b, run)


def last_kernel(width, own, far_a, far_b, b0, b1, w, g, t_own, t_far, t_ref, b_ref):
    b = gathered(b_ref, b0, b1)
    start = w.shape[1] - b.shape[0]

    def run(real, imag):
        t_ref[0] = t_own[...] + part_of_t(b, own.at[0], own.at[1], w[0, start:, :], g[...], width)
        t_ref[1] = t_far[...] + part_of_t(b, real, imag, w[1, start:, :], g[...], width)

    either_way(far_a, far_b, run)


def packed(u, at, columns):
    third = columns // 3
    tall = jnp.concatenate([u[:, at + p * third : at + (p + 1) * third] for p in range(3)], 0)
    rows = tall.shape[0] // 5
    return jnp.concatenate([tall[g * rows : (g + 1) * rows] for g in range(5)], 1)


def unpacked(value, columns):
    third = columns // 3
    tall = jnp.concatenate([value[:, g * third : (g + 1) * third] for g in range(5)], 0)
    rows = tall.shape[0] // 3
    return jnp.concatenate([tall[p * rows : (p + 1) * rows] for p in range(3)], 1)


def cluster_kernel(
    width, columns, own, near, far_a, far_b, diag_a, diag_b, t, t_yh, t_core, t_diag, out, u_ref
):
    yh, core, odd = lax.axis_index("yh"), lax.axis_index("core"), odd_x()
    chips, _, lanes = out.shape
    span = 2 * chips * columns
    shift = span % 128
    window = pl.ds(pl.multiple_of(yh * (span - shift), 128), span + shift)
    half = 4 * width
    swap = jnp.full(t.shape[1:], odd) > 0
    total = None
    for value, first, second, swapped in (
        (t[0] + t_yh[1], own.at[0], own.at[1], False),
        (t_core[0] + t_diag[1], near.at[0], near.at[1], False),
        (t[1] + t_yh[0], far_a, far_b, True),
        (t_core[1] + t_diag[0], diag_a, diag_b, True),
    ):
        partner = turned(value, width, -1)
        if swapped:
            value, partner = jnp.where(swap, partner, value), jnp.where(swap, value, partner)
        for factor, data in ((value, first), (partner, second)):
            high = factor.astype(BF16)
            low = (factor - high.astype(F32)).astype(BF16)
            u = jnp.dot(jnp.concatenate([high, low], 0), data[:, window], preferred_element_type=F32)
            total = u if total is None else total + u
    u_ref[...] = total[:half] + total[half:]
    for row in range(2):
        for parity in range(2):

            @pl.when((yh == row) & (core == parity))
            def _():
                for chip in range(chips):
                    piece = packed(u_ref[...], (2 * chip + parity) * columns + row * shift, columns)
                    spare = jnp.zeros((piece.shape[0], lanes - piece.shape[1]), F32)
                    out[chip] = jnp.concatenate([piece, spare], 1)


def final_kernel(arrived, mask, out):
    total = arrived[0]
    for chip in range(1, arrived.shape[0]):
        total = total + arrived[chip]
    cells, width, parts, columns = out.shape
    value = unpacked(total, columns)
    for f in range(cells):
        for part in range(parts):
            for j in range(width):
                row = (f * parts + part) * width + j
                out[f, j, pl.ds(part, 1), :] = value[row : row + 1] * mask[pl.ds(f, 1), :]


def call(kernel, name, shapes, specs, scratch=(), mib=16, flops=0):
    return pl.pallas_call(
        kernel,
        out_shape=shapes,
        in_specs=[pl.BlockSpec(memory_space=space) for space in specs],
        out_specs=jax.tree.map(lambda _: pl.BlockSpec(memory_space=pltpu.VMEM), shapes),
        scratch_shapes=scratch,
        compiler_params=pltpu.CompilerParams(vmem_limit_bytes=mib * 2**20),
        cost_estimate=pl.CostEstimate(flops=flops, bytes_accessed=2**20, transcendentals=0),
        name=name,
    )


def shards(coefficients, class_weight, diff_class, frag_cells, block_pattern):
    own = coefficients[0]
    _, occupied, functions = own.shape
    yh, z, core = (lax.axis_index(name) for name in KA)
    band = lax.axis_index("yl") * PARTS[4] + lax.axis_index("x")
    width = occupied // (PARTS[3] * PARTS[4])
    group = 2 * width
    kpoint_count = PARTS[0] * PARTS[1] * PARTS[2]
    cells = frag_cells.shape[0]
    up = [(i, (i + 1) % PARTS[1]) for i in range(PARTS[1])]
    down = [(j, i) for i, j in up]
    swap = [(0, 1), (1, 0)]
    right = [(i, (i + 1) % PARTS[4]) for i in range(PARTS[4])]
    left = [(j, i) for i, j in right]
    vmem, smem = pltpu.VMEM, pltpu.SMEM

    far_a = lax.ppermute(lax.dynamic_index_in_dim(own, odd_x(), 0, keepdims=False), "yh", swap)
    near = lax.ppermute(own, "core", swap)
    block = lax.dynamic_slice_in_dim(own, band * width, width, 1).reshape(group, functions)
    blocks = [block]
    offsets = [0, -1, 1, -2, 2, -3, 3, -4]
    from_below = from_above = block
    for step in range(1, PARTS[1] // 2):
        from_below = lax.ppermute(from_below, "z", up)
        from_above = lax.ppermute(from_above, "z", down)
        if step == 2:
            from_below, from_above, near = lax.optimization_barrier((from_below, from_above, near))
        if step == 3:
            from_below, from_above, far_a = lax.optimization_barrier((from_below, from_above, far_a))
        blocks += [from_below, from_above]
    mid = occupied // 2
    from_left = lax.ppermute(far_a[:mid], "x", right)
    from_right = lax.ppermute(far_a[mid:], "x", left)
    split = 5
    first = jnp.concatenate(blocks[:split], 0)
    first_near = lax.ppermute(first, "core", swap)

    k_points = []
    for these in (offsets[:split], offsets[split:]):
        k_points += [(offset, False) for offset in these] + [(offset, True) for offset in these]
    early, late = 2 * split * group, 2 * (len(offsets) - split) * group
    angles = 2.0 * np.pi * np.arange(kpoint_count) / kpoint_count
    tables = [jnp.asarray((f(angles) / kpoint_count).astype(np.float32)) for f in (np.cos, np.sin)]
    later_cells, _ = lax.optimization_barrier((frag_cells, first))
    weights, g_first, g_last = call(
        functools.partial(prep_kernel, width, functions, k_points),
        "phases",
        (
            jax.ShapeDtypeStruct((2, early + late, 1), F32),
            jax.ShapeDtypeStruct((8 * width, early), BF16),
            jax.ShapeDtypeStruct((8 * width, late), BF16),
        ),
        [smem] * 5,
    )(later_cells, diff_class, class_weight, *tables)

    one = jax.ShapeDtypeStruct((4 * width, occupied), F32)
    scratch = [pltpu.VMEM((early, functions), BF16)]
    b_first = (first, first_near, weights, g_first)
    kernel = functools.partial(own_kernel, width)
    t_own = call(kernel, "own_first", one, [vmem] * 5, scratch, flops=10**9)(own, *b_first)
    cut = 24
    blocks.append(lax.ppermute(from_below[:cut], "z", up))
    blocks.append(lax.ppermute(from_above[cut:], "z", down))
    held = (blocks[-2], blocks[-1], from_left, from_right, t_own)
    blocks[-2], blocks[-1], from_left, from_right, t_own = lax.optimization_barrier(held)
    last = jnp.concatenate(blocks[split:], 0)
    far_b = jnp.concatenate([from_left, from_right], 0)
    last, far_b = lax.optimization_barrier((last, far_b))
    last_near = lax.ppermute(last, "core", swap)
    later_a, _ = lax.optimization_barrier((far_a, far_b))
    diag_a, diag_b = (lax.ppermute(half, "core", swap) for half in (later_a, far_b))
    kernel = functools.partial(far_kernel, width)
    t_far = call(kernel, "far_first", one, [vmem] * 6, scratch, flops=10**9)(far_a, far_b, *b_first)
    t = call(
        functools.partial(last_kernel, width),
        "last_terms",
        jax.ShapeDtypeStruct((2,) + one.shape, F32),
        [vmem] * 9,
        [pltpu.VMEM((late, functions), BF16)],
        flops=10**9,
    )(own, far_a, far_b, last, last_near, weights, g_last, t_own, t_far)

    t_yh = lax.ppermute(t, "yh", swap)
    t_core = lax.ppermute(t, "core", swap)
    t_diag = lax.ppermute(t_yh, "core", swap)
    chips = PARTS[1]
    columns = functions // kpoint_count
    span = 2 * chips * columns
    pieces = call(
        functools.partial(cluster_kernel, width, columns),
        "cluster_terms",
        jax.ShapeDtypeStruct((chips, 4 * width * 3 // 5, 128), F32),
        [vmem] * 10,
        [pltpu.VMEM((4 * width, span + span % 128), F32)],
        flops=10**9,
    )(own, near, far_a, far_b, diag_a, diag_b, t, t_yh, t_core, t_diag)

    arrived = lax.all_to_all(pieces, "z", 0, 0, tiled=True)
    index = (yh * PARTS[1] + z) * 2 + core
    block_size = functions // block_pattern.shape[1]
    local_ids = (index * columns + jnp.arange(columns, dtype=jnp.int32)) // block_size
    block_ids = jnp.arange(block_pattern.shape[1], dtype=jnp.int32)
    onehot = (block_ids[:, None] == local_ids[None, :]).astype(F32)
    mask = jnp.dot(block_pattern.astype(F32), onehot, precision=lax.Precision.HIGHEST)
    cluster = call(
        final_kernel,
        "sum_and_mask",
        jax.ShapeDtypeStruct((cells, width, 2, columns), F32),
        [vmem] * 2,
        mib=4,
    )(arrived, mask)
    return jnp.transpose(cluster, (0, 2, 1, 3))


def solution(mesh):
    placed = (P(KA, None, None, None), P(), P(), P(), P())
    return jax.shard_map(
        shards,
        mesh=Mesh(mesh.devices.reshape(PARTS), AXES),
        in_specs=placed,
        out_specs=P(None, None, BAND, KA),
        check_vma=False,
    )
```

```python
import functools

import jax
import jax.numpy as jnp
import numpy as np
from jax import lax
from jax.experimental import pallas as pl
from jax.experimental.pallas import tpu as pltpu
from jax.sharding import Mesh
from jax.sharding import PartitionSpec as P

AXES = ("yh", "z", "core", "yl", "x")
KA = ("yh", "z", "core")
BAND = ("yl", "x")
PARTS = (2, 8, 2, 2, 4)
F32 = jnp.float32
BF16 = jnp.bfloat16


def prep_kernel(width, functions, k_points, cells, diff_class, class_weight, cos_table, sin_table, w_ref, g0, g1):
    yh, z, core = (lax.axis_index(name) for name in KA)
    group = 2 * width
    count = len(k_points)
    rows, lanes = 4 * width, group * count
    points = []
    for offset, flip in k_points:
        points.append((yh * PARTS[1] + lax.rem(z + offset + PARTS[1], PARTS[1])) * 2 + (1 - core if flip else core))
    for q, row in enumerate((yh, 1 - yh)):
        q_point = (row * PARTS[1] + z) * 2 + core
        for at, point in enumerate(points):
            weight = jnp.full((group, 1), class_weight[diff_class[point, q_point]], F32)
            w_ref[q, pl.ds(at * group, group), :] = weight / functions
    lane = lax.broadcasted_iota(jnp.int32, (1, lanes), 1)
    tables = []
    for f in range(2):
        cosines = jnp.zeros((1, lanes), F32)
        sines = jnp.zeros((1, lanes), F32)
        for at, point in enumerate(points):
            here = (lane >= at * group) & (lane < (at + 1) * group)
            index = lax.rem(point * cells[f], cos_table.shape[0])
            cosines = jnp.where(here, cos_table[index], cosines)
            sines = jnp.where(here, sin_table[index], sines)
        tables.append((cosines, sines))
    row = lax.broadcasted_iota(jnp.int32, (rows, lanes), 0)
    col = lax.broadcasted_iota(jnp.int32, (rows, lanes), 1)
    first = row < group
    cosines = jnp.where(first, tables[0][0], tables[1][0])
    sines = jnp.where(first, tables[0][1], tables[1][1])
    real, real_m = row % group < width, col % group < width
    value = jnp.where(real == real_m, cosines, jnp.where(real, -sines, sines))
    value = jnp.where(row % width == col % width, value, 0.0)
    high = value.astype(BF16)
    low = (value - high.astype(F32)).astype(BF16)
    both = jnp.concatenate([high, low], 0)
    g0[...] = both[:, : g0.shape[1]]
    g1[...] = both[:, g0.shape[1] :]


def turned(value, width, sign):
    rows = value.shape[0]
    real = lax.broadcasted_iota(jnp.int32, value.shape, 0) % (2 * width) < width
    up, down = pltpu.roll(value, rows - width, 0), pltpu.roll(value, width, 0)
    return jnp.where(real, up, -down) if sign > 0 else jnp.where(real, -up, down)


def part_of_t(b, real, imag, w, g, width):
    contract = (((1,), (1,)), ((), ()))
    m = lax.dot_general(b, real[...], contract, preferred_element_type=F32)
    m = m + turned(lax.dot_general(b, imag[...], contract, preferred_element_type=F32), width, 1)
    t = jnp.dot(g, (w * m).astype(BF16), preferred_element_type=F32)
    half = t.shape[0] // 2
    return t[:half] + t[half:]


def odd_x():
    return jnp.bitwise_and(lax.axis_index("x"), 1)


def either_way(far_a, far_b, run):
    odd = odd_x()

    @pl.when(odd == 0)
    def _():
        run(far_a, far_b)

    @pl.when(odd != 0)
    def _():
        run(far_b, far_a)


def gathered(b_ref, b0, b1):
    half = b0.shape[0]
    b_ref[:half, :] = b0[...]
    b_ref[half:, :] = b1[...]
    return b_ref[...]


def own_kernel(width, own, b0, b1, w, g, t_ref, b_ref):
    b = gathered(b_ref, b0, b1)
    t_ref[...] = part_of_t(b, own.at[0], own.at[1], w[0, : b.shape[0], :], g[...], width)


def far_kernel(width, far_a, far_b, b0, b1, w, g, t_ref, b_ref):
    b = gathered(b_ref, b0, b1)

    def run(real, imag):
        t_ref[...] = part_of_t(b, real, imag, w[1, : b.shape[0], :], g[...], width)

    either_way(far_a, far_b, run)


def last_kernel(width, own, far_a, far_b, b0, b1, w, g, t_own, t_far, t_ref, b_ref):
    b = gathered(b_ref, b0, b1)
    start = w.shape[1] - b.shape[0]

    def run(real, imag):
        of_own = t_own[...] + part_of_t(b, own.at[0], own.at[1], w[0, start:, :], g[...], width)
        of_far = t_far[...] + part_of_t(b, real, imag, w[1, start:, :], g[...], width)
        t_ref[...] = dense(of_own, of_far)

    either_way(far_a, far_b, run)


def dense(own, far):
    mid, tail = own.shape[0] // 2, own.shape[1] - 128
    rest = [part[rows, 128:] for rows in (slice(None, mid), slice(mid, None)) for part in (own, far)]
    assert 4 * tail == 128
    return jnp.concatenate([own[:, :128], far[:, :128], jnp.concatenate(rest, 1)], 0)


def spread(value):
    rows = value.shape[0] * 2 // 5
    rest = value[2 * rows :]
    pairs = []
    for at in range(2):
        tail = [rest[:, 32 * part : 32 * (part + 1)] for part in (at, at + 2)]
        pairs.append(jnp.concatenate([value[at * rows : (at + 1) * rows], jnp.concatenate(tail, 0)], 1))
    return pairs


def coded(piece, lanes):
    largest = jnp.maximum(jnp.max(jnp.abs(piece), axis=1, keepdims=True), 1e-30)
    exponent = jnp.floor(jnp.log2(largest)) + 1.0
    values = jnp.floor(piece * jnp.exp2(14.0 - exponent) + 0.5)
    rows, columns = piece.shape
    tail = jnp.broadcast_to(exponent, (rows, lanes - columns))
    return jnp.concatenate([values, tail], 1).astype(jnp.int32).astype(jnp.int16)


def decoded(value):
    value = value.astype(jnp.int32).astype(F32)
    return value * jnp.exp2(value[:, 125:126] - 14.0)


def packed(u, at, columns):
    third = columns // 3
    tall = jnp.concatenate([u[:, at + p * third : at + (p + 1) * third] for p in range(3)], 0)
    rows = tall.shape[0] // 5
    return jnp.concatenate([tall[g * rows : (g + 1) * rows] for g in range(5)], 1)


def unpacked(value, columns):
    third = columns // 3
    tall = jnp.concatenate([value[:, g * third : (g + 1) * third] for g in range(5)], 0)
    rows = tall.shape[0] // 3
    return jnp.concatenate([tall[p * rows : (p + 1) * rows] for p in range(3)], 1)


def cluster_kernel(
    width, columns, own, near, far_a, far_b, diag_a, diag_b, t, t_yh, t_core, t_diag, out, u_ref
):
    yh, core, odd = lax.axis_index("yh"), lax.axis_index("core"), odd_x()
    chips, _, lanes = out.shape
    span = 2 * chips * columns
    shift = span % 128
    window = pl.ds(pl.multiple_of(yh * (span - shift), 128), span + shift)
    half = 4 * width
    t, t_yh, t_core, t_diag = (spread(ref[...]) for ref in (t, t_yh, t_core, t_diag))
    swap = jnp.full(t[0].shape, odd) > 0
    total = None
    for value, first, second, swapped in (
        (t[0] + t_yh[1], own.at[0], own.at[1], False),
        (t_core[0] + t_diag[1], near.at[0], near.at[1], False),
        (t[1] + t_yh[0], far_a, far_b, True),
        (t_core[1] + t_diag[0], diag_a, diag_b, True),
    ):
        partner = turned(value, width, -1)
        if swapped:
            value, partner = jnp.where(swap, partner, value), jnp.where(swap, value, partner)
        for factor, data in ((value, first), (partner, second)):
            high = factor.astype(BF16)
            low = (factor - high.astype(F32)).astype(BF16)
            u = jnp.dot(jnp.concatenate([high, low], 0), data[:, window], preferred_element_type=F32)
            total = u if total is None else total + u
    u_ref[...] = total[:half] + total[half:]
    for row in range(2):
        for parity in range(2):

            @pl.when((yh == row) & (core == parity))
            def _():
                for chip in range(chips):
                    piece = packed(u_ref[...], (2 * chip + parity) * columns + row * shift, columns)
                    out[chip] = coded(piece, lanes)


def final_kernel(arrived, mask, out):
    total = decoded(arrived[0])
    for chip in range(1, arrived.shape[0]):
        total = total + decoded(arrived[chip])
    cells, width, parts, columns = out.shape
    value = unpacked(total, columns)
    for f in range(cells):
        for part in range(parts):
            for j in range(width):
                row = (f * parts + part) * width + j
                out[f, j, pl.ds(part, 1), :] = value[row : row + 1] * mask[pl.ds(f, 1), :]


def call(kernel, name, shapes, specs, scratch=(), mib=8, flops=0):
    return pl.pallas_call(
        kernel,
        out_shape=shapes,
        in_specs=[pl.BlockSpec(memory_space=space) for space in specs],
        out_specs=jax.tree.map(lambda _: pl.BlockSpec(memory_space=pltpu.VMEM), shapes),
        scratch_shapes=scratch,
        compiler_params=pltpu.CompilerParams(vmem_limit_bytes=mib * 2**20),
        cost_estimate=pl.CostEstimate(flops=flops, bytes_accessed=2**20, transcendentals=0),
        name=name,
    )


def shards(coefficients, class_weight, diff_class, frag_cells, block_pattern):
    own = coefficients[0]
    _, occupied, functions = own.shape
    yh, z, core = (lax.axis_index(name) for name in KA)
    band = lax.axis_index("yl") * PARTS[4] + lax.axis_index("x")
    width = occupied // (PARTS[3] * PARTS[4])
    group = 2 * width
    kpoint_count = PARTS[0] * PARTS[1] * PARTS[2]
    cells = frag_cells.shape[0]
    up = [(i, (i + 1) % PARTS[1]) for i in range(PARTS[1])]
    down = [(j, i) for i, j in up]
    swap = [(0, 1), (1, 0)]
    right = [(i, (i + 1) % PARTS[4]) for i in range(PARTS[4])]
    left = [(j, i) for i, j in right]
    vmem, smem = pltpu.VMEM, pltpu.SMEM

    far_a = lax.ppermute(lax.dynamic_index_in_dim(own, odd_x(), 0, keepdims=False), "yh", swap)
    near = lax.ppermute(own, "core", swap)
    block = lax.dynamic_slice_in_dim(own, band * width, width, 1).reshape(group, functions)
    blocks = [block]
    offsets = [0, -1, 1, -2, 2, -3, 3, -4]
    from_below = from_above = block
    for step in range(1, PARTS[1] // 2):
        from_below = lax.ppermute(from_below, "z", up)
        from_above = lax.ppermute(from_above, "z", down)
        if step == 2:
            from_below, from_above, near = lax.optimization_barrier((from_below, from_above, near))
        if step == 3:
            from_below, from_above, far_a = lax.optimization_barrier((from_below, from_above, far_a))
        blocks += [from_below, from_above]
    mid = occupied // 2
    from_left = lax.ppermute(far_a[:mid], "x", right)
    from_right = lax.ppermute(far_a[mid:], "x", left)
    split = 5
    first = jnp.concatenate(blocks[:split], 0)
    first_near = lax.ppermute(first, "core", swap)

    k_points = []
    for these in (offsets[:split], offsets[split:]):
        k_points += [(offset, False) for offset in these] + [(offset, True) for offset in these]
    early, late = 2 * split * group, 2 * (len(offsets) - split) * group
    angles = 2.0 * np.pi * np.arange(kpoint_count) / kpoint_count
    tables = [jnp.asarray((f(angles) / kpoint_count).astype(np.float32)) for f in (np.cos, np.sin)]
    later_cells, _ = lax.optimization_barrier((frag_cells, first))
    weights, g_first, g_last = call(
        functools.partial(prep_kernel, width, functions, k_points),
        "phases",
        (
            jax.ShapeDtypeStruct((2, early + late, 1), F32),
            jax.ShapeDtypeStruct((8 * width, early), BF16),
            jax.ShapeDtypeStruct((8 * width, late), BF16),
        ),
        [smem] * 5,
    )(later_cells, diff_class, class_weight, *tables)

    one = jax.ShapeDtypeStruct((4 * width, occupied), F32)
    scratch = [pltpu.VMEM((early, functions), BF16)]
    b_first = (first, first_near, weights, g_first)
    kernel = functools.partial(own_kernel, width)
    t_own = call(kernel, "own_first", one, [vmem] * 5, scratch, flops=10**9)(own, *b_first)
    cut = 24
    blocks.append(lax.ppermute(from_below[:cut], "z", up))
    blocks.append(lax.ppermute(from_above[cut:], "z", down))
    held = (blocks[-2], blocks[-1], from_left, from_right, t_own)
    blocks[-2], blocks[-1], from_left, from_right, t_own = lax.optimization_barrier(held)
    last = jnp.concatenate(blocks[split:], 0)
    far_b = jnp.concatenate([from_left, from_right], 0)
    last, far_b = lax.optimization_barrier((last, far_b))
    last_near = lax.ppermute(last, "core", swap)
    later_a, _ = lax.optimization_barrier((far_a, far_b))
    diag_a, diag_b = (lax.ppermute(half, "core", swap) for half in (later_a, far_b))
    kernel = functools.partial(far_kernel, width)
    t_far = call(kernel, "far_first", one, [vmem] * 6, scratch, flops=10**9)(far_a, far_b, *b_first)
    t = call(
        functools.partial(last_kernel, width),
        "last_terms",
        jax.ShapeDtypeStruct((20 * width // 2, 128), F32),
        [vmem] * 9,
        [pltpu.VMEM((late, functions), BF16)],
        flops=10**9,
    )(own, far_a, far_b, last, last_near, weights, g_last, t_own, t_far)

    t_yh = lax.ppermute(t, "yh", swap)
    t_core = lax.ppermute(t, "core", swap)
    t_diag = lax.ppermute(t_yh, "core", swap)
    chips = PARTS[1]
    columns = functions // kpoint_count
    span = 2 * chips * columns
    pieces = call(
        functools.partial(cluster_kernel, width, columns),
        "cluster_terms",
        jax.ShapeDtypeStruct((chips, 4 * width * 3 // 5, 128), jnp.int16),
        [vmem] * 10,
        [pltpu.VMEM((4 * width, span + span % 128), F32)],
        flops=10**9,
    )(own, near, far_a, far_b, diag_a, diag_b, t, t_yh, t_core, t_diag)

    arrived = lax.all_to_all(pieces, "z", 0, 0, tiled=True)
    index = (yh * PARTS[1] + z) * 2 + core
    block_size = functions // block_pattern.shape[1]
    local_ids = (index * columns + jnp.arange(columns, dtype=jnp.int32)) // block_size
    block_ids = jnp.arange(block_pattern.shape[1], dtype=jnp.int32)
    onehot = (block_ids[:, None] == local_ids[None, :]).astype(F32)
    mask = jnp.dot(block_pattern.astype(F32), onehot, precision=lax.Precision.HIGHEST)
    cluster = call(
        final_kernel,
        "sum_and_mask",
        jax.ShapeDtypeStruct((cells, width, 2, columns), F32),
        [vmem] * 2,
        mib=4,
    )(arrived, mask)
    return jnp.transpose(cluster, (0, 2, 1, 3))


def solution(mesh):
    placed = (P(KA, None, None, None), P(), P(), P(), P())
    return jax.shard_map(
        shards,
        mesh=Mesh(mesh.devices.reshape(PARTS), AXES),
        in_specs=placed,
        out_specs=P(None, None, BAND, KA),
        check_vma=False,
    )
```

```python
import functools

import jax
import jax.numpy as jnp
import numpy as np
from jax import lax
from jax.experimental import pallas as pl
from jax.experimental.pallas import tpu as pltpu
from jax.sharding import Mesh
from jax.sharding import PartitionSpec as P

AXES = ("yh", "z", "core", "yl", "x")
KA = ("yh", "z", "core")
BAND = ("yl", "x")
PARTS = (2, 8, 2, 2, 4)
F32 = jnp.float32
BF16 = jnp.bfloat16


def prep_kernel(width, functions, k_points, cells, diff_class, class_weight, cos_table, sin_table, w_ref, g0, g1):
    yh, z, core = (lax.axis_index(name) for name in KA)
    group = 2 * width
    count = len(k_points)
    rows, lanes = 4 * width, group * count
    points = []
    for offset, flip in k_points:
        points.append((yh * PARTS[1] + lax.rem(z + offset + PARTS[1], PARTS[1])) * 2 + (1 - core if flip else core))
    for q, row in enumerate((yh, 1 - yh)):
        q_point = (row * PARTS[1] + z) * 2 + core
        for at, point in enumerate(points):
            weight = jnp.full((group, 1), class_weight[diff_class[point, q_point]], F32)
            w_ref[q, pl.ds(at * group, group), :] = weight / functions
    lane = lax.broadcasted_iota(jnp.int32, (1, lanes), 1)
    tables = []
    for f in range(2):
        cosines = jnp.zeros((1, lanes), F32)
        sines = jnp.zeros((1, lanes), F32)
        for at, point in enumerate(points):
            here = (lane >= at * group) & (lane < (at + 1) * group)
            index = lax.rem(point * cells[f], cos_table.shape[0])
            cosines = jnp.where(here, cos_table[index], cosines)
            sines = jnp.where(here, sin_table[index], sines)
        tables.append((cosines, sines))
    row = lax.broadcasted_iota(jnp.int32, (rows, lanes), 0)
    col = lax.broadcasted_iota(jnp.int32, (rows, lanes), 1)
    first = row < group
    cosines = jnp.where(first, tables[0][0], tables[1][0])
    sines = jnp.where(first, tables[0][1], tables[1][1])
    real, real_m = row % group < width, col % group < width
    value = jnp.where(real == real_m, cosines, jnp.where(real, -sines, sines))
    value = jnp.where(row % width == col % width, value, 0.0)
    high = value.astype(BF16)
    low = (value - high.astype(F32)).astype(BF16)
    both = jnp.concatenate([high, low], 0)
    g0[...] = both[:, : g0.shape[1]]
    g1[...] = both[:, g0.shape[1] :]


def turned(value, width, sign):
    rows = value.shape[0]
    real = lax.broadcasted_iota(jnp.int32, value.shape, 0) % (2 * width) < width
    up, down = pltpu.roll(value, rows - width, 0), pltpu.roll(value, width, 0)
    return jnp.where(real, up, -down) if sign > 0 else jnp.where(real, -up, down)


def part_of_t(b, real, imag, w, g, width):
    contract = (((1,), (1,)), ((), ()))
    m = lax.dot_general(b, real[...], contract, preferred_element_type=F32)
    m = m + turned(lax.dot_general(b, imag[...], contract, preferred_element_type=F32), width, 1)
    t = jnp.dot(g, (w * m).astype(BF16), preferred_element_type=F32)
    half = t.shape[0] // 2
    return t[:half] + t[half:]


def odd_x():
    return jnp.bitwise_and(lax.axis_index("x"), 1)


def either_way(far_a, far_b, run):
    odd = odd_x()

    @pl.when(odd == 0)
    def _():
        run(far_a, far_b)

    @pl.when(odd != 0)
    def _():
        run(far_b, far_a)


def gathered(b_ref, b0, b1):
    half = b0.shape[0]
    b_ref[:half, :] = b0[...]
    b_ref[half:, :] = b1[...]
    return b_ref[...]


def own_kernel(width, own, b0, b1, w, g, t_ref, b_ref):
    b = gathered(b_ref, b0, b1)
    t_ref[...] = part_of_t(b, own.at[0], own.at[1], w[0, : b.shape[0], :], g[...], width)


def far_kernel(width, far_a, far_b, b0, b1, w, g, t_ref, b_ref):
    b = gathered(b_ref, b0, b1)

    def run(real, imag):
        t_ref[...] = part_of_t(b, real, imag, w[1, : b.shape[0], :], g[...], width)

    either_way(far_a, far_b, run)


def last_kernel(width, own, far_a, far_b, b0, b1, w, g, t_own, t_far, t_ref, b_ref):
    b = gathered(b_ref, b0, b1)
    start = w.shape[1] - b.shape[0]

    def run(real, imag):
        of_own = t_own[...] + part_of_t(b, own.at[0], own.at[1], w[0, start:, :], g[...], width)
        of_far = t_far[...] + part_of_t(b, real, imag, w[1, start:, :], g[...], width)
        t_ref[...] = dense(of_own, of_far)

    either_way(far_a, far_b, run)


def dense(own, far):
    mid, tail = own.shape[0] // 2, own.shape[1] - 128
    rest = [part[rows, 128:] for rows in (slice(None, mid), slice(mid, None)) for part in (own, far)]
    assert 4 * tail == 128
    return jnp.concatenate([own[:, :128], far[:, :128], jnp.concatenate(rest, 1)], 0)


def spread(value):
    rows = value.shape[0] * 2 // 5
    rest = value[2 * rows :]
    pairs = []
    for at in range(2):
        tail = [rest[:, 32 * part : 32 * (part + 1)] for part in (at, at + 2)]
        pairs.append(jnp.concatenate([value[at * rows : (at + 1) * rows], jnp.concatenate(tail, 0)], 1))
    return pairs


def coded(piece, lanes):
    largest = jnp.maximum(jnp.max(jnp.abs(piece), axis=1, keepdims=True), 1e-30)
    exponent = jnp.floor(jnp.log2(largest)) + 1.0
    values = jnp.floor(piece * jnp.exp2(14.0 - exponent) + 0.5)
    rows, columns = piece.shape
    tail = jnp.broadcast_to(exponent, (rows, lanes - columns))
    return jnp.concatenate([values, tail], 1).astype(jnp.int32).astype(jnp.int16)


def decoded(value):
    value = value.astype(jnp.int32).astype(F32)
    return value * jnp.exp2(value[:, 125:126] - 14.0)


def packed(u, at, columns):
    third = columns // 3
    tall = jnp.concatenate([u[:, at + p * third : at + (p + 1) * third] for p in range(3)], 0)
    rows = tall.shape[0] // 5
    return jnp.concatenate([tall[g * rows : (g + 1) * rows] for g in range(5)], 1)


def unpacked(value, columns):
    third = columns // 3
    tall = jnp.concatenate([value[:, g * third : (g + 1) * third] for g in range(5)], 0)
    rows = tall.shape[0] // 3
    return jnp.concatenate([tall[p * rows : (p + 1) * rows] for p in range(3)], 1)


def cluster_kernel(
    width, columns, own, far_a, far_b, near_hbm, diag_a_hbm, diag_b_hbm, t, t_yh, t_core, t_diag, out,
    u_ref, near, diag_a, diag_b, sems
):
    fetches = []
    for at, (source, target) in enumerate(((near_hbm, near), (diag_a_hbm, diag_a), (diag_b_hbm, diag_b))):
        fetches.append(pltpu.make_async_copy(source, target, sems.at[at]))
        fetches[-1].start()
    yh, core, odd = lax.axis_index("yh"), lax.axis_index("core"), odd_x()
    chips, lanes = PARTS[1], out.shape[1]
    span = 2 * chips * columns
    shift = span % 128
    window = pl.ds(pl.multiple_of(yh * (span - shift), 128), span + shift)
    half = 4 * width
    t, t_yh, t_core, t_diag = (spread(ref[...]) for ref in (t, t_yh, t_core, t_diag))
    swap = jnp.full(t[0].shape, odd) > 0
    total = None
    for value, first, second, swapped, waits in (
        (t[0] + t_yh[1], own.at[0], own.at[1], False, []),
        (t[1] + t_yh[0], far_a, far_b, True, []),
        (t_core[0] + t_diag[1], near.at[0], near.at[1], False, fetches[:1]),
        (t_core[1] + t_diag[0], diag_a, diag_b, True, fetches[1:]),
    ):
        for fetch in waits:
            fetch.wait()
        partner = turned(value, width, -1)
        if swapped:
            value, partner = jnp.where(swap, partner, value), jnp.where(swap, value, partner)
        for factor, data in ((value, first), (partner, second)):
            high = factor.astype(BF16)
            low = (factor - high.astype(F32)).astype(BF16)
            u = jnp.dot(jnp.concatenate([high, low], 0), data[:, window], preferred_element_type=F32)
            total = u if total is None else total + u
    u_ref[...] = total[:half] + total[half:]
    for row in range(2):
        for parity in range(2):

            @pl.when((yh == row) & (core == parity))
            def _():
                starts = [(2 * chip + parity) * columns + row * shift for chip in range(chips)]
                pieces = [packed(u_ref[...], at, columns) for at in starts]
                out[...] = coded(jnp.concatenate(pieces, 0), lanes)


def final_kernel(arrived, mask, out):
    total = decoded(arrived[0])
    for chip in range(1, arrived.shape[0]):
        total = total + decoded(arrived[chip])
    cells, width, parts, columns = out.shape
    value = unpacked(total, columns)
    for f in range(cells):
        for part in range(parts):
            for j in range(width):
                row = (f * parts + part) * width + j
                out[f, j, pl.ds(part, 1), :] = value[row : row + 1] * mask[pl.ds(f, 1), :]


def call(kernel, name, shapes, specs, scratch=(), mib=8, flops=0):
    return pl.pallas_call(
        kernel,
        out_shape=shapes,
        in_specs=[pl.BlockSpec(memory_space=space) for space in specs],
        out_specs=jax.tree.map(lambda _: pl.BlockSpec(memory_space=pltpu.VMEM), shapes),
        scratch_shapes=scratch,
        compiler_params=pltpu.CompilerParams(vmem_limit_bytes=mib * 2**20),
        cost_estimate=pl.CostEstimate(flops=flops, bytes_accessed=2**20, transcendentals=0),
        name=name,
    )


def shards(coefficients, class_weight, diff_class, frag_cells, block_pattern):
    own = coefficients[0]
    _, occupied, functions = own.shape
    yh, z, core = (lax.axis_index(name) for name in KA)
    band = lax.axis_index("yl") * PARTS[4] + lax.axis_index("x")
    width = occupied // (PARTS[3] * PARTS[4])
    group = 2 * width
    kpoint_count = PARTS[0] * PARTS[1] * PARTS[2]
    cells = frag_cells.shape[0]
    up = [(i, (i + 1) % PARTS[1]) for i in range(PARTS[1])]
    down = [(j, i) for i, j in up]
    swap = [(0, 1), (1, 0)]
    right = [(i, (i + 1) % PARTS[4]) for i in range(PARTS[4])]
    left = [(j, i) for i, j in right]
    vmem, smem = pltpu.VMEM, pltpu.SMEM

    far_a = lax.ppermute(lax.dynamic_index_in_dim(own, odd_x(), 0, keepdims=False), "yh", swap)
    near = lax.ppermute(own, "core", swap)
    block = lax.dynamic_slice_in_dim(own, band * width, width, 1).reshape(group, functions)
    blocks = [block]
    offsets = [0, -1, 1, -2, 2, -3, 3, -4]
    from_below = from_above = block
    for step in range(1, PARTS[1] // 2):
        from_below = lax.ppermute(from_below, "z", up)
        from_above = lax.ppermute(from_above, "z", down)
        if step == 2:
            from_below, from_above, near = lax.optimization_barrier((from_below, from_above, near))
        if step == 3:
            from_below, from_above, far_a = lax.optimization_barrier((from_below, from_above, far_a))
        blocks += [from_below, from_above]
    mid = occupied // 2
    from_left = lax.ppermute(far_a[:mid], "x", right)
    from_right = lax.ppermute(far_a[mid:], "x", left)
    split = 5
    first = jnp.concatenate(blocks[:split], 0)
    first_near = lax.ppermute(first, "core", swap)

    k_points = []
    for these in (offsets[:split], offsets[split:]):
        k_points += [(offset, False) for offset in these] + [(offset, True) for offset in these]
    early, late = 2 * split * group, 2 * (len(offsets) - split) * group
    angles = 2.0 * np.pi * np.arange(kpoint_count) / kpoint_count
    tables = [jnp.asarray((f(angles) / kpoint_count).astype(np.float32)) for f in (np.cos, np.sin)]
    later_cells, _ = lax.optimization_barrier((frag_cells, first))
    weights, g_first, g_last = call(
        functools.partial(prep_kernel, width, functions, k_points),
        "phases",
        (
            jax.ShapeDtypeStruct((2, early + late, 1), F32),
            jax.ShapeDtypeStruct((8 * width, early), BF16),
            jax.ShapeDtypeStruct((8 * width, late), BF16),
        ),
        [smem] * 5,
    )(later_cells, diff_class, class_weight, *tables)

    one = jax.ShapeDtypeStruct((4 * width, occupied), F32)
    scratch = [pltpu.VMEM((early, functions), BF16)]
    b_first = (first, first_near, weights, g_first)
    kernel = functools.partial(own_kernel, width)
    t_own = call(kernel, "own_first", one, [vmem] * 5, scratch, flops=10**9)(own, *b_first)
    cut = 24
    blocks.append(lax.ppermute(from_below[:cut], "z", up))
    blocks.append(lax.ppermute(from_above[cut:], "z", down))
    held = (blocks[-2], blocks[-1], from_left, from_right, t_own)
    blocks[-2], blocks[-1], from_left, from_right, t_own = lax.optimization_barrier(held)
    last = jnp.concatenate(blocks[split:], 0)
    far_b = jnp.concatenate([from_left, from_right], 0)
    last, far_b = lax.optimization_barrier((last, far_b))
    last_near = lax.ppermute(last, "core", swap)
    later_a, _ = lax.optimization_barrier((far_a, far_b))
    diag_a, diag_b = (lax.ppermute(half, "core", swap) for half in (later_a, far_b))
    kernel = functools.partial(far_kernel, width)
    t_far = call(kernel, "far_first", one, [vmem] * 6, scratch, flops=10**9)(far_a, far_b, *b_first)
    t = call(
        functools.partial(last_kernel, width),
        "last_terms",
        jax.ShapeDtypeStruct((20 * width // 2, 128), F32),
        [vmem] * 9,
        [pltpu.VMEM((late, functions), BF16)],
        flops=10**9,
    )(own, far_a, far_b, last, last_near, weights, g_last, t_own, t_far)

    t_yh = lax.ppermute(t, "yh", swap)
    t_core = lax.ppermute(t, "core", swap)
    t_diag = lax.ppermute(t_yh, "core", swap)
    chips = PARTS[1]
    columns = functions // kpoint_count
    span = 2 * chips * columns
    rows = 4 * width * 3 // 5
    pieces = call(
        functools.partial(cluster_kernel, width, columns),
        "cluster_terms",
        jax.ShapeDtypeStruct((chips * rows, 128), jnp.int16),
        [vmem] * 3 + [pl.ANY] * 3 + [vmem] * 4,
        [
            pltpu.VMEM((4 * width, span + span % 128), F32),
            pltpu.VMEM(own.shape, BF16),
            pltpu.VMEM(far_a.shape, BF16),
            pltpu.VMEM(far_a.shape, BF16),
            pltpu.SemaphoreType.DMA((3,)),
        ],
        mib=12,
        flops=10**9,
    )(own, far_a, far_b, near, diag_a, diag_b, t, t_yh, t_core, t_diag)

    pieces = pieces.reshape(chips, rows, 128)
    arrived = lax.all_to_all(pieces, "z", 0, 0, tiled=True)
    index = (yh * PARTS[1] + z) * 2 + core
    block_size = functions // block_pattern.shape[1]
    local_ids = (index * columns + jnp.arange(columns, dtype=jnp.int32)) // block_size
    block_ids = jnp.arange(block_pattern.shape[1], dtype=jnp.int32)
    onehot = (block_ids[:, None] == local_ids[None, :]).astype(F32)
    mask = jnp.dot(block_pattern.astype(F32), onehot, precision=lax.Precision.HIGHEST)
    cluster = call(
        final_kernel,
        "sum_and_mask",
        jax.ShapeDtypeStruct((cells, width, 2, columns), F32),
        [vmem] * 2,
        mib=4,
    )(arrived, mask)
    return jnp.transpose(cluster, (0, 2, 1, 3))


def solution(mesh):
    placed = (P(KA, None, None, None), P(), P(), P(), P())
    return jax.shard_map(
        shards,
        mesh=Mesh(mesh.devices.reshape(PARTS), AXES),
        in_specs=placed,
        out_specs=P(None, None, BAND, KA),
        check_vma=False,
    )
```

```python
import functools

import jax
import jax.numpy as jnp
import numpy as np
from jax import lax
from jax.experimental import pallas as pl
from jax.experimental.pallas import tpu as pltpu
from jax.sharding import Mesh
from jax.sharding import PartitionSpec as P

AXES = ("yh", "z", "core", "yl", "x")
KA = ("yh", "z", "core")
BAND = ("yl", "x")
PARTS = (2, 8, 2, 2, 4)
F32 = jnp.float32
BF16 = jnp.bfloat16


def prep_kernel(width, functions, k_points, cells, diff_class, class_weight, cos_table, sin_table, w_ref, g0, g1):
    yh, z, core = (lax.axis_index(name) for name in KA)
    group = 2 * width
    count = len(k_points)
    rows, lanes = 4 * width, group * count
    points = []
    for offset, flip in k_points:
        points.append((yh * PARTS[1] + lax.rem(z + offset + PARTS[1], PARTS[1])) * 2 + (1 - core if flip else core))
    for q, row in enumerate((yh, 1 - yh)):
        q_point = (row * PARTS[1] + z) * 2 + core
        for at, point in enumerate(points):
            weight = jnp.full((group, 1), class_weight[diff_class[point, q_point]], F32)
            w_ref[q, pl.ds(at * group, group), :] = weight / functions
    lane = lax.broadcasted_iota(jnp.int32, (1, lanes), 1)
    tables = []
    for f in range(2):
        cosines = jnp.zeros((1, lanes), F32)
        sines = jnp.zeros((1, lanes), F32)
        for at, point in enumerate(points):
            here = (lane >= at * group) & (lane < (at + 1) * group)
            index = lax.rem(point * cells[f], cos_table.shape[0])
            cosines = jnp.where(here, cos_table[index], cosines)
            sines = jnp.where(here, sin_table[index], sines)
        tables.append((cosines, sines))
    row = lax.broadcasted_iota(jnp.int32, (rows, lanes), 0)
    col = lax.broadcasted_iota(jnp.int32, (rows, lanes), 1)
    first = row < group
    cosines = jnp.where(first, tables[0][0], tables[1][0])
    sines = jnp.where(first, tables[0][1], tables[1][1])
    real, real_m = row % group < width, col % group < width
    value = jnp.where(real == real_m, cosines, jnp.where(real, -sines, sines))
    value = jnp.where(row % width == col % width, value, 0.0)
    high = value.astype(BF16)
    low = (value - high.astype(F32)).astype(BF16)
    both = jnp.concatenate([high, low], 0)
    g0[...] = both[:, : g0.shape[1]]
    g1[...] = both[:, g0.shape[1] :]


def turned(value, width, sign):
    rows = value.shape[0]
    real = lax.broadcasted_iota(jnp.int32, value.shape, 0) % (2 * width) < width
    up, down = pltpu.roll(value, rows - width, 0), pltpu.roll(value, width, 0)
    return jnp.where(real, up, -down) if sign > 0 else jnp.where(real, -up, down)


def overlaps(b, part):
    return lax.dot_general(b, part[...], (((1,), (1,)), ((), ())), preferred_element_type=F32)


def part_of_t(b, real, imag, w, g, width):
    return t_of(overlaps(b, real), overlaps(b, imag), w, g, width)


def t_of(real, imag, w, g, width):
    m = real + turned(imag, width, 1)
    t = jnp.dot(g, (w * m).astype(BF16), preferred_element_type=F32)
    half = t.shape[0] // 2
    return t[:half] + t[half:]


def odd_x():
    return jnp.bitwise_and(lax.axis_index("x"), 1)


def either_way(far_a, far_b, run):
    odd = odd_x()

    @pl.when(odd == 0)
    def _():
        run(far_a, far_b)

    @pl.when(odd != 0)
    def _():
        run(far_b, far_a)


def gathered(b_ref, b0, b1):
    half = b0.shape[0]
    b_ref[:half, :] = b0[...]
    b_ref[half:, :] = b1[...]
    return b_ref[...]


def own_kernel(width, own, b0, b1, w, g, t_ref, b_ref):
    b = gathered(b_ref, b0, b1)
    t_ref[...] = part_of_t(b, own.at[0], own.at[1], w[0, : b.shape[0], :], g[...], width)


def half_kernel(far_a, b0, b1, out, b_ref):
    out[...] = overlaps(gathered(b_ref, b0, b1), far_a)


def far_kernel(width, part_a, far_b, b0, b1, w, g, t_ref, b_ref):
    b = gathered(b_ref, b0, b1)
    part_b = overlaps(b, far_b)
    odd = odd_x()

    @pl.when(odd == 0)
    def _():
        t_ref[...] = t_of(part_a[...], part_b, w[1, : b.shape[0], :], g[...], width)

    @pl.when(odd != 0)
    def _():
        t_ref[...] = t_of(part_b, part_a[...], w[1, : b.shape[0], :], g[...], width)


def last_kernel(width, own, far_a, far_b, b0, b1, w, g, t_own, t_far, t_ref, b_ref):
    b = gathered(b_ref, b0, b1)
    start = w.shape[1] - b.shape[0]

    def run(real, imag):
        of_own = t_own[...] + part_of_t(b, own.at[0], own.at[1], w[0, start:, :], g[...], width)
        of_far = t_far[...] + part_of_t(b, real, imag, w[1, start:, :], g[...], width)
        t_ref[...] = dense(of_own, of_far)

    either_way(far_a, far_b, run)


def dense(own, far):
    mid, tail = own.shape[0] // 2, own.shape[1] - 128
    rest = [part[rows, 128:] for rows in (slice(None, mid), slice(mid, None)) for part in (own, far)]
    assert 4 * tail == 128
    return jnp.concatenate([own[:, :128], far[:, :128], jnp.concatenate(rest, 1)], 0)


def spread(value):
    rows = value.shape[0] * 2 // 5
    rest = value[2 * rows :]
    pairs = []
    for at in range(2):
        tail = [rest[:, 32 * part : 32 * (part + 1)] for part in (at, at + 2)]
        pairs.append(jnp.concatenate([value[at * rows : (at + 1) * rows], jnp.concatenate(tail, 0)], 1))
    return pairs


def coded(piece, lanes):
    rows, columns = piece.shape
    piece = jnp.concatenate([piece, jnp.zeros((rows, lanes - columns), F32)], 1)
    largest = jnp.maximum(jnp.max(jnp.abs(piece), axis=0, keepdims=True), 1e-30)
    exponent = jnp.floor(jnp.log2(largest)) + 1.0
    values = jnp.floor(piece * jnp.exp2(14.0 - exponent) + 0.5)
    return jnp.concatenate([values, jnp.broadcast_to(exponent, (8, lanes))], 0)


def decoded(value):
    value = value.astype(jnp.int32).astype(F32)
    rows = value.shape[0] - 8
    return value[:rows] * jnp.exp2(value[rows : rows + 1] - 14.0)


def packed(u, at, columns):
    third = columns // 3
    tall = jnp.concatenate([u[:, at + p * third : at + (p + 1) * third] for p in range(3)], 0)
    rows = tall.shape[0] // 5
    return jnp.concatenate([tall[g * rows : (g + 1) * rows] for g in range(5)], 1)


def unpacked(value, columns):
    third = columns // 3
    tall = jnp.concatenate([value[:, g * third : (g + 1) * third] for g in range(5)], 0)
    rows = tall.shape[0] // 3
    return jnp.concatenate([tall[p * rows : (p + 1) * rows] for p in range(3)], 1)


def cluster_kernel(
    width, columns, own, far_a, far_b, near_hbm, diag_a_hbm, diag_b_hbm, t, t_yh, t_core, t_diag, out,
    u_ref, near, diag_a, diag_b, sems
):
    fetches = []
    for at, (source, target) in enumerate(((near_hbm, near), (diag_a_hbm, diag_a), (diag_b_hbm, diag_b))):
        fetches.append(pltpu.make_async_copy(source, target, sems.at[at]))
        fetches[-1].start()
    yh, core, odd = lax.axis_index("yh"), lax.axis_index("core"), odd_x()
    chips, lanes = PARTS[1], out.shape[1]
    span = 2 * chips * columns
    shift = span % 128
    window = pl.ds(pl.multiple_of(yh * (span - shift), 128), span + shift)
    half = 4 * width
    t, t_yh, t_core, t_diag = (spread(ref[...]) for ref in (t, t_yh, t_core, t_diag))
    swap = jnp.full(t[0].shape, odd) > 0
    total = None
    for value, first, second, swapped, waits in (
        (t[0] + t_yh[1], own.at[0], own.at[1], False, []),
        (t[1] + t_yh[0], far_a, far_b, True, []),
        (t_core[0] + t_diag[1], near.at[0], near.at[1], False, fetches[:1]),
        (t_core[1] + t_diag[0], diag_a, diag_b, True, fetches[1:]),
    ):
        for fetch in waits:
            fetch.wait()
        partner = turned(value, width, -1)
        if swapped:
            value, partner = jnp.where(swap, partner, value), jnp.where(swap, value, partner)
        for factor, data in ((value, first), (partner, second)):
            high = factor.astype(BF16)
            low = (factor - high.astype(F32)).astype(BF16)
            u = jnp.dot(jnp.concatenate([high, low], 0), data[:, window], preferred_element_type=F32)
            total = u if total is None else total + u
    u_ref[...] = total[:half] + total[half:]
    for row in range(2):
        for parity in range(2):

            @pl.when((yh == row) & (core == parity))
            def _():
                starts = [(2 * chip + parity) * columns + row * shift for chip in range(chips)]
                pieces = [coded(packed(u_ref[...], at, columns), lanes) for at in starts]
                out[...] = jnp.concatenate(pieces, 0).astype(jnp.int32).astype(jnp.int16)


def final_kernel(arrived, mask, out):
    total = decoded(arrived[0])
    for chip in range(1, arrived.shape[0]):
        total = total + decoded(arrived[chip])
    cells, width, parts, columns = out.shape
    value = unpacked(total, columns)
    for f in range(cells):
        kept = value[f * parts * width : (f + 1) * parts * width] * mask[pl.ds(f, 1), :]
        for part in range(parts):
            for j in range(width):
                out[f, j, pl.ds(part, 1), :] = kept[part * width + j : part * width + j + 1]


def call(kernel, name, shapes, specs, scratch=(), mib=8, flops=0):
    return pl.pallas_call(
        kernel,
        out_shape=shapes,
        in_specs=[pl.BlockSpec(memory_space=space) for space in specs],
        out_specs=jax.tree.map(lambda _: pl.BlockSpec(memory_space=pltpu.VMEM), shapes),
        scratch_shapes=scratch,
        compiler_params=pltpu.CompilerParams(vmem_limit_bytes=mib * 2**20),
        cost_estimate=pl.CostEstimate(flops=flops, bytes_accessed=2**20, transcendentals=0),
        name=name,
    )


def shards(coefficients, class_weight, diff_class, frag_cells, block_pattern):
    own = coefficients[0]
    _, occupied, functions = own.shape
    yh, z, core = (lax.axis_index(name) for name in KA)
    band = lax.axis_index("yl") * PARTS[4] + lax.axis_index("x")
    width = occupied // (PARTS[3] * PARTS[4])
    group = 2 * width
    kpoint_count = PARTS[0] * PARTS[1] * PARTS[2]
    cells = frag_cells.shape[0]
    up = [(i, (i + 1) % PARTS[1]) for i in range(PARTS[1])]
    down = [(j, i) for i, j in up]
    swap = [(0, 1), (1, 0)]
    right = [(i, (i + 1) % PARTS[4]) for i in range(PARTS[4])]
    left = [(j, i) for i, j in right]
    vmem, smem = pltpu.VMEM, pltpu.SMEM

    far_a = lax.ppermute(lax.dynamic_index_in_dim(own, odd_x(), 0, keepdims=False), "yh", swap)
    near = lax.ppermute(own, "core", swap)
    block = lax.dynamic_slice_in_dim(own, band * width, width, 1).reshape(group, functions)
    blocks = [block]
    offsets = [0, -1, 1, -2, 2, -3, 3, -4]
    from_below = from_above = block
    for step in range(1, PARTS[1] // 2):
        from_below = lax.ppermute(from_below, "z", up)
        from_above = lax.ppermute(from_above, "z", down)
        if step == 2:
            from_below, from_above, near = lax.optimization_barrier((from_below, from_above, near))
        if step == 3:
            from_below, from_above, far_a = lax.optimization_barrier((from_below, from_above, far_a))
        blocks += [from_below, from_above]
    mid = occupied // 2
    from_left = lax.ppermute(far_a[:mid], "x", right)
    from_right = lax.ppermute(far_a[mid:], "x", left)
    split = 5
    first = jnp.concatenate(blocks[:split], 0)
    first_near = lax.ppermute(first, "core", swap)

    k_points = []
    for these in (offsets[:split], offsets[split:]):
        k_points += [(offset, False) for offset in these] + [(offset, True) for offset in these]
    early, late = 2 * split * group, 2 * (len(offsets) - split) * group
    angles = 2.0 * np.pi * np.arange(kpoint_count) / kpoint_count
    tables = [jnp.asarray((f(angles) / kpoint_count).astype(np.float32)) for f in (np.cos, np.sin)]
    later_cells, _ = lax.optimization_barrier((frag_cells, first))
    weights, g_first, g_last = call(
        functools.partial(prep_kernel, width, functions, k_points),
        "phases",
        (
            jax.ShapeDtypeStruct((2, early + late, 1), F32),
            jax.ShapeDtypeStruct((8 * width, early), BF16),
            jax.ShapeDtypeStruct((8 * width, late), BF16),
        ),
        [smem] * 5,
    )(later_cells, diff_class, class_weight, *tables)

    one = jax.ShapeDtypeStruct((4 * width, occupied), F32)
    scratch = [pltpu.VMEM((early, functions), BF16)]
    b_first = (first, first_near, weights, g_first)
    kernel = functools.partial(own_kernel, width)
    t_own = call(kernel, "own_first", one, [vmem] * 5, scratch, flops=10**9)(own, *b_first)
    cut = 24
    blocks.append(lax.ppermute(from_below[:cut], "z", up))
    blocks.append(lax.ppermute(from_above[cut:], "z", down))
    part = jax.ShapeDtypeStruct((early, occupied), F32)
    part_a = call(half_kernel, "far_half", part, [vmem] * 3, scratch, flops=10**9)(far_a, first, first_near)
    held = (blocks[-2], blocks[-1], from_left, from_right, t_own, part_a)
    blocks[-2], blocks[-1], from_left, from_right, t_own, part_a = lax.optimization_barrier(held)
    last = jnp.concatenate(blocks[split:], 0)
    far_b = jnp.concatenate([from_left, from_right], 0)
    last, far_b = lax.optimization_barrier((last, far_b))
    last_near = lax.ppermute(last, "core", swap)
    later_a, _ = lax.optimization_barrier((far_a, far_b))
    diag_a, diag_b = (lax.ppermute(half, "core", swap) for half in (later_a, far_b))
    kernel = functools.partial(far_kernel, width)
    t_far = call(kernel, "far_first", one, [vmem] * 6, scratch, flops=10**9)(part_a, far_b, *b_first)
    t = call(
        functools.partial(last_kernel, width),
        "last_terms",
        jax.ShapeDtypeStruct((20 * width // 2, 128), F32),
        [vmem] * 9,
        [pltpu.VMEM((late, functions), BF16)],
        flops=10**9,
    )(own, far_a, far_b, last, last_near, weights, g_last, t_own, t_far)

    t_yh = lax.ppermute(t, "yh", swap)
    t_core = lax.ppermute(t, "core", swap)
    t_diag = lax.ppermute(t_yh, "core", swap)
    chips = PARTS[1]
    columns = functions // kpoint_count
    span = 2 * chips * columns
    rows = 4 * width * 3 // 5 + 8
    pieces = call(
        functools.partial(cluster_kernel, width, columns),
        "cluster_terms",
        jax.ShapeDtypeStruct((chips * rows, 128), jnp.int16),
        [vmem] * 3 + [pl.ANY] * 3 + [vmem] * 4,
        [
            pltpu.VMEM((4 * width, span + span % 128), F32),
            pltpu.VMEM(own.shape, BF16),
            pltpu.VMEM(far_a.shape, BF16),
            pltpu.VMEM(far_a.shape, BF16),
            pltpu.SemaphoreType.DMA((3,)),
        ],
        mib=12,
        flops=10**9,
    )(own, far_a, far_b, near, diag_a, diag_b, t, t_yh, t_core, t_diag)

    pieces = pieces.reshape(chips, rows, 128)
    arrived = lax.all_to_all(pieces, "z", 0, 0, tiled=True)
    index = (yh * PARTS[1] + z) * 2 + core
    block_size = functions // block_pattern.shape[1]
    local_ids = (index * columns + jnp.arange(columns, dtype=jnp.int32)) // block_size
    block_ids = jnp.arange(block_pattern.shape[1], dtype=jnp.int32)
    onehot = (block_ids[:, None] == local_ids[None, :]).astype(F32)
    mask = jnp.dot(block_pattern.astype(F32), onehot, precision=lax.Precision.HIGHEST)
    cluster = call(
        final_kernel,
        "sum_and_mask",
        jax.ShapeDtypeStruct((cells, width, 2, columns), F32),
        [vmem] * 2,
        mib=4,
    )(arrived, mask)
    return jnp.transpose(cluster, (0, 2, 1, 3))


def solution(mesh):
    placed = (P(KA, None, None, None), P(), P(), P(), P())
    return jax.shard_map(
        shards,
        mesh=Mesh(mesh.devices.reshape(PARTS), AXES),
        in_specs=placed,
        out_specs=P(None, None, BAND, KA),
        check_vma=False,
    )
```

```python
import functools

import jax
import jax.numpy as jnp
import numpy as np
from jax import lax
from jax.experimental import pallas as pl
from jax.experimental.pallas import tpu as pltpu
from jax.sharding import Mesh
from jax.sharding import PartitionSpec as P

AXES = ("yh", "z", "core", "yl", "x")
KA = ("yh", "z", "core")
BAND = ("yl", "x")
PARTS = (2, 8, 2, 2, 4)
F32 = jnp.float32
BF16 = jnp.bfloat16


def prep_kernel(width, functions, k_points, cells, diff_class, class_weight, cos_table, sin_table, w_ref, g0, g1):
    yh, z, core = (lax.axis_index(name) for name in KA)
    group = 2 * width
    count = len(k_points)
    rows, lanes = 4 * width, group * count
    points = []
    for offset, flip in k_points:
        points.append((yh * PARTS[1] + lax.rem(z + offset + PARTS[1], PARTS[1])) * 2 + (1 - core if flip else core))
    for q, row in enumerate((yh, 1 - yh)):
        q_point = (row * PARTS[1] + z) * 2 + core
        for at, point in enumerate(points):
            weight = jnp.full((group, 1), class_weight[diff_class[point, q_point]], F32)
            w_ref[q, pl.ds(at * group, group), :] = weight / functions
    lane = lax.broadcasted_iota(jnp.int32, (1, lanes), 1)
    tables = []
    for f in range(2):
        cosines = jnp.zeros((1, lanes), F32)
        sines = jnp.zeros((1, lanes), F32)
        for at, point in enumerate(points):
            here = (lane >= at * group) & (lane < (at + 1) * group)
            index = lax.rem(point * cells[f], cos_table.shape[0])
            cosines = jnp.where(here, cos_table[index], cosines)
            sines = jnp.where(here, sin_table[index], sines)
        tables.append((cosines, sines))
    row = lax.broadcasted_iota(jnp.int32, (rows, lanes), 0)
    col = lax.broadcasted_iota(jnp.int32, (rows, lanes), 1)
    first = row < group
    cosines = jnp.where(first, tables[0][0], tables[1][0])
    sines = jnp.where(first, tables[0][1], tables[1][1])
    real, real_m = row % group < width, col % group < width
    value = jnp.where(real == real_m, cosines, jnp.where(real, -sines, sines))
    value = jnp.where(row % width == col % width, value, 0.0)
    high = value.astype(BF16)
    low = (value - high.astype(F32)).astype(BF16)
    both = jnp.concatenate([high, low], 0)
    g0[...] = both[:, : g0.shape[1]]
    g1[...] = both[:, g0.shape[1] :]


def turned(value, width, sign):
    rows = value.shape[0]
    real = lax.broadcasted_iota(jnp.int32, value.shape, 0) % (2 * width) < width
    up, down = pltpu.roll(value, rows - width, 0), pltpu.roll(value, width, 0)
    return jnp.where(real, up, -down) if sign > 0 else jnp.where(real, -up, down)


def overlaps(b, part):
    return lax.dot_general(b, part[...], (((1,), (1,)), ((), ())), preferred_element_type=F32)


def part_of_t(b, real, imag, w, g, width):
    return t_of(overlaps(b, real), overlaps(b, imag), w, g, width)


def t_of(real, imag, w, g, width):
    m = real + turned(imag, width, 1)
    t = jnp.dot(g, (w * m).astype(BF16), preferred_element_type=F32)
    half = t.shape[0] // 2
    return t[:half] + t[half:]


def odd_x():
    return jnp.bitwise_and(lax.axis_index("x"), 1)


def either_way(far_a, far_b, run):
    odd = odd_x()

    @pl.when(odd == 0)
    def _():
        run(far_a, far_b)

    @pl.when(odd != 0)
    def _():
        run(far_b, far_a)


def gathered(b_ref, b0, b1):
    half = b0.shape[0]
    b_ref[:half, :] = b0[...]
    b_ref[half:, :] = b1[...]
    return b_ref[...]


def own_kernel(width, own, b0, b1, w, g, t_ref, b_ref):
    b = gathered(b_ref, b0, b1)
    t_ref[...] = part_of_t(b, own.at[0], own.at[1], w[0, : b.shape[0], :], g[...], width)


def half_kernel(far_a, b0, b1, out, b_ref):
    out[...] = overlaps(gathered(b_ref, b0, b1), far_a)


def far_kernel(width, part_a, far_b, b0, b1, w, g, t_ref, b_ref):
    b = gathered(b_ref, b0, b1)
    part_b = overlaps(b, far_b)
    odd = odd_x()

    @pl.when(odd == 0)
    def _():
        t_ref[...] = t_of(part_a[...], part_b, w[1, : b.shape[0], :], g[...], width)

    @pl.when(odd != 0)
    def _():
        t_ref[...] = t_of(part_b, part_a[...], w[1, : b.shape[0], :], g[...], width)


def last_kernel(width, own, far_a, far_b, b0, b1, w, g, t_own, t_far, t_ref, b_ref):
    b = gathered(b_ref, b0, b1)
    start = w.shape[1] - b.shape[0]

    def run(real, imag):
        of_own = t_own[...] + part_of_t(b, own.at[0], own.at[1], w[0, start:, :], g[...], width)
        of_far = t_far[...] + part_of_t(b, real, imag, w[1, start:, :], g[...], width)
        t_ref[...] = dense(of_own, of_far)

    either_way(far_a, far_b, run)


def dense(own, far):
    mid, tail = own.shape[0] // 2, own.shape[1] - 128
    rest = [part[rows, 128:] for rows in (slice(None, mid), slice(mid, None)) for part in (own, far)]
    assert 4 * tail == 128
    return jnp.concatenate([own[:, :128], far[:, :128], jnp.concatenate(rest, 1)], 0)


def spread(value):
    rows = value.shape[0] * 2 // 5
    rest = value[2 * rows :]
    pairs = []
    for at in range(2):
        tail = [rest[:, 32 * part : 32 * (part + 1)] for part in (at, at + 2)]
        pairs.append(jnp.concatenate([value[at * rows : (at + 1) * rows], jnp.concatenate(tail, 0)], 1))
    return pairs


def coded(pieces, lanes):
    rows, columns = pieces[0].shape
    spare = jnp.zeros((rows, lanes - columns), F32)
    pieces = [jnp.concatenate([piece, spare], 1) for piece in pieces]
    largest = jnp.concatenate([jnp.max(jnp.abs(piece), axis=0, keepdims=True) for piece in pieces], 0)
    exponents = jnp.floor(jnp.log2(jnp.maximum(largest, 1e-30))) + 1.0
    scales = jnp.exp2(14.0 - exponents)
    out = []
    for at, piece in enumerate(pieces):
        out.append(jnp.floor(piece * scales[at : at + 1] + 0.5))
        out.append(jnp.broadcast_to(exponents[at : at + 1], (8, lanes)))
    return jnp.concatenate(out, 0).astype(jnp.int32).astype(jnp.int16)


def decoded(value):
    value = value.astype(jnp.int32).astype(F32)
    rows = value.shape[0] - 8
    return value[:rows] * jnp.exp2(value[rows : rows + 1] - 14.0)


def packed(u, at, columns):
    third = columns // 3
    tall = jnp.concatenate([u[:, at + p * third : at + (p + 1) * third] for p in range(3)], 0)
    rows = tall.shape[0] // 5
    return jnp.concatenate([tall[g * rows : (g + 1) * rows] for g in range(5)], 1)


def unpacked(value, columns):
    third = columns // 3
    tall = jnp.concatenate([value[:, g * third : (g + 1) * third] for g in range(5)], 0)
    rows = tall.shape[0] // 3
    return jnp.concatenate([tall[p * rows : (p + 1) * rows] for p in range(3)], 1)


def cluster_kernel(
    width, columns, own, far_a, far_b, near_hbm, diag_a_hbm, diag_b_hbm, t, t_yh, t_core, t_diag, out,
    u_ref, near, diag_a, diag_b, sems
):
    fetches = []
    for at, (source, target) in enumerate(((near_hbm, near), (diag_a_hbm, diag_a), (diag_b_hbm, diag_b))):
        fetches.append(pltpu.make_async_copy(source, target, sems.at[at]))
        fetches[-1].start()
    yh, core, odd = lax.axis_index("yh"), lax.axis_index("core"), odd_x()
    chips, lanes = PARTS[1], out.shape[1]
    span = 2 * chips * columns
    shift = span % 128
    window = pl.ds(pl.multiple_of(yh * (span - shift), 128), span + shift)
    half = 4 * width
    t, t_yh, t_core, t_diag = (spread(ref[...]) for ref in (t, t_yh, t_core, t_diag))
    swap = jnp.full(t[0].shape, odd) > 0
    total = None
    for value, first, second, swapped, waits in (
        (t[0] + t_yh[1], own.at[0], own.at[1], False, []),
        (t[1] + t_yh[0], far_a, far_b, True, []),
        (t_core[0] + t_diag[1], near.at[0], near.at[1], False, fetches[:1]),
        (t_core[1] + t_diag[0], diag_a, diag_b, True, fetches[1:]),
    ):
        for fetch in waits:
            fetch.wait()
        partner = turned(value, width, -1)
        if swapped:
            value, partner = jnp.where(swap, partner, value), jnp.where(swap, value, partner)
        for factor, data in ((value, first), (partner, second)):
            high = factor.astype(BF16)
            low = (factor - high.astype(F32)).astype(BF16)
            u = jnp.dot(jnp.concatenate([high, low], 0), data[:, window], preferred_element_type=F32)
            total = u if total is None else total + u
    u_ref[...] = total[:half] + total[half:]
    for row in range(2):
        for parity in range(2):

            @pl.when((yh == row) & (core == parity))
            def _():
                starts = [(2 * chip + parity) * columns + row * shift for chip in range(chips)]
                out[...] = coded([packed(u_ref[...], at, columns) for at in starts], lanes)


def final_kernel(arrived, mask, out):
    total = decoded(arrived[0])
    for chip in range(1, arrived.shape[0]):
        total = total + decoded(arrived[chip])
    cells, width, parts, columns = out.shape
    value = unpacked(total, columns)
    for f in range(cells):
        kept = value[f * parts * width : (f + 1) * parts * width] * mask[pl.ds(f, 1), :]
        for part in range(parts):
            for j in range(width):
                out[f, j, pl.ds(part, 1), :] = kept[part * width + j : part * width + j + 1]


def call(kernel, name, shapes, specs, scratch=(), mib=8, flops=0):
    return pl.pallas_call(
        kernel,
        out_shape=shapes,
        in_specs=[pl.BlockSpec(memory_space=space) for space in specs],
        out_specs=jax.tree.map(lambda _: pl.BlockSpec(memory_space=pltpu.VMEM), shapes),
        scratch_shapes=scratch,
        compiler_params=pltpu.CompilerParams(vmem_limit_bytes=mib * 2**20),
        cost_estimate=pl.CostEstimate(flops=flops, bytes_accessed=2**20, transcendentals=0),
        name=name,
    )


def shards(coefficients, class_weight, diff_class, frag_cells, block_pattern):
    own = coefficients[0]
    _, occupied, functions = own.shape
    yh, z, core = (lax.axis_index(name) for name in KA)
    band = lax.axis_index("yl") * PARTS[4] + lax.axis_index("x")
    width = occupied // (PARTS[3] * PARTS[4])
    group = 2 * width
    kpoint_count = PARTS[0] * PARTS[1] * PARTS[2]
    cells = frag_cells.shape[0]
    up = [(i, (i + 1) % PARTS[1]) for i in range(PARTS[1])]
    down = [(j, i) for i, j in up]
    swap = [(0, 1), (1, 0)]
    right = [(i, (i + 1) % PARTS[4]) for i in range(PARTS[4])]
    left = [(j, i) for i, j in right]
    vmem, smem = pltpu.VMEM, pltpu.SMEM

    far_a = lax.ppermute(lax.dynamic_index_in_dim(own, odd_x(), 0, keepdims=False), "yh", swap)
    near = lax.ppermute(own, "core", swap)
    block = lax.dynamic_slice_in_dim(own, band * width, width, 1).reshape(group, functions)
    blocks = [block]
    offsets = [0, -1, 1, -2, 2, -3, 3, -4]
    from_below = from_above = block
    for step in range(1, PARTS[1] // 2):
        from_below = lax.ppermute(from_below, "z", up)
        from_above = lax.ppermute(from_above, "z", down)
        if step == 2:
            from_below, from_above, near = lax.optimization_barrier((from_below, from_above, near))
        if step == 3:
            from_below, from_above, far_a = lax.optimization_barrier((from_below, from_above, far_a))
        blocks += [from_below, from_above]
    mid = occupied // 2
    from_left = lax.ppermute(far_a[:mid], "x", right)
    from_right = lax.ppermute(far_a[mid:], "x", left)
    split = 5
    first = jnp.concatenate(blocks[:split], 0)
    first_near = lax.ppermute(first, "core", swap)

    k_points = []
    for these in (offsets[:split], offsets[split:]):
        k_points += [(offset, False) for offset in these] + [(offset, True) for offset in these]
    early, late = 2 * split * group, 2 * (len(offsets) - split) * group
    angles = 2.0 * np.pi * np.arange(kpoint_count) / kpoint_count
    tables = [jnp.asarray((f(angles) / kpoint_count).astype(np.float32)) for f in (np.cos, np.sin)]
    later_cells, _ = lax.optimization_barrier((frag_cells, first))
    weights, g_first, g_last = call(
        functools.partial(prep_kernel, width, functions, k_points),
        "phases",
        (
            jax.ShapeDtypeStruct((2, early + late, 1), F32),
            jax.ShapeDtypeStruct((8 * width, early), BF16),
            jax.ShapeDtypeStruct((8 * width, late), BF16),
        ),
        [smem] * 5,
    )(later_cells, diff_class, class_weight, *tables)

    one = jax.ShapeDtypeStruct((4 * width, occupied), F32)
    scratch = [pltpu.VMEM((early, functions), BF16)]
    b_first = (first, first_near, weights, g_first)
    kernel = functools.partial(own_kernel, width)
    t_own = call(kernel, "own_first", one, [vmem] * 5, scratch, flops=10**9)(own, *b_first)
    cut = 24
    blocks.append(lax.ppermute(from_below[:cut], "z", up))
    blocks.append(lax.ppermute(from_above[cut:], "z", down))
    part = jax.ShapeDtypeStruct((early, occupied), F32)
    part_a = call(half_kernel, "far_half", part, [vmem] * 3, scratch, flops=10**9)(far_a, first, first_near)
    held = (blocks[-2], blocks[-1], from_left, from_right, t_own, part_a)
    blocks[-2], blocks[-1], from_left, from_right, t_own, part_a = lax.optimization_barrier(held)
    last = jnp.concatenate(blocks[split:], 0)
    far_b = jnp.concatenate([from_left, from_right], 0)
    last, far_b = lax.optimization_barrier((last, far_b))
    last_near = lax.ppermute(last, "core", swap)
    later_a, _ = lax.optimization_barrier((far_a, far_b))
    diag_a, diag_b = (lax.ppermute(value, "core", swap) for value in (later_a, far_b))
    kernel = functools.partial(far_kernel, width)
    t_far = call(kernel, "far_first", one, [vmem] * 6, scratch, flops=10**9)(part_a, far_b, *b_first)
    t = call(
        functools.partial(last_kernel, width),
        "last_terms",
        jax.ShapeDtypeStruct((20 * width // 2, 128), F32),
        [vmem] * 9,
        [pltpu.VMEM((late, functions), BF16)],
        flops=10**9,
    )(own, far_a, far_b, last, last_near, weights, g_last, t_own, t_far)

    t_yh = lax.ppermute(t, "yh", swap)
    t_core = lax.ppermute(t, "core", swap)
    t_diag = lax.ppermute(t_yh, "core", swap)
    chips = PARTS[1]
    columns = functions // kpoint_count
    span = 2 * chips * columns
    rows = 4 * width * 3 // 5 + 8
    pieces = call(
        functools.partial(cluster_kernel, width, columns),
        "cluster_terms",
        jax.ShapeDtypeStruct((chips * rows, 128), jnp.int16),
        [vmem] * 3 + [pltpu.HBM] * 3 + [vmem] * 4,
        [
            pltpu.VMEM((4 * width, span + span % 128), F32),
            pltpu.VMEM(own.shape, BF16),
            pltpu.VMEM(far_a.shape, BF16),
            pltpu.VMEM(far_a.shape, BF16),
            pltpu.SemaphoreType.DMA((3,)),
        ],
        mib=12,
        flops=10**9,
    )(own, far_a, far_b, near, diag_a, diag_b, t, t_yh, t_core, t_diag)

    pieces = pieces.reshape(chips, rows, 128)
    arrived = lax.all_to_all(pieces, "z", 0, 0, tiled=True)
    index = (yh * PARTS[1] + z) * 2 + core
    block_size = functions // block_pattern.shape[1]
    local_ids = (index * columns + jnp.arange(columns, dtype=jnp.int32)) // block_size
    block_ids = jnp.arange(block_pattern.shape[1], dtype=jnp.int32)
    onehot = (block_ids[:, None] == local_ids[None, :]).astype(F32)
    mask = jnp.dot(block_pattern.astype(F32), onehot, precision=lax.Precision.HIGHEST)
    cluster = call(
        final_kernel,
        "sum_and_mask",
        jax.ShapeDtypeStruct((cells, width, 2, columns), F32),
        [vmem] * 2,
        mib=4,
    )(arrived, mask)
    return jnp.transpose(cluster, (0, 2, 1, 3))


def solution(mesh):
    placed = (P(KA, None, None, None), P(), P(), P(), P())
    return jax.shard_map(
        shards,
        mesh=Mesh(mesh.devices.reshape(PARTS), AXES),
        in_specs=placed,
        out_specs=P(None, None, BAND, KA),
        check_vma=False,
    )
```

```python
import functools

import jax
import jax.numpy as jnp
import numpy as np
from jax import lax
from jax.experimental import pallas as pl
from jax.experimental.pallas import tpu as pltpu
from jax.sharding import Mesh
from jax.sharding import PartitionSpec as P

AXES = ("yh", "z", "core", "yl", "x")
KA = ("yh", "z", "core")
BAND = ("yl", "x")
PARTS = (2, 8, 2, 2, 4)
F32 = jnp.float32
BF16 = jnp.bfloat16


def prep_kernel(width, functions, k_points, cells, diff_class, class_weight, cos_table, sin_table, w_ref, g0, g1):
    yh, z, core = (lax.axis_index(name) for name in KA)
    group = 2 * width
    count = len(k_points)
    rows, lanes = 4 * width, group * count
    points = []
    for offset, flip in k_points:
        points.append((yh * PARTS[1] + lax.rem(z + offset + PARTS[1], PARTS[1])) * 2 + (1 - core if flip else core))
    for q, row in enumerate((yh, 1 - yh)):
        q_point = (row * PARTS[1] + z) * 2 + core
        for at, point in enumerate(points):
            weight = jnp.full((group, 1), class_weight[diff_class[point, q_point]], F32)
            w_ref[q, pl.ds(at * group, group), :] = weight / functions
    lane = lax.broadcasted_iota(jnp.int32, (1, lanes), 1)
    tables = []
    for f in range(2):
        cosines = jnp.zeros((1, lanes), F32)
        sines = jnp.zeros((1, lanes), F32)
        for at, point in enumerate(points):
            here = (lane >= at * group) & (lane < (at + 1) * group)
            index = lax.rem(point * cells[f], cos_table.shape[0])
            cosines = jnp.where(here, cos_table[index], cosines)
            sines = jnp.where(here, sin_table[index], sines)
        tables.append((cosines, sines))
    row = lax.broadcasted_iota(jnp.int32, (rows, lanes), 0)
    col = lax.broadcasted_iota(jnp.int32, (rows, lanes), 1)
    first = row < group
    cosines = jnp.where(first, tables[0][0], tables[1][0])
    sines = jnp.where(first, tables[0][1], tables[1][1])
    real, real_m = row % group < width, col % group < width
    value = jnp.where(real == real_m, cosines, jnp.where(real, -sines, sines))
    value = jnp.where(row % width == col % width, value, 0.0)
    high = value.astype(BF16)
    low = (value - high.astype(F32)).astype(BF16)
    both = jnp.concatenate([high, low], 0)
    g0[...] = both[:, : g0.shape[1]]
    g1[...] = both[:, g0.shape[1] :]


def turned(value, width, sign):
    rows = value.shape[0]
    real = lax.broadcasted_iota(jnp.int32, value.shape, 0) % (2 * width) < width
    up, down = pltpu.roll(value, rows - width, 0), pltpu.roll(value, width, 0)
    return jnp.where(real, up, -down) if sign > 0 else jnp.where(real, -up, down)


def part_of_t(b, real, imag, w, g, width):
    contract = (((1,), (1,)), ((), ()))
    m = lax.dot_general(b, real[...], contract, preferred_element_type=F32)
    m = m + turned(lax.dot_general(b, imag[...], contract, preferred_element_type=F32), width, 1)
    t = jnp.dot(g, (w * m).astype(BF16), preferred_element_type=F32)
    half = t.shape[0] // 2
    return t[:half] + t[half:]


def odd_x():
    return jnp.bitwise_and(lax.axis_index("x"), 1)


def either_way(far_a, far_b, run):
    odd = odd_x()

    @pl.when(odd == 0)
    def _():
        run(far_a, far_b)

    @pl.when(odd != 0)
    def _():
        run(far_b, far_a)


def gathered(b_ref, b0, b1):
    half = b0.shape[0]
    b_ref[:half, :] = b0[...]
    b_ref[half:, :] = b1[...]
    return b_ref[...]


def own_kernel(width, own, b0, b1, w, g, t_ref, b_ref):
    b = gathered(b_ref, b0, b1)
    t_ref[...] = part_of_t(b, own.at[0], own.at[1], w[0, : b.shape[0], :], g[...], width)


def far_kernel(width, far_a, far_b, b0, b1, w, g, t_ref, b_ref):
    b = gathered(b_ref, b0, b1)

    def run(real, imag):
        t_ref[...] = part_of_t(b, real, imag, w[1, : b.shape[0], :], g[...], width)

    either_way(far_a, far_b, run)


def last_kernel(width, own, far_a, far_b, b0, b1, w, g, t_own, t_far, t_ref, b_ref):
    b = gathered(b_ref, b0, b1)
    start = w.shape[1] - b.shape[0]

    def run(real, imag):
        of_own = t_own[...] + part_of_t(b, own.at[0], own.at[1], w[0, start:, :], g[...], width)
        of_far = t_far[...] + part_of_t(b, real, imag, w[1, start:, :], g[...], width)
        t_ref[...] = dense(of_own, of_far)

    either_way(far_a, far_b, run)


def dense(own, far):
    mid, tail = own.shape[0] // 2, own.shape[1] - 128
    rest = [part[rows, 128:] for rows in (slice(None, mid), slice(mid, None)) for part in (own, far)]
    assert 4 * tail == 128
    return jnp.concatenate([own[:, :128], far[:, :128], jnp.concatenate(rest, 1)], 0)


def spread(value):
    rows = value.shape[0] * 2 // 5
    rest = value[2 * rows :]
    pairs = []
    for at in range(2):
        tail = [rest[:, 32 * part : 32 * (part + 1)] for part in (at, at + 2)]
        pairs.append(jnp.concatenate([value[at * rows : (at + 1) * rows], jnp.concatenate(tail, 0)], 1))
    return pairs


def coded(pieces, lanes):
    rows, columns = pieces[0].shape
    spare = jnp.zeros((rows, lanes - columns), F32)
    pieces = [jnp.concatenate([piece, spare], 1) for piece in pieces]
    largest = jnp.concatenate([jnp.max(jnp.abs(piece), axis=0, keepdims=True) for piece in pieces], 0)
    exponents = jnp.floor(jnp.log2(jnp.maximum(largest, 1e-30))) + 1.0
    scales = jnp.exp2(14.0 - exponents)
    out = []
    for at, piece in enumerate(pieces):
        out.append(jnp.floor(piece * scales[at : at + 1] + 0.5))
        out.append(jnp.broadcast_to(exponents[at : at + 1], (8, lanes)))
    return jnp.concatenate(out, 0).astype(jnp.int32).astype(jnp.int16)


def decoded(value):
    value = value.astype(jnp.int32).astype(F32)
    rows = value.shape[0] - 8
    return value[:rows] * jnp.exp2(value[rows : rows + 1] - 14.0)


def packed(u, at, columns):
    third = columns // 3
    tall = jnp.concatenate([u[:, at + p * third : at + (p + 1) * third] for p in range(3)], 0)
    rows = tall.shape[0] // 5
    return jnp.concatenate([tall[g * rows : (g + 1) * rows] for g in range(5)], 1)


def unpacked(value, columns):
    third = columns // 3
    tall = jnp.concatenate([value[:, g * third : (g + 1) * third] for g in range(5)], 0)
    rows = tall.shape[0] // 3
    return jnp.concatenate([tall[p * rows : (p + 1) * rows] for p in range(3)], 1)


def cluster_kernel(
    width, columns, own, far_a, far_b, near_hbm, diag_a_hbm, diag_b_hbm, t, t_yh, t_core, t_diag, out,
    u_ref, near, diag_a, diag_b, sems
):
    fetches = []
    for at, (source, target) in enumerate(((near_hbm, near), (diag_a_hbm, diag_a), (diag_b_hbm, diag_b))):
        fetches.append(pltpu.make_async_copy(source, target, sems.at[at]))
        fetches[-1].start()
    yh, core, odd = lax.axis_index("yh"), lax.axis_index("core"), odd_x()
    chips, lanes = PARTS[1], out.shape[1]
    span = 2 * chips * columns
    shift = span % 128
    window = pl.ds(pl.multiple_of(yh * (span - shift), 128), span + shift)
    half = 4 * width
    t, t_yh, t_core, t_diag = (spread(ref[...]) for ref in (t, t_yh, t_core, t_diag))
    swap = jnp.full(t[0].shape, odd) > 0
    total = None
    for value, first, second, swapped, waits in (
        (t[0] + t_yh[1], own.at[0], own.at[1], False, []),
        (t[1] + t_yh[0], far_a, far_b, True, []),
        (t_core[0] + t_diag[1], near.at[0], near.at[1], False, fetches[:1]),
        (t_core[1] + t_diag[0], diag_a, diag_b, True, fetches[1:]),
    ):
        for fetch in waits:
            fetch.wait()
        partner = turned(value, width, -1)
        if swapped:
            value, partner = jnp.where(swap, partner, value), jnp.where(swap, value, partner)
        for factor, data in ((value, first), (partner, second)):
            high = factor.astype(BF16)
            low = (factor - high.astype(F32)).astype(BF16)
            u = jnp.dot(jnp.concatenate([high, low], 0), data[:, window], preferred_element_type=F32)
            total = u if total is None else total + u
    u_ref[...] = total[:half] + total[half:]
    for row in range(2):
        for parity in range(2):

            @pl.when((yh == row) & (core == parity))
            def _():
                starts = [(2 * chip + parity) * columns + row * shift for chip in range(chips)]
                out[...] = coded([packed(u_ref[...], at, columns) for at in starts], lanes)


def final_kernel(arrived, mask, out):
    total = decoded(arrived[0])
    for chip in range(1, arrived.shape[0]):
        total = total + decoded(arrived[chip])
    cells, width, parts, columns = out.shape
    value = unpacked(total, columns)
    for f in range(cells):
        kept = value[f * parts * width : (f + 1) * parts * width] * mask[pl.ds(f, 1), :]
        for part in range(parts):
            for j in range(width):
                out[f, j, pl.ds(part, 1), :] = kept[part * width + j : part * width + j + 1]


def call(kernel, name, shapes, specs, scratch=(), mib=8, flops=0):
    return pl.pallas_call(
        kernel,
        out_shape=shapes,
        in_specs=[pl.BlockSpec(memory_space=space) for space in specs],
        out_specs=jax.tree.map(lambda _: pl.BlockSpec(memory_space=pltpu.VMEM), shapes),
        scratch_shapes=scratch,
        compiler_params=pltpu.CompilerParams(vmem_limit_bytes=mib * 2**20),
        cost_estimate=pl.CostEstimate(flops=flops, bytes_accessed=2**20, transcendentals=0),
        name=name,
    )


def shards(coefficients, class_weight, diff_class, frag_cells, block_pattern):
    own = coefficients[0]
    _, occupied, functions = own.shape
    yh, z, core = (lax.axis_index(name) for name in KA)
    band = lax.axis_index("yl") * PARTS[4] + lax.axis_index("x")
    width = occupied // (PARTS[3] * PARTS[4])
    group = 2 * width
    kpoint_count = PARTS[0] * PARTS[1] * PARTS[2]
    cells = frag_cells.shape[0]
    up = [(i, (i + 1) % PARTS[1]) for i in range(PARTS[1])]
    down = [(j, i) for i, j in up]
    swap = [(0, 1), (1, 0)]
    right = [(i, (i + 1) % PARTS[4]) for i in range(PARTS[4])]
    left = [(j, i) for i, j in right]
    vmem, smem = pltpu.VMEM, pltpu.SMEM

    half = lax.dynamic_index_in_dim(own, odd_x(), 0, keepdims=False)
    rows_1, rows_2 = 3 * occupied // 5, 2 * occupied // 5
    far_1 = lax.ppermute(half[:rows_1], "yh", swap)
    near = lax.ppermute(own, "core", swap)
    block = lax.dynamic_slice_in_dim(own, band * width, width, 1).reshape(group, functions)
    blocks = [block]
    offsets = [0, -1, 1, -2, 2, -3, 3, -4]
    from_below = from_above = block
    for step in range(1, PARTS[1] // 2):
        from_below = lax.ppermute(from_below, "z", up)
        from_above = lax.ppermute(from_above, "z", down)
        if step == 1:
            half_2, _ = lax.optimization_barrier((half[rows_1:], from_below))
            far_2 = lax.ppermute(half_2, "yh", swap)
        if step == 2:
            held = (from_below, from_above, near, far_1)
            from_below, from_above, near, far_1 = lax.optimization_barrier(held)
            left_1 = lax.ppermute(far_1[: rows_1 // 2], "x", right)
            right_1 = lax.ppermute(far_1[rows_1 // 2 :], "x", left)
        if step == 3:
            from_below, from_above, far_2 = lax.optimization_barrier((from_below, from_above, far_2))
        blocks += [from_below, from_above]
    left_2 = lax.ppermute(far_2[: rows_2 // 2], "x", right)
    right_2 = lax.ppermute(far_2[rows_2 // 2 :], "x", left)
    far_a = jnp.concatenate([far_1, far_2], 0)
    split = 5
    first = jnp.concatenate(blocks[:split], 0)
    first_near = lax.ppermute(first, "core", swap)

    k_points = []
    for these in (offsets[:split], offsets[split:]):
        k_points += [(offset, False) for offset in these] + [(offset, True) for offset in these]
    early, late = 2 * split * group, 2 * (len(offsets) - split) * group
    angles = 2.0 * np.pi * np.arange(kpoint_count) / kpoint_count
    tables = [jnp.asarray((f(angles) / kpoint_count).astype(np.float32)) for f in (np.cos, np.sin)]
    later_cells, _ = lax.optimization_barrier((frag_cells, first))
    weights, g_first, g_last = call(
        functools.partial(prep_kernel, width, functions, k_points),
        "phases",
        (
            jax.ShapeDtypeStruct((2, early + late, 1), F32),
            jax.ShapeDtypeStruct((8 * width, early), BF16),
            jax.ShapeDtypeStruct((8 * width, late), BF16),
        ),
        [smem] * 5,
    )(later_cells, diff_class, class_weight, *tables)

    one = jax.ShapeDtypeStruct((4 * width, occupied), F32)
    scratch = [pltpu.VMEM((early, functions), BF16)]
    b_first = (first, first_near, weights, g_first)
    kernel = functools.partial(own_kernel, width)
    t_own = call(kernel, "own_first", one, [vmem] * 5, scratch, flops=10**9)(own, *b_first)
    cut = 24
    blocks.append(lax.ppermute(from_below[:cut], "z", up))
    blocks.append(lax.ppermute(from_above[cut:], "z", down))
    held = (blocks[-2], blocks[-1], left_1, right_1, left_2, right_2, t_own)
    blocks[-2], blocks[-1], left_1, right_1, left_2, right_2, t_own = lax.optimization_barrier(held)
    last = jnp.concatenate(blocks[split:], 0)
    far_b = jnp.concatenate([left_1, right_1, left_2, right_2], 0)
    last, far_b = lax.optimization_barrier((last, far_b))
    last_near = lax.ppermute(last, "core", swap)
    later_a, _ = lax.optimization_barrier((far_a, far_b))
    diag_a, diag_b = (lax.ppermute(half, "core", swap) for half in (later_a, far_b))
    kernel = functools.partial(far_kernel, width)
    t_far = call(kernel, "far_first", one, [vmem] * 6, scratch, flops=10**9)(far_a, far_b, *b_first)
    t = call(
        functools.partial(last_kernel, width),
        "last_terms",
        jax.ShapeDtypeStruct((20 * width // 2, 128), F32),
        [vmem] * 9,
        [pltpu.VMEM((late, functions), BF16)],
        flops=10**9,
    )(own, far_a, far_b, last, last_near, weights, g_last, t_own, t_far)

    t_yh = lax.ppermute(t, "yh", swap)
    t_core = lax.ppermute(t, "core", swap)
    t_diag = lax.ppermute(t_yh, "core", swap)
    chips = PARTS[1]
    columns = functions // kpoint_count
    span = 2 * chips * columns
    rows = 4 * width * 3 // 5 + 8
    pieces = call(
        functools.partial(cluster_kernel, width, columns),
        "cluster_terms",
        jax.ShapeDtypeStruct((chips * rows, 128), jnp.int16),
        [vmem] * 3 + [pl.ANY] * 3 + [vmem] * 4,
        [
            pltpu.VMEM((4 * width, span + span % 128), F32),
            pltpu.VMEM(own.shape, BF16),
            pltpu.VMEM(far_a.shape, BF16),
            pltpu.VMEM(far_a.shape, BF16),
            pltpu.SemaphoreType.DMA((3,)),
        ],
        mib=12,
        flops=10**9,
    )(own, far_a, far_b, near, diag_a, diag_b, t, t_yh, t_core, t_diag)

    pieces = pieces.reshape(chips, rows, 128)
    arrived = lax.all_to_all(pieces, "z", 0, 0, tiled=True)
    index = (yh * PARTS[1] + z) * 2 + core
    block_size = functions // block_pattern.shape[1]
    local_ids = (index * columns + jnp.arange(columns, dtype=jnp.int32)) // block_size
    block_ids = jnp.arange(block_pattern.shape[1], dtype=jnp.int32)
    onehot = (block_ids[:, None] == local_ids[None, :]).astype(F32)
    mask = jnp.dot(block_pattern.astype(F32), onehot, precision=lax.Precision.HIGHEST)
    cluster = call(
        final_kernel,
        "sum_and_mask",
        jax.ShapeDtypeStruct((cells, width, 2, columns), F32),
        [vmem] * 2,
        mib=4,
    )(arrived, mask)
    return jnp.transpose(cluster, (0, 2, 1, 3))


def solution(mesh):
    placed = (P(KA, None, None, None), P(), P(), P(), P())
    return jax.shard_map(
        shards,
        mesh=Mesh(mesh.devices.reshape(PARTS), AXES),
        in_specs=placed,
        out_specs=P(None, None, BAND, KA),
        check_vma=False,
    )
```

```python
import functools

import jax
import jax.numpy as jnp
import numpy as np
from jax import lax
from jax.experimental import pallas as pl
from jax.experimental.pallas import tpu as pltpu
from jax.sharding import Mesh
from jax.sharding import PartitionSpec as P

AXES = ("yh", "z", "core", "yl", "x")
KA = ("yh", "z", "core")
BAND = ("yl", "x")
PARTS = (2, 8, 2, 2, 4)
F32 = jnp.float32
BF16 = jnp.bfloat16


def prep_kernel(width, functions, k_points, cells, diff_class, class_weight, cos_table, sin_table, w_ref, g0, g1):
    yh, z, core = (lax.axis_index(name) for name in KA)
    group = 2 * width
    count = len(k_points)
    rows, lanes = 4 * width, group * count
    points = []
    for offset, flip in k_points:
        points.append((yh * PARTS[1] + lax.rem(z + offset + PARTS[1], PARTS[1])) * 2 + (1 - core if flip else core))
    for q, row in enumerate((yh, 1 - yh)):
        q_point = (row * PARTS[1] + z) * 2 + core
        for at, point in enumerate(points):
            weight = jnp.full((group, 1), class_weight[diff_class[point, q_point]], F32)
            w_ref[q, pl.ds(at * group, group), :] = weight / functions
    lane = lax.broadcasted_iota(jnp.int32, (1, lanes), 1)
    tables = []
    for f in range(2):
        cosines = jnp.zeros((1, lanes), F32)
        sines = jnp.zeros((1, lanes), F32)
        for at, point in enumerate(points):
            here = (lane >= at * group) & (lane < (at + 1) * group)
            index = lax.rem(point * cells[f], cos_table.shape[0])
            cosines = jnp.where(here, cos_table[index], cosines)
            sines = jnp.where(here, sin_table[index], sines)
        tables.append((cosines, sines))
    row = lax.broadcasted_iota(jnp.int32, (rows, lanes), 0)
    col = lax.broadcasted_iota(jnp.int32, (rows, lanes), 1)
    first = row < group
    cosines = jnp.where(first, tables[0][0], tables[1][0])
    sines = jnp.where(first, tables[0][1], tables[1][1])
    real, real_m = row % group < width, col % group < width
    value = jnp.where(real == real_m, cosines, jnp.where(real, -sines, sines))
    value = jnp.where(row % width == col % width, value, 0.0)
    high = value.astype(BF16)
    low = (value - high.astype(F32)).astype(BF16)
    both = jnp.concatenate([high, low], 0)
    g0[...] = both[:, : g0.shape[1]]
    g1[...] = both[:, g0.shape[1] :]


def turned(value, width, sign):
    rows = value.shape[0]
    real = lax.broadcasted_iota(jnp.int32, value.shape, 0) % (2 * width) < width
    up, down = pltpu.roll(value, rows - width, 0), pltpu.roll(value, width, 0)
    return jnp.where(real, up, -down) if sign > 0 else jnp.where(real, -up, down)


def part_of_t(b, real, imag, w, g, width):
    contract = (((1,), (1,)), ((), ()))
    m = lax.dot_general(b, real[...], contract, preferred_element_type=F32)
    m = m + turned(lax.dot_general(b, imag[...], contract, preferred_element_type=F32), width, 1)
    t = jnp.dot(g, (w * m).astype(BF16), preferred_element_type=F32)
    half = t.shape[0] // 2
    return t[:half] + t[half:]


def odd_x():
    return jnp.bitwise_and(lax.axis_index("x"), 1)


def either_way(far_a, far_b, run):
    odd = odd_x()

    @pl.when(odd == 0)
    def _():
        run(far_a, far_b)

    @pl.when(odd != 0)
    def _():
        run(far_b, far_a)


def gathered(b_ref, b0, b1):
    half = b0.shape[0]
    b_ref[:half, :] = b0[...]
    b_ref[half:, :] = b1[...]
    return b_ref[...]


def own_kernel(width, own, b0, b1, w, g, t_ref, b_ref):
    b = gathered(b_ref, b0, b1)
    t_ref[...] = part_of_t(b, own.at[0], own.at[1], w[0, : b.shape[0], :], g[...], width)


def far_kernel(width, far_a, far_b, b0, b1, w, g, t_ref, b_ref):
    b = gathered(b_ref, b0, b1)

    def run(real, imag):
        t_ref[...] = part_of_t(b, real, imag, w[1, : b.shape[0], :], g[...], width)

    either_way(far_a, far_b, run)


def last_kernel(width, own, far_a, far_b, b0, b1, w, g, t_own, t_far, t_ref, b_ref):
    b = gathered(b_ref, b0, b1)
    start = w.shape[1] - b.shape[0]

    def run(real, imag):
        of_own = t_own[...] + part_of_t(b, own.at[0], own.at[1], w[0, start:, :], g[...], width)
        of_far = t_far[...] + part_of_t(b, real, imag, w[1, start:, :], g[...], width)
        t_ref[...] = dense(of_own, of_far)

    either_way(far_a, far_b, run)


def dense(own, far):
    mid, tail = own.shape[0] // 2, own.shape[1] - 128
    rest = [part[rows, 128:] for rows in (slice(None, mid), slice(mid, None)) for part in (own, far)]
    assert 4 * tail == 128
    return jnp.concatenate([own[:, :128], far[:, :128], jnp.concatenate(rest, 1)], 0)


def spread(value):
    rows = value.shape[0] * 2 // 5
    rest = value[2 * rows :]
    pairs = []
    for at in range(2):
        tail = [rest[:, 32 * part : 32 * (part + 1)] for part in (at, at + 2)]
        pairs.append(jnp.concatenate([value[at * rows : (at + 1) * rows], jnp.concatenate(tail, 0)], 1))
    return pairs


def coded(pieces, lanes):
    rows, columns = pieces[0].shape
    spare = jnp.zeros((rows, lanes - columns), F32)
    pieces = [jnp.concatenate([piece, spare], 1) for piece in pieces]
    largest = jnp.concatenate([jnp.max(jnp.abs(piece), axis=0, keepdims=True) for piece in pieces], 0)
    exponents = jnp.floor(jnp.log2(jnp.maximum(largest, 1e-30))) + 1.0
    scales = jnp.exp2(14.0 - exponents)
    out = []
    for at, piece in enumerate(pieces):
        out.append(jnp.floor(piece * scales[at : at + 1] + 0.5))
        out.append(jnp.broadcast_to(exponents[at : at + 1], (8, lanes)))
    return jnp.concatenate(out, 0).astype(jnp.int32).astype(jnp.int16)


def decoded(value):
    value = value.astype(jnp.int32).astype(F32)
    rows = value.shape[0] - 8
    return value[:rows] * jnp.exp2(value[rows : rows + 1] - 14.0)


def packed(u, at, columns):
    third = columns // 3
    tall = jnp.concatenate([u[:, at + p * third : at + (p + 1) * third] for p in range(3)], 0)
    rows = tall.shape[0] // 5
    return jnp.concatenate([tall[g * rows : (g + 1) * rows] for g in range(5)], 1)


def unpacked(value, columns):
    third = columns // 3
    tall = jnp.concatenate([value[:, g * third : (g + 1) * third] for g in range(5)], 0)
    rows = tall.shape[0] // 3
    return jnp.concatenate([tall[p * rows : (p + 1) * rows] for p in range(3)], 1)


def cluster_kernel(
    width, columns, own, far_a, far_b, near_hbm, diag_a_hbm, diag_b_hbm, t, t_yh, t_core, t_diag, out,
    u_ref, near, diag_a, diag_b, sems
):
    fetches = []
    for at, (source, target) in enumerate(((near_hbm, near), (diag_a_hbm, diag_a), (diag_b_hbm, diag_b))):
        fetches.append(pltpu.make_async_copy(source, target, sems.at[at]))
        fetches[-1].start()
    yh, core, odd = lax.axis_index("yh"), lax.axis_index("core"), odd_x()
    chips, lanes = PARTS[1], out.shape[1]
    span = 2 * chips * columns
    shift = span % 128
    window = pl.ds(pl.multiple_of(yh * (span - shift), 128), span + shift)
    half = 4 * width
    t, t_yh, t_core, t_diag = (spread(ref[...]) for ref in (t, t_yh, t_core, t_diag))
    swap = jnp.full(t[0].shape, odd) > 0
    total = None
    for value, first, second, swapped, waits in (
        (t[0] + t_yh[1], own.at[0], own.at[1], False, []),
        (t[1] + t_yh[0], far_a, far_b, True, []),
        (t_core[0] + t_diag[1], near.at[0], near.at[1], False, fetches[:1]),
        (t_core[1] + t_diag[0], diag_a, diag_b, True, fetches[1:]),
    ):
        for fetch in waits:
            fetch.wait()
        partner = turned(value, width, -1)
        if swapped:
            value, partner = jnp.where(swap, partner, value), jnp.where(swap, value, partner)
        for factor, data in ((value, first), (partner, second)):
            high = factor.astype(BF16)
            low = (factor - high.astype(F32)).astype(BF16)
            u = jnp.dot(jnp.concatenate([high, low], 0), data[:, window], preferred_element_type=F32)
            total = u if total is None else total + u
    u_ref[...] = total[:half] + total[half:]
    for row in range(2):
        for parity in range(2):

            @pl.when((yh == row) & (core == parity))
            def _():
                starts = [(2 * chip + parity) * columns + row * shift for chip in range(chips)]
                out[...] = coded([packed(u_ref[...], at, columns) for at in starts], lanes)


def final_kernel(arrived, mask, out):
    total = decoded(arrived[0])
    for chip in range(1, arrived.shape[0]):
        total = total + decoded(arrived[chip])
    cells, width, parts, columns = out.shape
    value = unpacked(total, columns)
    for f in range(cells):
        kept = value[f * parts * width : (f + 1) * parts * width] * mask[pl.ds(f, 1), :]
        for part in range(parts):
            for j in range(width):
                out[f, j, pl.ds(part, 1), :] = kept[part * width + j : part * width + j + 1]


def call(kernel, name, shapes, specs, scratch=(), mib=8, flops=0):
    return pl.pallas_call(
        kernel,
        out_shape=shapes,
        in_specs=[pl.BlockSpec(memory_space=space) for space in specs],
        out_specs=jax.tree.map(lambda _: pl.BlockSpec(memory_space=pltpu.VMEM), shapes),
        scratch_shapes=scratch,
        compiler_params=pltpu.CompilerParams(vmem_limit_bytes=mib * 2**20),
        cost_estimate=pl.CostEstimate(flops=flops, bytes_accessed=2**20, transcendentals=0),
        name=name,
    )


def shards(coefficients, class_weight, diff_class, frag_cells, block_pattern):
    own = coefficients[0]
    _, occupied, functions = own.shape
    yh, z, core = (lax.axis_index(name) for name in KA)
    band = lax.axis_index("yl") * PARTS[4] + lax.axis_index("x")
    width = occupied // (PARTS[3] * PARTS[4])
    group = 2 * width
    kpoint_count = PARTS[0] * PARTS[1] * PARTS[2]
    cells = frag_cells.shape[0]
    up = [(i, (i + 1) % PARTS[1]) for i in range(PARTS[1])]
    down = [(j, i) for i, j in up]
    swap = [(0, 1), (1, 0)]
    right = [(i, (i + 1) % PARTS[4]) for i in range(PARTS[4])]
    left = [(j, i) for i, j in right]
    vmem, smem = pltpu.VMEM, pltpu.SMEM

    far_a = lax.ppermute(lax.dynamic_index_in_dim(own, odd_x(), 0, keepdims=False), "yh", swap)
    near = lax.ppermute(own, "core", swap)
    block = lax.dynamic_slice_in_dim(own, band * width, width, 1).reshape(group, functions)
    blocks = [block]
    offsets = [0, -1, 1, -2, 2, -3, 3, -4]
    from_below = from_above = block
    for step in range(1, PARTS[1] // 2):
        from_below = lax.ppermute(from_below, "z", up)
        from_above = lax.ppermute(from_above, "z", down)
        if step == 2:
            from_below, from_above, near = lax.optimization_barrier((from_below, from_above, near))
        if step == 3:
            from_below, from_above, far_a = lax.optimization_barrier((from_below, from_above, far_a))
        blocks += [from_below, from_above]
    mid = occupied // 2
    from_left = lax.ppermute(far_a[:mid], "x", right)
    from_right = lax.ppermute(far_a[mid:], "x", left)
    split = 5
    first = jnp.concatenate(blocks[:split], 0)
    first_near = lax.ppermute(first, "core", swap)

    k_points = []
    for these in (offsets[:split], offsets[split:]):
        k_points += [(offset, False) for offset in these] + [(offset, True) for offset in these]
    early, late = 2 * split * group, 2 * (len(offsets) - split) * group
    angles = 2.0 * np.pi * np.arange(kpoint_count) / kpoint_count
    tables = [jnp.asarray((f(angles) / kpoint_count).astype(np.float32)) for f in (np.cos, np.sin)]
    later_cells, _ = lax.optimization_barrier((frag_cells, first))
    weights, g_first, g_last = call(
        functools.partial(prep_kernel, width, functions, k_points),
        "phases",
        (
            jax.ShapeDtypeStruct((2, early + late, 1), F32),
            jax.ShapeDtypeStruct((8 * width, early), BF16),
            jax.ShapeDtypeStruct((8 * width, late), BF16),
        ),
        [smem] * 5,
    )(later_cells, diff_class, class_weight, *tables)

    one = jax.ShapeDtypeStruct((4 * width, occupied), F32)
    scratch = [pltpu.VMEM((early, functions), BF16)]
    b_first = (first, first_near, weights, g_first)
    kernel = functools.partial(own_kernel, width)
    t_own = call(kernel, "own_first", one, [vmem] * 5, scratch, flops=10**9)(own, *b_first)
    cut = 24
    blocks.append(lax.ppermute(from_below[:cut], "z", up))
    blocks.append(lax.ppermute(from_above[cut:], "z", down))
    held = (blocks[-2], blocks[-1], from_left, from_right, t_own)
    blocks[-2], blocks[-1], from_left, from_right, t_own = lax.optimization_barrier(held)
    last = jnp.concatenate(blocks[split:], 0)
    far_b = jnp.concatenate([from_left, from_right], 0)
    last, far_b = lax.optimization_barrier((last, far_b))
    last_near = lax.ppermute(last, "core", swap)
    later_a, _ = lax.optimization_barrier((far_a, far_b))
    diag_a, diag_b = (lax.ppermute(half, "core", swap) for half in (later_a, far_b))
    kernel = functools.partial(far_kernel, width)
    t_far = call(kernel, "far_first", one, [vmem] * 6, scratch, flops=10**9)(far_a, far_b, *b_first)
    t = call(
        functools.partial(last_kernel, width),
        "last_terms",
        jax.ShapeDtypeStruct((20 * width // 2, 128), F32),
        [vmem] * 9,
        [pltpu.VMEM((late, functions), BF16)],
        flops=10**9,
    )(own, far_a, far_b, last, last_near, weights, g_last, t_own, t_far)

    t_yh = lax.ppermute(t, "yh", swap)
    t_core = lax.ppermute(t, "core", swap)
    t_diag = lax.ppermute(t_yh, "core", swap)
    chips = PARTS[1]
    columns = functions // kpoint_count
    span = 2 * chips * columns
    rows = 4 * width * 3 // 5 + 8
    pieces = call(
        functools.partial(cluster_kernel, width, columns),
        "cluster_terms",
        jax.ShapeDtypeStruct((chips * rows, 128), jnp.int16),
        [vmem] * 3 + [pl.ANY] * 3 + [vmem] * 4,
        [
            pltpu.VMEM((4 * width, span + span % 128), F32),
            pltpu.VMEM(own.shape, BF16),
            pltpu.VMEM(far_a.shape, BF16),
            pltpu.VMEM(far_a.shape, BF16),
            pltpu.SemaphoreType.DMA((3,)),
        ],
        mib=12,
        flops=10**9,
    )(own, far_a, far_b, near, diag_a, diag_b, t, t_yh, t_core, t_diag)

    pieces = pieces.reshape(chips, rows, 128)
    arrived = lax.all_to_all(pieces, "z", 0, 0, tiled=True)
    index = (yh * PARTS[1] + z) * 2 + core
    block_size = functions // block_pattern.shape[1]
    local_ids = (index * columns + jnp.arange(columns, dtype=jnp.int32)) // block_size
    block_ids = jnp.arange(block_pattern.shape[1], dtype=jnp.int32)
    onehot = (block_ids[:, None] == local_ids[None, :]).astype(F32)
    mask = jnp.dot(block_pattern.astype(F32), onehot, precision=lax.Precision.HIGHEST)
    cluster = call(
        final_kernel,
        "sum_and_mask",
        jax.ShapeDtypeStruct((cells, width, 2, columns), F32),
        [vmem] * 2,
        mib=4,
    )(arrived, mask)
    return jnp.transpose(cluster, (0, 2, 1, 3))


def solution(mesh):
    placed = (P(KA, None, None, None), P(), P(), P(), P())
    return jax.shard_map(
        shards,
        mesh=Mesh(mesh.devices.reshape(PARTS), AXES),
        in_specs=placed,
        out_specs=P(None, None, BAND, KA),
        check_vma=False,
    )
```
